32 devices in a mesh: bz: 4 (over z), bxy: 8 (over y, x, core).
Axes of the slice: x: 2, y: 2, z: 4, core: 2. Of those that a mesh axis runs over, the one named last changes fastest.
Arguments:
- pdfs: float32 [19, 4, 256, 4096], P(None, None, 'bxy', 'bz'), may hold values from 0.008 to 0.57, as said below
- relax: float32 [4, 256, 4096], P(None, 'bxy', 'bz'), may hold values from 0.6 to 1.9
- fluid: int32 [4, 256, 4096], P(None, 'bxy', 'bz'), may hold values 0 or 1
- targets: int32 [4, 8, 4], P('bz', 'bxy'), may hold values from 0 to 31, as said below
Outputs:
- moved: float32 [19, 4, 256, 4096], P(None, None, 'bxy', 'bz')
The draws below stay inside these ranges and needn't reach their ends.
Inputs may be any that keep to these rules, and one draw needn't show every extreme that they name: `pdfs`: every entry is positive. Within each row along bz, targets is a permutation of the 32 positions; a block's new owner is its owner or the owner just before or after it along bxy (no wrap), and at most 2 blocks of one owner go to one neighbouring owner.
All inputs are finite; a program needn't handle non-finite values. No bound on the sum of `fluid` on one device may be relied on, other than what follows from the above.
Results may differ from the reference program's by a relative error of at most 0.0003.
Values sent between devices are 32-bit elements; how exact they have to be, the bound alone decides.
A program may use at most 192 MiB of HBM per device.

```python
import jax
import jax.numpy as jnp

EDGE = 32
BLK_DEV = 4
STEPS = 2
MOVE = 2
NX = 256
NYZ = 4096
N_BZ = 4
N_BXY = 8


WEIGHT_TABLE = (1.0 / 3.0,) + (1.0 / 18.0,) * 6 + (1.0 / 36.0,) * 12


def draw_pdfs(key, part):
    shape = (19, BLK_DEV, NX, NYZ)
    weights = jnp.array(WEIGHT_TABLE, jnp.float32).reshape((19, 1, 1, 1))
    factor = 1.0 + 0.35 * jnp.clip(jax.random.normal(key, shape, jnp.float32), -2.0, 2.0)
    return (weights * factor).astype(jnp.float32)


def draw_targets(key, part):
    rows = N_BZ
    owners = N_BXY
    blocks = BLK_DEV
    keys = jax.random.split(key, 3)
    bounds = jax.random.randint(keys[0], (rows, owners - 1), 1, MOVE + 1).astype(jnp.int32)
    forced = jax.random.randint(keys[1], (rows, 1), 0, owners - 1).astype(jnp.int32)
    bound_ids = jnp.arange(owners - 1, dtype=jnp.int32)[None, :]
    bounds = jnp.where(bound_ids == forced, MOVE, bounds)
    zeros = jnp.zeros((rows, 1), jnp.int32)
    right_count = jnp.concatenate([bounds, zeros], axis=1)
    left_count = jnp.concatenate([zeros, bounds], axis=1)
    scores = jax.random.randint(keys[2], (rows, owners, blocks), 0, 1 << 16).astype(jnp.int32) * blocks
    scores = scores + jnp.arange(blocks, dtype=jnp.int32)[None, None, :]
    order = jnp.argsort(scores, axis=-1).astype(jnp.int32)
    rank = jnp.argsort(order, axis=-1).astype(jnp.int32)
    order_next = jnp.roll(order, -1, axis=1)
    right_next = jnp.roll(right_count, -1, axis=1)
    order_prev = jnp.roll(order, 1, axis=1)
    right_here = right_count[:, :, None]
    left_here = left_count[:, :, None]
    right_index = jnp.clip(right_next[:, :, None] + rank, 0, blocks - 1)
    left_index = jnp.clip(rank - right_here, 0, blocks - 1)
    right_slot = jnp.take_along_axis(order_next, right_index, axis=-1)
    left_slot = jnp.take_along_axis(order_prev, left_index, axis=-1)
    owner_ids = jnp.arange(owners, dtype=jnp.int32)[None, :, None]
    slots = jnp.arange(blocks, dtype=jnp.int32)[None, None, :]
    goes_right = rank < right_here
    goes_left = (rank >= right_here) & (rank < right_here + left_here)
    result = jnp.where(goes_right, (owner_ids + 1) * blocks + right_slot, jnp.where(goes_left, (owner_ids - 1) * blocks + left_slot, owner_ids * blocks + slots))
    return result.astype(jnp.int32)


def touch_ends(drawn, stream_key, low, high):
    index_at = [jax.random.randint(jax.random.fold_in(stream_key, axis), (), 0, length) for axis, length in enumerate(drawn.shape)]
    widest = drawn.shape.index(max(drawn.shape))
    beside = index_at[:widest] + [(index_at[widest] + 1) % drawn.shape[widest]] + index_at[widest + 1:]
    return drawn.at[tuple(index_at)].set(low).at[tuple(beside)].set(high)


def levels(rng, extent, cuts, low, top_value):
    level = 1.0
    for axis_at, blocks in cuts:
        draws = jax.random.uniform(jax.random.fold_in(jax.random.fold_in(rng, 6), axis_at), (blocks,), jnp.float32, low / len(cuts), top_value / len(cuts))
        level = level * jnp.repeat(jnp.exp(draws), extent[axis_at] // blocks).reshape((-1,) + (1,) * (len(extent) - 1 - axis_at))
    return level


def setup_inputs(seed: int = 0) -> dict:
    arg_keys = jax.random.split(jax.random.key(seed), 5)
    return {
        "pdfs": draw_pdfs(jax.random.fold_in(arg_keys[4], 71), 0),
        "relax": jnp.clip(0.6 + 1.3 * jax.random.uniform(arg_keys[1], (BLK_DEV, NX, NYZ), jnp.float32) ** levels(arg_keys[1], (BLK_DEV, NX, NYZ), ((1, 8), (2, 4)), -0.2, 0.2), 0.6, 1.9),
        "fluid": touch_ends((jax.random.randint(arg_keys[2], (BLK_DEV, NX, NYZ), 0, 5) < 4).astype(jnp.int32), jax.random.fold_in(arg_keys[2], 1), 0, 1),
        "targets": draw_targets(jax.random.fold_in(arg_keys[4], 71), 0),
    }


VELOCITIES = ((0, 0, 0), (1, 0, 0), (-1, 0, 0), (0, 1, 0), (0, -1, 0), (0, 0, 1), (0, 0, -1),
              (1, 1, 0), (-1, -1, 0), (1, -1, 0), (-1, 1, 0), (1, 0, 1), (-1, 0, -1),
              (1, 0, -1), (-1, 0, 1), (0, 1, 1), (0, -1, -1), (0, 1, -1), (0, -1, 1))
OPPOSITE = (0, 2, 1, 4, 3, 6, 5, 8, 7, 10, 9, 12, 11, 14, 13, 16, 15, 18, 17)
WEIGHTS = (1.0 / 3.0,) + (1.0 / 18.0,) * 6 + (1.0 / 36.0,) * 12


def component(populations, axis_number):
    total = jnp.zeros_like(populations[0])
    for index, velocity in enumerate(VELOCITIES):
        if velocity[axis_number] == 1:
            total = total + populations[index]
        elif velocity[axis_number] == -1:
            total = total - populations[index]
    return total


def collide(populations, rates):
    density = jnp.zeros_like(populations[0])
    for index in range(19):
        density = density + populations[index]
    speed = [component(populations, axis_number) / density for axis_number in range(3)]
    square = speed[0] * speed[0] + speed[1] * speed[1] + speed[2] * speed[2]
    result = []
    for index, velocity in enumerate(VELOCITIES):
        along = jnp.zeros_like(density)
        for axis_number in range(3):
            if velocity[axis_number] == 1:
                along = along + speed[axis_number]
            elif velocity[axis_number] == -1:
                along = along - speed[axis_number]
        balance = WEIGHTS[index] * density * (1.0 + 3.0 * along + 4.5 * along * along - 1.5 * square)
        result.append(populations[index] + rates * (balance - populations[index]))
    return jnp.stack(result)


def pulled(field, velocity):
    padded = jnp.pad(field, 1)
    sizes = field.shape
    return padded[1 - velocity[0]:1 - velocity[0] + sizes[0],
                  1 - velocity[1]:1 - velocity[1] + sizes[1],
                  1 - velocity[2]:1 - velocity[2] + sizes[2]]


def to_grid(array):
    lead = array.shape[:-3]
    blocks, width_x, width_yz = array.shape[-3:]
    shaped = array.reshape(lead + (blocks, width_x, width_yz // EDGE, EDGE))
    shaped = jnp.moveaxis(shaped, -4, -2)
    return shaped.reshape(lead + (width_x, width_yz // EDGE, blocks * EDGE))


def from_grid(grid):
    width_x, width_y, width_z = grid.shape[1:]
    blocks = width_z // EDGE
    shaped = grid.reshape((19, width_x, width_y, blocks, EDGE))
    shaped = jnp.moveaxis(shaped, -2, -4)
    return shaped.reshape((19, blocks, width_x, width_y * EDGE))


def reference(pdfs, relax, fluid, targets):
    blocks = pdfs.shape[1]
    fluid_grid = to_grid(fluid)
    fluid_cells = fluid_grid > 0
    fluid_value = fluid_grid.astype(jnp.float32)
    rates = to_grid(relax)
    populations = to_grid(pdfs)
    for step in range(STEPS):
        post = collide(populations, rates)
        result = []
        for index, velocity in enumerate(VELOCITIES):
            source = pulled(fluid_value, velocity)
            incoming = pulled(post[index], velocity)
            value = jnp.where(source > 0.5, incoming, post[OPPOSITE[index]])
            result.append(jnp.where(fluid_cells, value, populations[index]))
        populations = jnp.stack(result)
    final = from_grid(populations)
    count = N_BXY * blocks
    grouped = final.reshape((19, blocks, N_BXY, EDGE, N_BZ, EDGE * EDGE))
    grouped = jnp.transpose(grouped, (4, 2, 1, 0, 3, 5)).reshape((N_BZ, count, 19, EDGE, EDGE * EDGE))
    flat = targets.reshape((N_BZ, count)).astype(jnp.int32)
    row_index = jnp.broadcast_to(jnp.arange(N_BZ, dtype=jnp.int32)[:, None], (N_BZ, count))
    anchor = jnp.zeros((N_BZ, count), jnp.int32).at[row_index, flat].set(
        jnp.broadcast_to(jnp.arange(count, dtype=jnp.int32)[None, :], (N_BZ, count)))
    placed = jnp.take_along_axis(grouped, anchor[:, :, None, None, None], axis=1)
    placed = placed.reshape((N_BZ, N_BXY, blocks, 19, EDGE, EDGE * EDGE))
    placed = jnp.transpose(placed, (3, 2, 1, 4, 0, 5))
    return placed.reshape((19, blocks, N_BXY * EDGE, N_BZ * EDGE * EDGE))
```

```python
import functools
import math

import jax
import jax.numpy as jnp
from jax import lax
from jax.experimental import pallas as pl
from jax.experimental.pallas import tpu as pltpu
from jax.sharding import PartitionSpec as P

MESH = pl.DeviceIdType.MESH
VELOCITIES = (
    (0, 0, 0), (1, 0, 0), (-1, 0, 0), (0, 1, 0), (0, -1, 0), (0, 0, 1), (0, 0, -1),
    (1, 1, 0), (-1, -1, 0), (1, -1, 0), (-1, 1, 0), (1, 0, 1), (-1, 0, -1),
    (1, 0, -1), (-1, 0, 1), (0, 1, 1), (0, -1, -1), (0, 1, -1), (0, -1, 1),
)
OPPOSITE = (0, 2, 1, 4, 3, 6, 5, 8, 7, 10, 9, 12, 11, 14, 13, 16, 15, 18, 17)
Q = 19
TURNS = tuple(tuple(i for i in range(Q) if VELOCITIES[i][axis]) for axis in range(3))
Y_SENT = tuple(tuple(i for i in range(Q) if VELOCITIES[i][1] == c) for c in (1, -1))
X_SENT = tuple(tuple(i for i in range(Q) if VELOCITIES[i][0] == c) for c in (1, -1))
CORNERS = (7, 8, 9, 10)
SIDE = {1: 0, -1: 1}
VMEM_LIMIT = 60 * 1024 * 1024


def collide(f, rate):
    pair = {i: (f[i] + f[i + 1], f[i] - f[i + 1]) for i in range(1, Q, 2)}
    density = f[0]
    for i in range(1, Q, 2):
        density = density + pair[i][0]
    scale = 3.0 / density
    flow = []
    for axis in range(3):
        total = None
        for i in range(1, Q, 2):
            c = VELOCITIES[i][axis]
            if c:
                d = pair[i][1]
                total = d if total is None else (total + d if c == 1 else total - d)
        flow.append(total * scale)
    base = 1.0 - (flow[0] * flow[0] + flow[1] * flow[1] + flow[2] * flow[2]) * (1.0 / 6.0)
    keep = 1.0 - rate
    drive = rate * density
    post = [None] * Q
    post[0] = keep * f[0] + (drive * (1.0 / 3.0)) * base
    near, far = drive * (1.0 / 18.0), drive * (1.0 / 36.0)
    for i in range(1, Q, 2):
        along = None
        for axis in range(3):
            c = VELOCITIES[i][axis]
            if c:
                along = flow[axis] if along is None else (along + flow[axis] if c == 1 else along - flow[axis])
        even = base + 0.5 * (along * along)
        weight = near if i < 7 else far
        post[i] = keep * f[i] + weight * (even + along)
        post[i + 1] = keep * f[i + 1] + weight * (even - along)
    return post


def remote(src, dst, send_sem, recv_sem, device):
    return pltpu.make_async_remote_copy(
        src_ref=src, dst_ref=dst, send_sem=send_sem, recv_sem=recv_sem, device_id=device, device_id_type=MESH)


def lane_shift(velocity, slot, edge, here, below, above, beside):
    _cx, cy, cz = velocity
    width = here.shape[1]
    step = cy * edge + cz
    moved = here if step == 0 else pltpu.roll(here, step % width, 1)
    if cz:
        depth = lax.broadcasted_iota(jnp.int32, here.shape, 1) % edge
        other, face = (below, 0) if cz == 1 else (above, edge - 1)
        carry = step - cz * edge
        wrapped = other if carry == 0 else pltpu.roll(other, carry % width, 1)
        moved = jnp.where(depth == face, wrapped, moved)
    if cy:
        lane = lax.broadcasted_iota(jnp.int32, (here.shape[0], 128), 1)
        offset = 128 if cy == 1 else 256 - edge
        outside = pltpu.roll(beside, lax.rem(offset + cz + 128 - slot * edge, 128), 1)
        if cy == 1:
            moved = jnp.concatenate([jnp.where(lane < edge, outside, moved[:, :128]), moved[:, 128:]], axis=1)
        else:
            moved = jnp.concatenate(
                [moved[:, :-128], jnp.where(lane >= 128 - edge, outside, moved[:, -128:])], axis=1)
    return moved


def arrive(i, slot, edge, slots, here, below, above, yr_ref, xr_ref, cr_ref, fluid):
    velocity = cx, cy, cz = VELOCITIES[i]
    beside = None
    if cy:
        side = SIDE[cy]
        beside = yr_ref[side, 5 if fluid else Y_SENT[side].index(i)]
    moved = lane_shift(velocity, slot, edge, here, below, above, beside)
    if cx:
        side = SIDE[cx]
        row = 5 if fluid else X_SENT[side].index(i)
        rows = moved.shape[0]

        def plane(s):
            return jnp.broadcast_to(xr_ref[side, s, row:row + 1, :], (8, moved.shape[1]))

        corner = None
        if cy:
            k = CORNERS.index(i)
            n = 1 if fluid else 0
            corner = jnp.broadcast_to(cr_ref[k, n:n + 1, :], (8, 128))
        entering = lane_shift(
            velocity, slot, edge, plane(slot), plane(jnp.maximum(slot - 1, 0)) if cz == 1 else None,
            plane(jnp.minimum(slot + 1, slots - 1)) if cz == -1 else None, corner)
        index = lax.broadcasted_iota(jnp.int32, (8, moved.shape[1]), 0)
        moved = pltpu.roll(moved, cx % rows, 0)
        if cx == 1:
            moved = jnp.concatenate([jnp.where(index == 0, entering, moved[:8]), moved[8:]], axis=0)
        else:
            moved = jnp.concatenate([moved[:-8], jnp.where(index == 7, entering, moved[-8:])], axis=0)
    return moved


def collide_tiles(rows, width, read, rate, write):
    tiles = width // 128

    def body(step, carry):
        r = pl.multiple_of((step // tiles) * 8, 8)
        c = pl.multiple_of((step % tiles) * 128, 128)
        at = (pl.ds(r, 8), pl.ds(c, 128))
        post = collide([read(i, at) for i in range(Q)], rate(at))
        for i in range(Q):
            write(i, at, post[i])
        return carry

    lax.fori_loop(0, (rows // 8) * tiles, body, 0, unroll=4)


def emit_halo(slot, edge, post_ref, fluid_ref, ys_ref, xs_ref):
    rows, width = fluid_ref.shape[1:]
    lane = lax.broadcasted_iota(jnp.int32, (rows, 128), 1)
    mine = lane // edge == slot
    for side, first in ((0, width - 128), (1, 0)):
        turn = lax.rem(slot * edge + (edge if side == 0 else 0), 128)
        for n in range(6):
            if n < 5:
                tile = post_ref[Y_SENT[side][n], slot, :, first:first + 128]
            else:
                tile = fluid_ref[slot, :, first:first + 128].astype(jnp.float32)
            ys_ref[side, n] = jnp.where(mine, pltpu.roll(tile, turn, 1), ys_ref[side, n])
    for side, row in ((0, rows - 1), (1, 0)):
        for n in range(5):
            xs_ref[side, slot, n:n + 1, :] = post_ref[X_SENT[side][n], slot, row:row + 1, :]
        xs_ref[side, slot, 5:6, :] = fluid_ref[slot, row:row + 1, :].astype(jnp.float32)
        xs_ref[side, slot, 6:8, :] = jnp.zeros((2, width), jnp.float32)


def emit_corners(rows, ys_ref, cs_ref):
    for k, i in enumerate(CORNERS):
        cx, cy, _z = VELOCITIES[i]
        row = rows - 1 if cx == 1 else 0
        ys = SIDE[cy]
        cs_ref[k, 0:1, :] = ys_ref[ys, Y_SENT[ys].index(i), row:row + 1, :]
        cs_ref[k, 1:2, :] = ys_ref[ys, 5, row:row + 1, :]
        cs_ref[k, 2:8, :] = jnp.zeros((6, 128), jnp.float32)


def stream_slot(slot, edge, slots, mask_ref, post_ref, halo, write):
    below, above = jnp.maximum(slot - 1, 0), jnp.minimum(slot + 1, slots - 1)
    write(0, post_ref[0, slot])
    for i in range(1, Q):
        cz = VELOCITIES[i][2]
        own = post_ref[i, slot]
        value = arrive(
            i, slot, edge, slots, own, post_ref[i, below] if cz == 1 else None,
            post_ref[i, above] if cz == -1 else None, *halo, False)
        mask = mask_ref[slot]
        stay = jnp.where(mask > 0, post_ref[OPPOSITE[i], slot], own)
        write(i, jnp.where((mask & (1 << i)) != 0, value, stay))


def make_mask(slot, edge, slots, fluid_ref, halo, mask_ref):
    rows, width = fluid_ref.shape[1:]
    row = lax.broadcasted_iota(jnp.int32, (rows, width), 0)
    lane = lax.broadcasted_iota(jnp.int32, (rows, width), 1)
    depth = lane % edge
    z, b = lax.axis_index("bz"), lax.axis_index("bxy")
    at_end = (b == 0, b == lax.axis_size("bxy") - 1, z == 0, z == lax.axis_size("bz") - 1)
    fluid = fluid_ref[slot].astype(jnp.float32)
    below = fluid_ref[jnp.maximum(slot - 1, 0)].astype(jnp.float32)
    above = fluid_ref[jnp.minimum(slot + 1, slots - 1)].astype(jnp.float32)
    bits = jnp.ones((rows, width), jnp.int32)
    for i in range(1, Q):
        cx, cy, cz = VELOCITIES[i]
        source = arrive(i, slot, edge, slots, fluid, below if cz == 1 else None,
                        above if cz == -1 else None, *halo, True)
        bit = jnp.where(source > 0.5, 1 << i, 0)
        if cx:
            edge_row = 0 if cx == 1 else rows - 1
            bit = jnp.where((row == edge_row) & at_end[0 if cx == 1 else 1], 0, bit)
        if cy:
            outer = lane < edge if cy == 1 else lane >= width - edge
            bit = jnp.where(outer & at_end[2 if cy == 1 else 3], 0, bit)
        if cz:
            final = 0 if cz == 1 else slots - 1
            face = 0 if cz == 1 else edge - 1
            bit = jnp.where((depth == face) & (slot == final), 0, bit)
        bits = bits | bit
    mask_ref[slot] = jnp.where(fluid_ref[slot] > 0, bits, 0)


def pack_shell(step, i, edge, value, hz, hx, hy):
    rows, width = value.shape
    for axis, c in enumerate(VELOCITIES[i]):
        if not c:
            continue
        n = TURNS[axis].index(i) + step * len(TURNS[axis])
        if axis == 0:
            row = 0 if c == 1 else rows - 1
            hx[n:n + 1, :] = value[row:row + 1, :]
        elif axis == 1:
            per = 128 // edge
            t, g = n // per, n % per
            tile = value[:, :128] if c == 1 else value[:, width - 128:]
            shift = (g * edge - (0 if c == 1 else 128 - edge)) % 128
            tile = pltpu.roll(tile, shift, 1) if shift else tile
            if g:
                lane = lax.broadcasted_iota(jnp.int32, tile.shape, 1)
                tile = jnp.where(lane >= g * edge, tile, hy[:, t * 128:(t + 1) * 128])
            hy[:, t * 128:(t + 1) * 128] = tile
        else:
            depth = lax.broadcasted_iota(jnp.int32, value.shape, 1) % edge
            shift = (n - (0 if c == 1 else edge - 1)) % width
            turned = pltpu.roll(value, shift, 1) if shift else value
            hz[...] = turned if n == 0 else jnp.where(depth == n, turned, hz[...])


def patch_shell(step, i, edge, value, hz, hx, hy):
    rows, width = value.shape
    for axis, c in enumerate(VELOCITIES[i]):
        if not c:
            continue
        n = TURNS[axis].index(i) + step * len(TURNS[axis])
        if axis == 0:
            row = 0 if c == 1 else rows - 1
            index = lax.broadcasted_iota(jnp.int32, value.shape, 0)
            value = jnp.where(index == row, jnp.broadcast_to(hx[n:n + 1, :], value.shape), value)
        elif axis == 1:
            per = 128 // edge
            t, g = n // per, n % per
            shift = ((0 if c == 1 else 128 - edge) - g * edge) % 128
            tile = hy[:, t * 128:(t + 1) * 128]
            tile = pltpu.roll(tile, shift, 1) if shift else tile
            lane = lax.broadcasted_iota(jnp.int32, tile.shape, 1)
            if c == 1:
                value = jnp.concatenate([jnp.where(lane < edge, tile, value[:, :128]), value[:, 128:]], axis=1)
            else:
                value = jnp.concatenate(
                    [value[:, :-128], jnp.where(lane >= 128 - edge, tile, value[:, -128:])], axis=1)
        else:
            depth = lax.broadcasted_iota(jnp.int32, value.shape, 1) % edge
            face = 0 if c == 1 else edge - 1
            shift = (face - n) % width
            turned = pltpu.roll(hz[...], shift, 1) if shift else hz[...]
            value = jnp.where(depth == face, turned, value)
    return value


def pulled(i, edge, here):
    cx, cy, cz = VELOCITIES[i]
    lanes = (cy * edge + cz) % here.shape[1]
    here = pltpu.roll(here, lanes, 1) if lanes else here
    return pltpu.roll(here, cx % here.shape[0], 0) if cx else here


def redo_block(edge, f, hz, hx, hy, mask_ref, next_ref):
    rows, width = f.shape[1:]
    fluid = jnp.where(f[Q] > 0.0, 1.0, 0.0)
    bits = jnp.ones((rows, width), jnp.int32)
    for i in range(1, Q):
        bits = bits | jnp.where(pulled(i, edge, fluid) > 0.5, 1 << i, 0)
    mask_ref[...] = jnp.where(f[Q] > 0.0, bits, 0)

    def put(i, at, value):
        f[(i,) + at] = value

    def stream(step):
        next_ref[0] = f[0]
        for i in range(1, Q):
            own = f[i]
            mask = mask_ref[...]
            stay = jnp.where(mask > 0, f[OPPOSITE[i]], own)
            value = jnp.where((mask & (1 << i)) != 0, pulled(i, edge, own), stay)
            next_ref[i] = patch_shell(step, i, edge, value, hz, hx, hy)

    def rate(at):
        return f[(Q,) + at]

    collide_tiles(rows, width, lambda i, at: f[(i,) + at], rate, put)
    stream(0)
    collide_tiles(rows, width, lambda i, at: next_ref[(i,) + at], rate, put)
    stream(1)


def choose(picks, values):
    taken = []
    for pick in picks:
        out = values[0]
        for j in range(1, len(values)):
            out = jnp.where(pick == j, values[j], out)
        taken.append(out)
    return taken


def cuts_of(n):
    half = (n + 1) // 2
    cuts = (0, half // 2, half, half + (n - half + 1) // 2, n)
    return [slice(cuts[k], cuts[k + 1]) for k in range(4)]


EARLY = cuts_of(Q + 1)
LATE = cuts_of(Q)
PIECES = 11


def solve_kernel(edge, pdfs, relax_ref, fluid_ref, goal_ref, own_out, left_out, right_out, table_ref,
                 a_ref, b_ref, next_ref, mask_ref, ys1, xs1, cs1, yr1, xr1, cr1, ys2, xs2, cs2, yr2, xr2, cr2,
                 hz, hx, hy, early_s, hz_s, hx_s, hy_s, late_s, early_r, hz_r, hx_r, hy_r,
                 early_p, hz_p, hx_p, hy_p, late_p, redo_ref, redo_mask, note_s, note_r, note_m,
                 load_sem, out_sem, halo_send, halo_recv, note_send, note_recv, note_sem, send_sem, recv_sem):
    slots, rows, width = fluid_ref.shape
    nz, nb = lax.axis_size("bz"), lax.axis_size("bxy")
    z, b = lax.axis_index("bz"), lax.axis_index("bxy")

    loads = [pltpu.make_async_copy(pdfs.at[slice(s.start, min(s.stop, Q))], a_ref.at[slice(s.start, min(s.stop, Q))],
                                   load_sem.at[n]) for n, s in enumerate(EARLY)]
    for load in loads:
        load.start()

    across = math.isqrt(nb // 2)
    row = 2 * across
    bends = across == 2 and nb == 2 * row
    cut = row - 1 if bends else nb
    low, high = cut + 1 - row, cut + row
    no = b < 0
    goes_right, goes_left = (b < nb - 1) & (b != cut), (b > 0) & (b != cut + 1)
    at_cut, past_cut, is_low, is_high = (
        (b == cut, b == cut + 1, b == low, b == high) if bends else (no, no, no, no))

    def there(dz, db):
        exists = None
        for at, step, count in ((z, dz, nz), (b, db, nb)):
            if step:
                inside = at < count - 1 if step == 1 else at > 0
                exists = inside if exists is None else exists & inside
        return exists

    ways = [(1, 0), (-1, 0), (0, 1), (0, -1)] + [(VELOCITIES[i][1], VELOCITIES[i][0]) for i in CORNERS]
    meets = [(there(dz, db), (z + dz, b + db)) for dz, db in ways]
    if bends:
        for who in (at_cut, past_cut):
            meets += [(who, (z, low)), (who, (z, high))]
        for who in (is_low, is_high):
            meets += [(who, (z, cut)), (who, (z, cut + 1))]
    barrier = pltpu.get_barrier_semaphore()
    count = 0
    for who, peer in meets:
        count = count + who.astype(jnp.int32)

        @pl.when(who)
        def _():
            pl.semaphore_signal(barrier, inc=1, device_id=peer, device_id_type=MESH)

    pl.semaphore_wait(barrier, count)

    goal = [goal_ref[0, 0, j] for j in range(slots)]
    base = b * slots

    def flag(t):
        return t.astype(jnp.int32)

    def nth(hits, n):
        before, found = jnp.int32(0), jnp.int32(0)
        for j in range(slots):
            found = found + jnp.where(hits[j] & (before == n), j, 0)
            before = before + flag(hits[j])
        return found

    to_right = [g >= base + slots for g in goal]
    to_left = [g < base for g in goal]
    first_pick = (nth(to_right, 0), nth(to_left, 0))
    second_pick = (nth(to_right, 1), nth(to_left, 1))

    at_row = lax.broadcasted_iota(jnp.int32, note_s.shape, 0)
    note = jnp.zeros(note_s.shape, jnp.int32)
    for j in range(slots):
        note = jnp.where(at_row == j, goal[j], note)
    note_s[...] = note

    def note_copy(n):
        db = 1 if n == 0 else -1
        return remote(note_s, note_r.at[n], note_send.at[n], note_recv.at[n], (z, b + db))

    for n, db in ((0, 1), (1, -1)):
        @pl.when(there(0, db))
        def _():
            note_copy(n).start()

    pieces = [(early_s.at[0, s], early_s.at[1, s], early_r.at[0, s], early_r.at[1, s], early_p.at[s], n < 2)
              for n, s in enumerate(EARLY)]
    for s, r, p, first in ((hz_s, hz_r, hz_p, True), (hx_s, hx_r, hx_p, False), (hy_s, hy_r, hy_p, False)):
        pieces.append((s.at[0], s.at[1], r.at[0], r.at[1], p, first))
    pieces += [(late_s.at[0, s], late_s.at[1, s], left_out.at[1, s], right_out.at[1, s], late_p.at[s], n >= 2)
               for n, s in enumerate(LATE)]

    def send(p):
        to_r, to_l, from_l, from_r, passing, first = pieces[p]

        @pl.when(goes_right)
        def _():
            remote(to_r, from_l, send_sem.at[0, p], recv_sem.at[0, p], (z, b + 1)).start()

        @pl.when(goes_left)
        def _():
            remote(to_l, from_r, send_sem.at[1, p], recv_sem.at[1, p], (z, b - 1)).start()

        if bends:
            @pl.when(at_cut)
            def _():
                remote(to_r, passing, send_sem.at[0, p], recv_sem.at[2, p], (z, low if first else high)).start()

            @pl.when(past_cut)
            def _():
                remote(to_l, passing, send_sem.at[1, p], recv_sem.at[2, p], (z, high if first else low)).start()

    def forward(p):
        to_r, to_l, from_l, from_r, passing, first = pieces[p]
        if bends:
            for who, ahead in ((is_low, True), (is_high, False)):
                @pl.when(who)
                def _():
                    remote(to_r, passing, send_sem.at[2, p], recv_sem.at[2, p], (z, cut)).wait_recv()
                    if first == ahead:
                        remote(passing, from_l, send_sem.at[2, p], recv_sem.at[0, p], (z, cut + 1)).start()
                    else:
                        remote(passing, from_r, send_sem.at[2, p], recv_sem.at[1, p], (z, cut)).start()

    def arrived(p):
        to_r, to_l, from_l, from_r, passing, first = pieces[p]

        @pl.when(b > 0)
        def _():
            remote(to_r, from_l, send_sem.at[0, p], recv_sem.at[0, p], (z, b - 1)).wait_recv()

        @pl.when(b < nb - 1)
        def _():
            remote(to_l, from_r, send_sem.at[1, p], recv_sem.at[1, p], (z, b + 1)).wait_recv()

    def sent(p):
        to_r, to_l, from_l, from_r, passing, first = pieces[p]

        @pl.when(b < nb - 1)
        def _():
            remote(to_r, from_l, send_sem.at[0, p], recv_sem.at[0, p], (z, b + 1)).wait_send()

        @pl.when(b > 0)
        def _():
            remote(to_l, from_r, send_sem.at[1, p], recv_sem.at[1, p], (z, b - 1)).wait_send()

        if bends:
            @pl.when(is_low | is_high)
            def _():
                remote(passing, from_l, send_sem.at[2, p], recv_sem.at[0, p], (z, cut)).wait_send()

    for n, s in enumerate(EARLY):
        loads[n].wait()

        def gather(i, carry):
            early_s[0, i], early_s[1, i] = choose(first_pick, [a_ref[i, j] for j in range(slots)])
            return carry

        lax.fori_loop(s.start, min(s.stop, Q), gather, 0)
        if s.stop == Q + 1:
            early_s[0, Q], early_s[1, Q] = choose(
                first_pick, [jnp.where(fluid_ref[j] > 0, relax_ref[j], 0.0) for j in range(slots)])
        send(n)

    def rate_of(slot):
        return lambda at: jnp.where(fluid_ref[(slot,) + at] > 0, relax_ref[(slot,) + at], 0.0)

    def first_step(slot, carry):
        def put(i, at, value):
            a_ref[(i, slot) + at] = value

        collide_tiles(rows, width, lambda i, at: a_ref[(i, slot) + at], rate_of(slot), put)
        emit_halo(slot, edge, a_ref, fluid_ref, ys1, xs1)
        return carry

    def routes(step):
        ys, xs, cs, yr, xr, cr = ((ys1, xs1, cs1, yr1, xr1, cr1), (ys2, xs2, cs2, yr2, xr2, cr2))[step]
        ends = [(ys.at[0], yr.at[0]), (ys.at[1], yr.at[1]), (xs.at[0], xr.at[0]), (xs.at[1], xr.at[1])]
        ends += [(cs.at[k], cr.at[k]) for k in range(4)]
        return [(src, dst, dz, db, step * 8 + n) for n, ((src, dst), (dz, db)) in enumerate(zip(ends, ways))]

    def exchange(step):
        for src, dst, dz, db, n in routes(step):
            @pl.when(there(dz, db))
            def _():
                remote(src, dst, halo_send.at[n], halo_recv.at[n], (z + dz, b + db)).start()

    def await_halo(step):
        for src, dst, dz, db, n in routes(step):
            @pl.when(there(-dz, -db))
            def _():
                remote(src, dst, halo_send.at[n], halo_recv.at[n], (z - dz, b - db)).wait_recv()

    ys1[...] = jnp.zeros(ys1.shape, jnp.float32)
    ys2[...] = jnp.zeros(ys2.shape, jnp.float32)
    lax.fori_loop(0, slots, first_step, 0)
    emit_corners(rows, ys1, cs1)
    exchange(0)
    await_halo(0)

    def middle_step(slot, carry):
        halo = (yr1, xr1, cr1)
        make_mask(slot, edge, slots, fluid_ref, halo, mask_ref)

        def write(i, value):
            next_ref[i] = value
            pack_shell(0, i, edge, value, hz.at[slot], hx.at[slot], hy.at[slot])

        stream_slot(slot, edge, slots, mask_ref, a_ref, halo, write)

        def put(i, at, value):
            b_ref[(i, slot) + at] = value

        collide_tiles(rows, width, lambda i, at: next_ref[(i,) + at], rate_of(slot), put)
        emit_halo(slot, edge, b_ref, fluid_ref, ys2, xs2)
        return carry

    lax.fori_loop(0, slots, middle_step, 0)
    emit_corners(rows, ys2, cs2)
    exchange(1)
    for n in (0, 2, 1, 3):
        forward(n)
    await_halo(1)

    def last_step(slot, carry):
        def write(i, value):
            a_ref[i, slot] = value
            pack_shell(1, i, edge, value, hz.at[slot], hx.at[slot], hy.at[slot])

        stream_slot(slot, edge, slots, mask_ref, b_ref, (yr2, xr2, cr2), write)
        return carry

    lax.fori_loop(0, slots, last_step, 0)
    keep = pltpu.make_async_copy(a_ref, own_out, out_sem.at[2])
    keep.start()
    for shell, staged in ((hz, hz_s), (hx, hx_s), (hy, hy_s)):
        staged[0], staged[1] = choose(first_pick, [shell[j] for j in range(slots)])
    for p in range(4, 7):
        send(p)
    for n, s in enumerate(LATE):
        def gather(i, carry):
            late_s[0, i], late_s[1, i] = choose(second_pick, [a_ref[i, j] for j in range(slots)])
            return carry

        lax.fori_loop(s.start, s.stop, gather, 0)
        send(7 + n)

    for p in (4, 5, 6):
        forward(p)
    for p in range(7):
        arrived(p)

    def redo(side, carry):
        redo_block(edge, early_r.at[side], hz_r.at[side], hx_r.at[side], hy_r.at[side], redo_mask, redo_ref.at[side])
        return carry

    lax.fori_loop(jnp.where(b > 0, 0, 1), jnp.where(b < nb - 1, 2, 1), redo, 0)
    redone = [(b > 0, pltpu.make_async_copy(redo_ref.at[0], left_out.at[0], out_sem.at[0])),
              (b < nb - 1, pltpu.make_async_copy(redo_ref.at[1], right_out.at[0], out_sem.at[1]))]
    for who, copy in redone:
        @pl.when(who)
        def _():
            copy.start()

    for p in (7, 9, 8, 10):
        forward(p)

    for n, db in ((0, 1), (1, -1)):
        @pl.when(there(0, -db))
        def _():
            remote(note_s, note_r.at[n], note_send.at[n], note_recv.at[n], (z, b - db)).wait_recv()

        @pl.when(there(0, db))
        def _():
            note_copy(n).wait_send()

    fetch = pltpu.make_async_copy(note_r, note_m, note_sem.at[0])
    fetch.start()
    fetch.wait()
    kind = [jnp.int32(0)] * slots
    index = [jnp.int32(k) for k in range(slots)]
    for k in range(slots):
        for j in range(slots):
            index[k] = jnp.where(goal[j] == base + k, j, index[k])
    for source, valid in ((1, b > 0), (2, b < nb - 1)):
        rank = jnp.int32(0)
        for j in range(slots):
            value = note_m[source - 1, j, 0]
            for k in range(slots):
                hit = valid & (value == base + k)
                kind[k] = jnp.where(hit, source, kind[k])
                index[k] = jnp.where(hit, rank, index[k])
            rank = rank + flag(valid & (value >= base) & (value < base + slots))
    for source in range(3):
        held = jnp.int32(0)
        for k in range(slots):
            held = jnp.where(kind[k] == source, index[k], held)
            table_ref[source, k] = held
    for k in range(slots):
        table_ref[3, k] = kind[k]

    for step in range(2):
        for src, dst, dz, db, n in routes(step):
            @pl.when(there(dz, db))
            def _():
                remote(src, dst, halo_send.at[n], halo_recv.at[n], (z + dz, b + db)).wait_send()

    for p in range(7):
        sent(p)
    keep.wait()
    for who, copy in redone:
        @pl.when(who)
        def _():
            copy.wait()

    for p in range(7, PIECES):
        sent(p)
        arrived(p)


def solve(pdfs, relax, fluid, targets):
    q, slots, rows, width = pdfs.shape
    edge = rows
    f32, i32 = jnp.float32, jnp.int32
    hbm = pl.BlockSpec(memory_space=pl.ANY)
    vmem = pl.BlockSpec(memory_space=pltpu.VMEM)
    smem = pl.BlockSpec(memory_space=pltpu.SMEM)
    per = 128 // edge
    turns = 2 * len(TURNS[0])
    x_rows = -(-turns // 8) * 8
    y_lanes = -(-turns // per) * 128
    ys, xs, cs = (2, 6, rows, 128), (2, slots, 8, width), (4, 8, 128)

    def shells(lead):
        return [pltpu.VMEM(lead + s, f32) for s in ((rows, width), (x_rows, width), (rows, y_lanes))]

    halo = [pltpu.VMEM(s, f32) for s in (ys, xs, cs)]
    dma = pltpu.SemaphoreType.DMA
    scratch = [pltpu.VMEM(pdfs.shape, f32), pltpu.VMEM(pdfs.shape, f32), pltpu.VMEM((q, rows, width), f32),
               pltpu.VMEM(fluid.shape, i32)] + halo * 4
    scratch += shells((slots,))
    scratch += [pltpu.VMEM((2, q + 1, rows, width), f32)] + shells((2,)) + [pltpu.VMEM((2, q, rows, width), f32)]
    scratch += [pltpu.VMEM((2, q + 1, rows, width), f32)] + shells((2,))
    scratch += [pltpu.VMEM((q + 1, rows, width), f32)] + shells(()) + [pltpu.VMEM((q, rows, width), f32)]
    scratch += [pltpu.VMEM((2, q, rows, width), f32), pltpu.VMEM((rows, width), i32)]
    scratch += [pltpu.VMEM((8, 128), i32), pltpu.VMEM((2, 8, 128), i32), pltpu.SMEM((2, 8, 128), i32)]
    scratch += [dma((4,)), dma((3,)), dma((16,)), dma((16,)), dma((2,)), dma((2,)), dma((1,)),
                dma((3, PIECES)), dma((3, PIECES))]
    got = jax.ShapeDtypeStruct((2, q, rows, width), f32)
    return pl.pallas_call(
        functools.partial(solve_kernel, edge),
        out_shape=[jax.ShapeDtypeStruct(pdfs.shape, f32), got, got, jax.ShapeDtypeStruct((4, slots), i32)],
        in_specs=[hbm, vmem, vmem, smem], out_specs=[hbm, hbm, hbm, smem], scratch_shapes=scratch,
        compiler_params=pltpu.CompilerParams(collective_id=0, has_side_effects=True, vmem_limit_bytes=VMEM_LIMIT),
        name="solve",
    )(pdfs, relax, fluid, targets)


def place_kernel(table_ref, final_ref, left_ref, right_ref, out_ref):
    kind = table_ref[3, pl.program_id(0)]

    @pl.when(kind == 0)
    def _():
        out_ref[...] = final_ref[...]

    @pl.when(kind == 1)
    def _():
        out_ref[:, 0] = left_ref[0]

    @pl.when(kind == 2)
    def _():
        out_ref[:, 0] = right_ref[0]


def place(final, left, right, table):
    q, blocks, rows, width = final.shape
    block = (q, 1, rows, width)

    def taken(kind):
        return pl.BlockSpec((1, q, rows, width), lambda k, table: (table[kind, k], 0, 0, 0))

    return pl.pallas_call(
        place_kernel,
        out_shape=jax.ShapeDtypeStruct(final.shape, final.dtype),
        grid_spec=pltpu.PrefetchScalarGridSpec(
            num_scalar_prefetch=1, grid=(blocks,),
            in_specs=[pl.BlockSpec(block, lambda k, table: (0, table[0, k], 0, 0)), taken(1), taken(2)],
            out_specs=pl.BlockSpec(block, lambda k, table: (0, k, 0, 0))),
        compiler_params=pltpu.CompilerParams(vmem_limit_bytes=VMEM_LIMIT),
        name="place",
    )(table, final, left, right)


def on_device(pdfs, relax, fluid, targets):
    own, left, right, table = solve(pdfs, relax, fluid, targets)
    return place(own, left, right, table)


def solution(mesh):
    placed = (
        P(None, None, "bxy", "bz"),
        P(None, "bxy", "bz"),
        P(None, "bxy", "bz"),
        P("bz", "bxy", None),
    )
    return jax.shard_map(
        on_device, mesh=mesh, in_specs=placed, out_specs=P(None, None, "bxy", "bz"), check_vma=False
    )
```

```python
import functools
import math

import jax
import jax.numpy as jnp
from jax import lax
from jax.experimental import pallas as pl
from jax.experimental.pallas import tpu as pltpu
from jax.sharding import PartitionSpec as P

MESH = pl.DeviceIdType.MESH
VELOCITIES = (
    (0, 0, 0), (1, 0, 0), (-1, 0, 0), (0, 1, 0), (0, -1, 0), (0, 0, 1), (0, 0, -1),
    (1, 1, 0), (-1, -1, 0), (1, -1, 0), (-1, 1, 0), (1, 0, 1), (-1, 0, -1),
    (1, 0, -1), (-1, 0, 1), (0, 1, 1), (0, -1, -1), (0, 1, -1), (0, -1, 1),
)
OPPOSITE = (0, 2, 1, 4, 3, 6, 5, 8, 7, 10, 9, 12, 11, 14, 13, 16, 15, 18, 17)
Q = 19
TURNS = tuple(tuple(i for i in range(Q) if VELOCITIES[i][axis]) for axis in range(3))
Y_SENT = tuple(tuple(i for i in range(Q) if VELOCITIES[i][1] == c) for c in (1, -1))
X_SENT = tuple(tuple(i for i in range(Q) if VELOCITIES[i][0] == c) for c in (1, -1))
CORNERS = (7, 8, 9, 10)
SIDE = {1: 0, -1: 1}
VMEM_LIMIT = 60 * 1024 * 1024


def collide(f, rate):
    pair = {i: (f[i] + f[i + 1], f[i] - f[i + 1]) for i in range(1, Q, 2)}
    density = f[0]
    for i in range(1, Q, 2):
        density = density + pair[i][0]
    scale = 3.0 / density
    flow = []
    for axis in range(3):
        total = None
        for i in range(1, Q, 2):
            c = VELOCITIES[i][axis]
            if c:
                d = pair[i][1]
                total = d if total is None else (total + d if c == 1 else total - d)
        flow.append(total * scale)
    base = 1.0 - (flow[0] * flow[0] + flow[1] * flow[1] + flow[2] * flow[2]) * (1.0 / 6.0)
    keep = 1.0 - rate
    drive = rate * density
    post = [None] * Q
    post[0] = keep * f[0] + (drive * (1.0 / 3.0)) * base
    near, far = drive * (1.0 / 18.0), drive * (1.0 / 36.0)
    for i in range(1, Q, 2):
        along = None
        for axis in range(3):
            c = VELOCITIES[i][axis]
            if c:
                along = flow[axis] if along is None else (along + flow[axis] if c == 1 else along - flow[axis])
        even = base + 0.5 * (along * along)
        weight = near if i < 7 else far
        post[i] = keep * f[i] + weight * (even + along)
        post[i + 1] = keep * f[i + 1] + weight * (even - along)
    return post


def remote(src, dst, send_sem, recv_sem, device):
    return pltpu.make_async_remote_copy(
        src_ref=src, dst_ref=dst, send_sem=send_sem, recv_sem=recv_sem, device_id=device, device_id_type=MESH)


def lane_shift(velocity, slot, edge, here, below, above, beside):
    _cx, cy, cz = velocity
    width = here.shape[1]
    step = cy * edge + cz
    moved = here if step == 0 else pltpu.roll(here, step % width, 1)
    if cz:
        depth = lax.broadcasted_iota(jnp.int32, here.shape, 1) % edge
        other, face = (below, 0) if cz == 1 else (above, edge - 1)
        carry = step - cz * edge
        wrapped = other if carry == 0 else pltpu.roll(other, carry % width, 1)
        moved = jnp.where(depth == face, wrapped, moved)
    if cy:
        lane = lax.broadcasted_iota(jnp.int32, (here.shape[0], 128), 1)
        offset = 128 if cy == 1 else 256 - edge
        outside = pltpu.roll(beside, lax.rem(offset + cz + 128 - slot * edge, 128), 1)
        if cy == 1:
            moved = jnp.concatenate([jnp.where(lane < edge, outside, moved[:, :128]), moved[:, 128:]], axis=1)
        else:
            moved = jnp.concatenate(
                [moved[:, :-128], jnp.where(lane >= 128 - edge, outside, moved[:, -128:])], axis=1)
    return moved


def arrive(i, slot, edge, slots, here, below, above, yr_ref, xr_ref, cr_ref, fluid):
    velocity = cx, cy, cz = VELOCITIES[i]
    beside = None
    if cy:
        side = SIDE[cy]
        beside = yr_ref[side, 5 if fluid else Y_SENT[side].index(i)]
    moved = lane_shift(velocity, slot, edge, here, below, above, beside)
    if cx:
        side = SIDE[cx]
        row = 5 if fluid else X_SENT[side].index(i)
        rows = moved.shape[0]

        def plane(s):
            return jnp.broadcast_to(xr_ref[side, s, row:row + 1, :], (8, moved.shape[1]))

        corner = None
        if cy:
            k = CORNERS.index(i)
            n = 1 if fluid else 0
            corner = jnp.broadcast_to(cr_ref[k, n:n + 1, :], (8, 128))
        entering = lane_shift(
            velocity, slot, edge, plane(slot), plane(jnp.maximum(slot - 1, 0)) if cz == 1 else None,
            plane(jnp.minimum(slot + 1, slots - 1)) if cz == -1 else None, corner)
        index = lax.broadcasted_iota(jnp.int32, (8, moved.shape[1]), 0)
        moved = pltpu.roll(moved, cx % rows, 0)
        if cx == 1:
            moved = jnp.concatenate([jnp.where(index == 0, entering, moved[:8]), moved[8:]], axis=0)
        else:
            moved = jnp.concatenate([moved[:-8], jnp.where(index == 7, entering, moved[-8:])], axis=0)
    return moved


def collide_tiles(rows, width, read, rate, write):
    tiles = width // 128

    def body(step, carry):
        r = pl.multiple_of((step // tiles) * 8, 8)
        c = pl.multiple_of((step % tiles) * 128, 128)
        at = (pl.ds(r, 8), pl.ds(c, 128))
        post = collide([read(i, at) for i in range(Q)], rate(at))
        for i in range(Q):
            write(i, at, post[i])
        return carry

    lax.fori_loop(0, (rows // 8) * tiles, body, 0, unroll=4)


def emit_halo(slot, edge, post_ref, fluid_ref, ys_ref, xs_ref):
    rows, width = fluid_ref.shape[1:]
    lane = lax.broadcasted_iota(jnp.int32, (rows, 128), 1)
    mine = lane // edge == slot
    for side, first in ((0, width - 128), (1, 0)):
        turn = lax.rem(slot * edge + (edge if side == 0 else 0), 128)
        for n in range(6):
            if n < 5:
                tile = post_ref[Y_SENT[side][n], slot, :, first:first + 128]
            else:
                tile = fluid_ref[slot, :, first:first + 128].astype(jnp.float32)
            ys_ref[side, n] = jnp.where(mine, pltpu.roll(tile, turn, 1), ys_ref[side, n])
    for side, row in ((0, rows - 1), (1, 0)):
        for n in range(5):
            xs_ref[side, slot, n:n + 1, :] = post_ref[X_SENT[side][n], slot, row:row + 1, :]
        xs_ref[side, slot, 5:6, :] = fluid_ref[slot, row:row + 1, :].astype(jnp.float32)
        xs_ref[side, slot, 6:8, :] = jnp.zeros((2, width), jnp.float32)


def emit_corners(rows, ys_ref, cs_ref):
    for k, i in enumerate(CORNERS):
        cx, cy, _z = VELOCITIES[i]
        row = rows - 1 if cx == 1 else 0
        ys = SIDE[cy]
        cs_ref[k, 0:1, :] = ys_ref[ys, Y_SENT[ys].index(i), row:row + 1, :]
        cs_ref[k, 1:2, :] = ys_ref[ys, 5, row:row + 1, :]
        cs_ref[k, 2:8, :] = jnp.zeros((6, 128), jnp.float32)


def stream_slot(slot, edge, slots, mask_ref, post_ref, halo, write):
    below, above = jnp.maximum(slot - 1, 0), jnp.minimum(slot + 1, slots - 1)
    write(0, post_ref[0, slot])
    for i in range(1, Q):
        cz = VELOCITIES[i][2]
        own = post_ref[i, slot]
        value = arrive(
            i, slot, edge, slots, own, post_ref[i, below] if cz == 1 else None,
            post_ref[i, above] if cz == -1 else None, *halo, False)
        mask = mask_ref[slot]
        stay = jnp.where(mask > 0, post_ref[OPPOSITE[i], slot], own)
        write(i, jnp.where((mask & (1 << i)) != 0, value, stay))


def make_mask(slot, edge, slots, fluid_ref, halo, mask_ref):
    rows, width = fluid_ref.shape[1:]
    row = lax.broadcasted_iota(jnp.int32, (rows, width), 0)
    lane = lax.broadcasted_iota(jnp.int32, (rows, width), 1)
    depth = lane % edge
    z, b = lax.axis_index("bz"), lax.axis_index("bxy")
    at_end = (b == 0, b == lax.axis_size("bxy") - 1, z == 0, z == lax.axis_size("bz") - 1)
    fluid = fluid_ref[slot].astype(jnp.float32)
    below = fluid_ref[jnp.maximum(slot - 1, 0)].astype(jnp.float32)
    above = fluid_ref[jnp.minimum(slot + 1, slots - 1)].astype(jnp.float32)
    bits = jnp.ones((rows, width), jnp.int32)
    for i in range(1, Q):
        cx, cy, cz = VELOCITIES[i]
        source = arrive(i, slot, edge, slots, fluid, below if cz == 1 else None,
                        above if cz == -1 else None, *halo, True)
        bit = jnp.where(source > 0.5, 1 << i, 0)
        if cx:
            edge_row = 0 if cx == 1 else rows - 1
            bit = jnp.where((row == edge_row) & at_end[0 if cx == 1 else 1], 0, bit)
        if cy:
            outer = lane < edge if cy == 1 else lane >= width - edge
            bit = jnp.where(outer & at_end[2 if cy == 1 else 3], 0, bit)
        if cz:
            final = 0 if cz == 1 else slots - 1
            face = 0 if cz == 1 else edge - 1
            bit = jnp.where((depth == face) & (slot == final), 0, bit)
        bits = bits | bit
    mask_ref[slot] = jnp.where(fluid_ref[slot] > 0, bits, 0)


def pack_shell(step, i, edge, value, hz, hx, hy):
    rows, width = value.shape
    for axis, c in enumerate(VELOCITIES[i]):
        if not c:
            continue
        n = TURNS[axis].index(i) + step * len(TURNS[axis])
        if axis == 0:
            row = 0 if c == 1 else rows - 1
            hx[n:n + 1, :] = value[row:row + 1, :]
        elif axis == 1:
            per = 128 // edge
            t, g = n // per, n % per
            tile = value[:, :128] if c == 1 else value[:, width - 128:]
            shift = (g * edge - (0 if c == 1 else 128 - edge)) % 128
            tile = pltpu.roll(tile, shift, 1) if shift else tile
            if g:
                lane = lax.broadcasted_iota(jnp.int32, tile.shape, 1)
                tile = jnp.where(lane >= g * edge, tile, hy[:, t * 128:(t + 1) * 128])
            hy[:, t * 128:(t + 1) * 128] = tile
        else:
            depth = lax.broadcasted_iota(jnp.int32, value.shape, 1) % edge
            shift = (n - (0 if c == 1 else edge - 1)) % width
            turned = pltpu.roll(value, shift, 1) if shift else value
            hz[...] = turned if n == 0 else jnp.where(depth == n, turned, hz[...])


def patch_shell(step, i, edge, value, hz, hx, hy):
    rows, width = value.shape
    for axis, c in enumerate(VELOCITIES[i]):
        if not c:
            continue
        n = TURNS[axis].index(i) + step * len(TURNS[axis])
        if axis == 0:
            row = 0 if c == 1 else rows - 1
            index = lax.broadcasted_iota(jnp.int32, value.shape, 0)
            value = jnp.where(index == row, jnp.broadcast_to(hx[n:n + 1, :], value.shape), value)
        elif axis == 1:
            per = 128 // edge
            t, g = n // per, n % per
            shift = ((0 if c == 1 else 128 - edge) - g * edge) % 128
            tile = hy[:, t * 128:(t + 1) * 128]
            tile = pltpu.roll(tile, shift, 1) if shift else tile
            lane = lax.broadcasted_iota(jnp.int32, tile.shape, 1)
            if c == 1:
                value = jnp.concatenate([jnp.where(lane < edge, tile, value[:, :128]), value[:, 128:]], axis=1)
            else:
                value = jnp.concatenate(
                    [value[:, :-128], jnp.where(lane >= 128 - edge, tile, value[:, -128:])], axis=1)
        else:
            depth = lax.broadcasted_iota(jnp.int32, value.shape, 1) % edge
            face = 0 if c == 1 else edge - 1
            shift = (face - n) % width
            turned = pltpu.roll(hz[...], shift, 1) if shift else hz[...]
            value = jnp.where(depth == face, turned, value)
    return value


def pulled(i, edge, here):
    cx, cy, cz = VELOCITIES[i]
    lanes = (cy * edge + cz) % here.shape[1]
    here = pltpu.roll(here, lanes, 1) if lanes else here
    return pltpu.roll(here, cx % here.shape[0], 0) if cx else here


def redo_block(edge, f, hz, hx, hy, mask_ref, next_ref):
    rows, width = f.shape[1:]
    fluid = jnp.where(f[Q] > 0.0, 1.0, 0.0)
    bits = jnp.ones((rows, width), jnp.int32)
    for i in range(1, Q):
        bits = bits | jnp.where(pulled(i, edge, fluid) > 0.5, 1 << i, 0)
    mask_ref[...] = jnp.where(f[Q] > 0.0, bits, 0)

    def put(i, at, value):
        f[(i,) + at] = value

    def stream(step):
        next_ref[0] = f[0]
        for i in range(1, Q):
            own = f[i]
            mask = mask_ref[...]
            stay = jnp.where(mask > 0, f[OPPOSITE[i]], own)
            value = jnp.where((mask & (1 << i)) != 0, pulled(i, edge, own), stay)
            next_ref[i] = patch_shell(step, i, edge, value, hz, hx, hy)

    def rate(at):
        return f[(Q,) + at]

    collide_tiles(rows, width, lambda i, at: f[(i,) + at], rate, put)
    stream(0)
    collide_tiles(rows, width, lambda i, at: next_ref[(i,) + at], rate, put)
    stream(1)


def choose(picks, values):
    taken = []
    for pick in picks:
        out = values[0]
        for j in range(1, len(values)):
            out = jnp.where(pick == j, values[j], out)
        taken.append(out)
    return taken


def cuts_of(n):
    half = (n + 1) // 2
    cuts = (0, half // 2, half, half + (n - half + 1) // 2, n)
    return [slice(cuts[k], cuts[k + 1]) for k in range(4)]


EARLY = cuts_of(Q + 1)
LATE = cuts_of(Q)
PIECES = 11


def solve_kernel(edge, pdfs, relax_ref, fluid_ref, goal_ref, own_out, left_out, right_out, table_ref,
                 a_ref, b_ref, next_ref, mask_ref, ys1, xs1, cs1, yr1, xr1, cr1, ys2, xs2, cs2, yr2, xr2, cr2,
                 hz, hx, hy, early_s, hz_s, hx_s, hy_s, late_s, early_r, hz_r, hx_r, hy_r,
                 early_p, hz_p, hx_p, hy_p, late_p, redo_ref, redo_mask, note_s, note_r, note_m,
                 load_sem, out_sem, halo_send, halo_recv, note_send, note_recv, note_sem, send_sem, recv_sem):
    slots, rows, width = fluid_ref.shape
    nz, nb = lax.axis_size("bz"), lax.axis_size("bxy")
    z, b = lax.axis_index("bz"), lax.axis_index("bxy")

    loads = [pltpu.make_async_copy(pdfs.at[slice(s.start, min(s.stop, Q))], a_ref.at[slice(s.start, min(s.stop, Q))],
                                   load_sem.at[n]) for n, s in enumerate(EARLY)]
    for load in loads:
        load.start()

    across = math.isqrt(nb // 2)
    row = 2 * across
    bends = across == 2 and nb == 2 * row
    cut = row - 1 if bends else nb
    low, high = cut + 1 - row, cut + row
    no = b < 0
    goes_right, goes_left = (b < nb - 1) & (b != cut), (b > 0) & (b != cut + 1)
    at_cut, past_cut, is_low, is_high = (
        (b == cut, b == cut + 1, b == low, b == high) if bends else (no, no, no, no))

    def there(dz, db):
        exists = None
        for at, step, count in ((z, dz, nz), (b, db, nb)):
            if step:
                inside = at < count - 1 if step == 1 else at > 0
                exists = inside if exists is None else exists & inside
        return exists

    ways = [(1, 0), (-1, 0), (0, 1), (0, -1)] + [(VELOCITIES[i][1], VELOCITIES[i][0]) for i in CORNERS]
    meets = [(there(dz, db), (z + dz, b + db)) for dz, db in ways]
    if bends:
        for who in (at_cut, past_cut):
            meets += [(who, (z, low)), (who, (z, high))]
        for who in (is_low, is_high):
            meets += [(who, (z, cut)), (who, (z, cut + 1))]
    barrier = pltpu.get_barrier_semaphore()
    count = 0
    for who, peer in meets:
        count = count + who.astype(jnp.int32)

        @pl.when(who)
        def _():
            pl.semaphore_signal(barrier, inc=1, device_id=peer, device_id_type=MESH)

    pl.semaphore_wait(barrier, count)

    goal = [goal_ref[0, 0, j] for j in range(slots)]
    base = b * slots

    def flag(t):
        return t.astype(jnp.int32)

    def nth(hits, n):
        before, found = jnp.int32(0), jnp.int32(0)
        for j in range(slots):
            found = found + jnp.where(hits[j] & (before == n), j, 0)
            before = before + flag(hits[j])
        return found

    to_right = [g >= base + slots for g in goal]
    to_left = [g < base for g in goal]
    first_pick = (nth(to_right, 0), nth(to_left, 0))
    second_pick = (nth(to_right, 1), nth(to_left, 1))

    at_row = lax.broadcasted_iota(jnp.int32, note_s.shape, 0)
    note = jnp.zeros(note_s.shape, jnp.int32)
    for j in range(slots):
        note = jnp.where(at_row == j, goal[j], note)
    note_s[...] = note

    def note_copy(n):
        db = 1 if n == 0 else -1
        return remote(note_s, note_r.at[n], note_send.at[n], note_recv.at[n], (z, b + db))

    for n, db in ((0, 1), (1, -1)):
        @pl.when(there(0, db))
        def _():
            note_copy(n).start()

    pieces = [(early_s.at[0, s], early_s.at[1, s], early_r.at[0, s], early_r.at[1, s], early_p.at[s], n < 2)
              for n, s in enumerate(EARLY)]
    for s, r, p, first in ((hz_s, hz_r, hz_p, True), (hx_s, hx_r, hx_p, False), (hy_s, hy_r, hy_p, False)):
        pieces.append((s.at[0], s.at[1], r.at[0], r.at[1], p, first))
    pieces += [(late_s.at[0, s], late_s.at[1, s], left_out.at[1, s], right_out.at[1, s], late_p.at[s], n >= 2)
               for n, s in enumerate(LATE)]

    def send(p):
        to_r, to_l, from_l, from_r, passing, first = pieces[p]

        @pl.when(goes_right)
        def _():
            remote(to_r, from_l, send_sem.at[0, p], recv_sem.at[0, p], (z, b + 1)).start()

        @pl.when(goes_left)
        def _():
            remote(to_l, from_r, send_sem.at[1, p], recv_sem.at[1, p], (z, b - 1)).start()

        if bends:
            @pl.when(at_cut)
            def _():
                remote(to_r, passing, send_sem.at[0, p], recv_sem.at[2, p], (z, low if first else high)).start()

            @pl.when(past_cut)
            def _():
                remote(to_l, passing, send_sem.at[1, p], recv_sem.at[2, p], (z, high if first else low)).start()

    def forward(p):
        to_r, to_l, from_l, from_r, passing, first = pieces[p]
        if bends:
            for who, ahead in ((is_low, True), (is_high, False)):
                @pl.when(who)
                def _():
                    remote(to_r, passing, send_sem.at[2, p], recv_sem.at[2, p], (z, cut)).wait_recv()
                    if first == ahead:
                        remote(passing, from_l, send_sem.at[2, p], recv_sem.at[0, p], (z, cut + 1)).start()
                    else:
                        remote(passing, from_r, send_sem.at[2, p], recv_sem.at[1, p], (z, cut)).start()

    def arrived(p):
        to_r, to_l, from_l, from_r, passing, first = pieces[p]

        @pl.when(b > 0)
        def _():
            remote(to_r, from_l, send_sem.at[0, p], recv_sem.at[0, p], (z, b - 1)).wait_recv()

        @pl.when(b < nb - 1)
        def _():
            remote(to_l, from_r, send_sem.at[1, p], recv_sem.at[1, p], (z, b + 1)).wait_recv()

    def sent(p):
        to_r, to_l, from_l, from_r, passing, first = pieces[p]

        @pl.when(b < nb - 1)
        def _():
            remote(to_r, from_l, send_sem.at[0, p], recv_sem.at[0, p], (z, b + 1)).wait_send()

        @pl.when(b > 0)
        def _():
            remote(to_l, from_r, send_sem.at[1, p], recv_sem.at[1, p], (z, b - 1)).wait_send()

        if bends:
            @pl.when(is_low | is_high)
            def _():
                remote(passing, from_l, send_sem.at[2, p], recv_sem.at[0, p], (z, cut)).wait_send()

    for n, s in enumerate(EARLY):
        loads[n].wait()

        def gather(i, carry):
            early_s[0, i], early_s[1, i] = choose(first_pick, [a_ref[i, j] for j in range(slots)])
            return carry

        lax.fori_loop(s.start, min(s.stop, Q), gather, 0)
        if s.stop == Q + 1:
            early_s[0, Q], early_s[1, Q] = choose(
                first_pick, [jnp.where(fluid_ref[j] > 0, relax_ref[j], 0.0) for j in range(slots)])
        if n < 1:
            send(n)

    def rate_of(slot):
        return lambda at: jnp.where(fluid_ref[(slot,) + at] > 0, relax_ref[(slot,) + at], 0.0)

    def first_step(slot, carry):
        def put(i, at, value):
            a_ref[(i, slot) + at] = value

        collide_tiles(rows, width, lambda i, at: a_ref[(i, slot) + at], rate_of(slot), put)
        emit_halo(slot, edge, a_ref, fluid_ref, ys1, xs1)
        return carry

    def routes(step):
        ys, xs, cs, yr, xr, cr = ((ys1, xs1, cs1, yr1, xr1, cr1), (ys2, xs2, cs2, yr2, xr2, cr2))[step]
        ends = [(ys.at[0], yr.at[0]), (ys.at[1], yr.at[1]), (xs.at[0], xr.at[0]), (xs.at[1], xr.at[1])]
        ends += [(cs.at[k], cr.at[k]) for k in range(4)]
        return [(src, dst, dz, db, step * 8 + n) for n, ((src, dst), (dz, db)) in enumerate(zip(ends, ways))]

    def exchange(step):
        for src, dst, dz, db, n in routes(step):
            @pl.when(there(dz, db))
            def _():
                remote(src, dst, halo_send.at[n], halo_recv.at[n], (z + dz, b + db)).start()

    def await_halo(step):
        for src, dst, dz, db, n in routes(step):
            @pl.when(there(-dz, -db))
            def _():
                remote(src, dst, halo_send.at[n], halo_recv.at[n], (z - dz, b - db)).wait_recv()

    ys1[...] = jnp.zeros(ys1.shape, jnp.float32)
    ys2[...] = jnp.zeros(ys2.shape, jnp.float32)
    lax.fori_loop(0, slots, first_step, 0)
    emit_corners(rows, ys1, cs1)
    exchange(0)
    send(1)
    send(2)
    await_halo(0)

    def middle_step(slot, carry):
        halo = (yr1, xr1, cr1)
        make_mask(slot, edge, slots, fluid_ref, halo, mask_ref)

        def write(i, value):
            next_ref[i] = value
            pack_shell(0, i, edge, value, hz.at[slot], hx.at[slot], hy.at[slot])

        stream_slot(slot, edge, slots, mask_ref, a_ref, halo, write)

        def put(i, at, value):
            b_ref[(i, slot) + at] = value

        collide_tiles(rows, width, lambda i, at: next_ref[(i,) + at], rate_of(slot), put)
        emit_halo(slot, edge, b_ref, fluid_ref, ys2, xs2)
        return carry

    lax.fori_loop(0, slots, middle_step, 0)
    emit_corners(rows, ys2, cs2)
    exchange(1)
    send(3)
    for n in (0, 2, 1, 3):
        forward(n)
    await_halo(1)

    def last_step(slot, carry):
        def write(i, value):
            a_ref[i, slot] = value
            pack_shell(1, i, edge, value, hz.at[slot], hx.at[slot], hy.at[slot])

        stream_slot(slot, edge, slots, mask_ref, b_ref, (yr2, xr2, cr2), write)
        return carry

    lax.fori_loop(0, slots, last_step, 0)
    keep = pltpu.make_async_copy(a_ref, own_out, out_sem.at[2])
    keep.start()
    for shell, staged in ((hz, hz_s), (hx, hx_s), (hy, hy_s)):
        staged[0], staged[1] = choose(first_pick, [shell[j] for j in range(slots)])
    for p in range(4, 7):
        send(p)
    for n, s in enumerate(LATE):
        def gather(i, carry):
            late_s[0, i], late_s[1, i] = choose(second_pick, [a_ref[i, j] for j in range(slots)])
            return carry

        lax.fori_loop(s.start, s.stop, gather, 0)
        send(7 + n)

    for p in (4, 5, 6):
        forward(p)
    for p in range(7):
        arrived(p)

    def redo(side, carry):
        redo_block(edge, early_r.at[side], hz_r.at[side], hx_r.at[side], hy_r.at[side], redo_mask, redo_ref.at[side])
        return carry

    lax.fori_loop(jnp.where(b > 0, 0, 1), jnp.where(b < nb - 1, 2, 1), redo, 0)
    redone = [(b > 0, pltpu.make_async_copy(redo_ref.at[0], left_out.at[0], out_sem.at[0])),
              (b < nb - 1, pltpu.make_async_copy(redo_ref.at[1], right_out.at[0], out_sem.at[1]))]
    for who, copy in redone:
        @pl.when(who)
        def _():
            copy.start()

    for p in (7, 9, 8, 10):
        forward(p)

    for n, db in ((0, 1), (1, -1)):
        @pl.when(there(0, -db))
        def _():
            remote(note_s, note_r.at[n], note_send.at[n], note_recv.at[n], (z, b - db)).wait_recv()

        @pl.when(there(0, db))
        def _():
            note_copy(n).wait_send()

    fetch = pltpu.make_async_copy(note_r, note_m, note_sem.at[0])
    fetch.start()
    fetch.wait()
    kind = [jnp.int32(0)] * slots
    index = [jnp.int32(k) for k in range(slots)]
    for k in range(slots):
        for j in range(slots):
            index[k] = jnp.where(goal[j] == base + k, j, index[k])
    for source, valid in ((1, b > 0), (2, b < nb - 1)):
        rank = jnp.int32(0)
        for j in range(slots):
            value = note_m[source - 1, j, 0]
            for k in range(slots):
                hit = valid & (value == base + k)
                kind[k] = jnp.where(hit, source, kind[k])
                index[k] = jnp.where(hit, rank, index[k])
            rank = rank + flag(valid & (value >= base) & (value < base + slots))
    for source in range(3):
        held = jnp.int32(0)
        for k in range(slots):
            held = jnp.where(kind[k] == source, index[k], held)
            table_ref[source, k] = held
    for k in range(slots):
        table_ref[3, k] = kind[k]

    for step in range(2):
        for src, dst, dz, db, n in routes(step):
            @pl.when(there(dz, db))
            def _():
                remote(src, dst, halo_send.at[n], halo_recv.at[n], (z + dz, b + db)).wait_send()

    for p in range(7):
        sent(p)
    keep.wait()
    for who, copy in redone:
        @pl.when(who)
        def _():
            copy.wait()

    for p in range(7, PIECES):
        sent(p)
        arrived(p)


def solve(pdfs, relax, fluid, targets):
    q, slots, rows, width = pdfs.shape
    edge = rows
    f32, i32 = jnp.float32, jnp.int32
    hbm = pl.BlockSpec(memory_space=pl.ANY)
    vmem = pl.BlockSpec(memory_space=pltpu.VMEM)
    smem = pl.BlockSpec(memory_space=pltpu.SMEM)
    per = 128 // edge
    turns = 2 * len(TURNS[0])
    x_rows = -(-turns // 8) * 8
    y_lanes = -(-turns // per) * 128
    ys, xs, cs = (2, 6, rows, 128), (2, slots, 8, width), (4, 8, 128)

    def shells(lead):
        return [pltpu.VMEM(lead + s, f32) for s in ((rows, width), (x_rows, width), (rows, y_lanes))]

    halo = [pltpu.VMEM(s, f32) for s in (ys, xs, cs)]
    dma = pltpu.SemaphoreType.DMA
    scratch = [pltpu.VMEM(pdfs.shape, f32), pltpu.VMEM(pdfs.shape, f32), pltpu.VMEM((q, rows, width), f32),
               pltpu.VMEM(fluid.shape, i32)] + halo * 4
    scratch += shells((slots,))
    scratch += [pltpu.VMEM((2, q + 1, rows, width), f32)] + shells((2,)) + [pltpu.VMEM((2, q, rows, width), f32)]
    scratch += [pltpu.VMEM((2, q + 1, rows, width), f32)] + shells((2,))
    scratch += [pltpu.VMEM((q + 1, rows, width), f32)] + shells(()) + [pltpu.VMEM((q, rows, width), f32)]
    scratch += [pltpu.VMEM((2, q, rows, width), f32), pltpu.VMEM((rows, width), i32)]
    scratch += [pltpu.VMEM((8, 128), i32), pltpu.VMEM((2, 8, 128), i32), pltpu.SMEM((2, 8, 128), i32)]
    scratch += [dma((4,)), dma((3,)), dma((16,)), dma((16,)), dma((2,)), dma((2,)), dma((1,)),
                dma((3, PIECES)), dma((3, PIECES))]
    got = jax.ShapeDtypeStruct((2, q, rows, width), f32)
    return pl.pallas_call(
        functools.partial(solve_kernel, edge),
        out_shape=[jax.ShapeDtypeStruct(pdfs.shape, f32), got, got, jax.ShapeDtypeStruct((4, slots), i32)],
        in_specs=[hbm, vmem, vmem, smem], out_specs=[hbm, hbm, hbm, smem], scratch_shapes=scratch,
        compiler_params=pltpu.CompilerParams(collective_id=0, has_side_effects=True, vmem_limit_bytes=VMEM_LIMIT),
        name="solve",
    )(pdfs, relax, fluid, targets)


def place_kernel(table_ref, final_ref, left_ref, right_ref, out_ref):
    kind = table_ref[3, pl.program_id(0)]

    @pl.when(kind == 0)
    def _():
        out_ref[...] = final_ref[...]

    @pl.when(kind == 1)
    def _():
        out_ref[:, 0] = left_ref[0]

    @pl.when(kind == 2)
    def _():
        out_ref[:, 0] = right_ref[0]


def place(final, left, right, table):
    q, blocks, rows, width = final.shape
    block = (q, 1, rows, width)

    def taken(kind):
        return pl.BlockSpec((1, q, rows, width), lambda k, table: (table[kind, k], 0, 0, 0))

    return pl.pallas_call(
        place_kernel,
        out_shape=jax.ShapeDtypeStruct(final.shape, final.dtype),
        grid_spec=pltpu.PrefetchScalarGridSpec(
            num_scalar_prefetch=1, grid=(blocks,),
            in_specs=[pl.BlockSpec(block, lambda k, table: (0, table[0, k], 0, 0)), taken(1), taken(2)],
            out_specs=pl.BlockSpec(block, lambda k, table: (0, k, 0, 0))),
        compiler_params=pltpu.CompilerParams(vmem_limit_bytes=VMEM_LIMIT),
        name="place",
    )(table, final, left, right)


def on_device(pdfs, relax, fluid, targets):
    own, left, right, table = solve(pdfs, relax, fluid, targets)
    return place(own, left, right, table)


def solution(mesh):
    placed = (
        P(None, None, "bxy", "bz"),
        P(None, "bxy", "bz"),
        P(None, "bxy", "bz"),
        P("bz", "bxy", None),
    )
    return jax.shard_map(
        on_device, mesh=mesh, in_specs=placed, out_specs=P(None, None, "bxy", "bz"), check_vma=False
    )
```

```python
import functools
import math

import jax
import jax.numpy as jnp
from jax import lax
from jax.experimental import pallas as pl
from jax.experimental.pallas import tpu as pltpu
from jax.sharding import PartitionSpec as P

MESH = pl.DeviceIdType.MESH
VELOCITIES = (
    (0, 0, 0), (1, 0, 0), (-1, 0, 0), (0, 1, 0), (0, -1, 0), (0, 0, 1), (0, 0, -1),
    (1, 1, 0), (-1, -1, 0), (1, -1, 0), (-1, 1, 0), (1, 0, 1), (-1, 0, -1),
    (1, 0, -1), (-1, 0, 1), (0, 1, 1), (0, -1, -1), (0, 1, -1), (0, -1, 1),
)
OPPOSITE = (0, 2, 1, 4, 3, 6, 5, 8, 7, 10, 9, 12, 11, 14, 13, 16, 15, 18, 17)
Q = 19
TURNS = tuple(tuple(i for i in range(Q) if VELOCITIES[i][axis]) for axis in range(3))
Y_SENT = tuple(tuple(i for i in range(Q) if VELOCITIES[i][1] == c) for c in (1, -1))
X_SENT = tuple(tuple(i for i in range(Q) if VELOCITIES[i][0] == c) for c in (1, -1))
CORNERS = (7, 8, 9, 10)
SIDE = {1: 0, -1: 1}
VMEM_LIMIT = 60 * 1024 * 1024


def collide(f, rate):
    pair = {i: (f[i] + f[i + 1], f[i] - f[i + 1]) for i in range(1, Q, 2)}
    density = f[0]
    for i in range(1, Q, 2):
        density = density + pair[i][0]
    scale = 3.0 / density
    flow = []
    for axis in range(3):
        total = None
        for i in range(1, Q, 2):
            c = VELOCITIES[i][axis]
            if c:
                d = pair[i][1]
                total = d if total is None else (total + d if c == 1 else total - d)
        flow.append(total * scale)
    base = 1.0 - (flow[0] * flow[0] + flow[1] * flow[1] + flow[2] * flow[2]) * (1.0 / 6.0)
    keep = 1.0 - rate
    drive = rate * density
    post = [None] * Q
    post[0] = keep * f[0] + (drive * (1.0 / 3.0)) * base
    near, far = drive * (1.0 / 18.0), drive * (1.0 / 36.0)
    for i in range(1, Q, 2):
        along = None
        for axis in range(3):
            c = VELOCITIES[i][axis]
            if c:
                along = flow[axis] if along is None else (along + flow[axis] if c == 1 else along - flow[axis])
        even = base + 0.5 * (along * along)
        weight = near if i < 7 else far
        post[i] = keep * f[i] + weight * (even + along)
        post[i + 1] = keep * f[i + 1] + weight * (even - along)
    return post


def remote(src, dst, send_sem, recv_sem, device):
    return pltpu.make_async_remote_copy(
        src_ref=src, dst_ref=dst, send_sem=send_sem, recv_sem=recv_sem, device_id=device, device_id_type=MESH)


def lane_shift(velocity, slot, edge, here, below, above, beside):
    _cx, cy, cz = velocity
    width = here.shape[1]
    step = cy * edge + cz
    moved = here if step == 0 else pltpu.roll(here, step % width, 1)
    if cz:
        depth = lax.broadcasted_iota(jnp.int32, here.shape, 1) % edge
        other, face = (below, 0) if cz == 1 else (above, edge - 1)
        carry = step - cz * edge
        wrapped = other if carry == 0 else pltpu.roll(other, carry % width, 1)
        moved = jnp.where(depth == face, wrapped, moved)
    if cy:
        lane = lax.broadcasted_iota(jnp.int32, (here.shape[0], 128), 1)
        offset = 128 if cy == 1 else 256 - edge
        outside = pltpu.roll(beside, lax.rem(offset + cz + 128 - slot * edge, 128), 1)
        if cy == 1:
            moved = jnp.concatenate([jnp.where(lane < edge, outside, moved[:, :128]), moved[:, 128:]], axis=1)
        else:
            moved = jnp.concatenate(
                [moved[:, :-128], jnp.where(lane >= 128 - edge, outside, moved[:, -128:])], axis=1)
    return moved


def arrive(i, slot, edge, slots, here, below, above, yr_ref, xr_ref, cr_ref, fluid):
    velocity = cx, cy, cz = VELOCITIES[i]
    beside = None
    if cy:
        side = SIDE[cy]
        beside = yr_ref[side, 5 if fluid else Y_SENT[side].index(i)]
    moved = lane_shift(velocity, slot, edge, here, below, above, beside)
    if cx:
        side = SIDE[cx]
        row = 5 if fluid else X_SENT[side].index(i)
        rows = moved.shape[0]

        def plane(s):
            return jnp.broadcast_to(xr_ref[side, s, row:row + 1, :], (8, moved.shape[1]))

        corner = None
        if cy:
            k = CORNERS.index(i)
            n = 1 if fluid else 0
            corner = jnp.broadcast_to(cr_ref[k, n:n + 1, :], (8, 128))
        entering = lane_shift(
            velocity, slot, edge, plane(slot), plane(jnp.maximum(slot - 1, 0)) if cz == 1 else None,
            plane(jnp.minimum(slot + 1, slots - 1)) if cz == -1 else None, corner)
        index = lax.broadcasted_iota(jnp.int32, (8, moved.shape[1]), 0)
        moved = pltpu.roll(moved, cx % rows, 0)
        if cx == 1:
            moved = jnp.concatenate([jnp.where(index == 0, entering, moved[:8]), moved[8:]], axis=0)
        else:
            moved = jnp.concatenate([moved[:-8], jnp.where(index == 7, entering, moved[-8:])], axis=0)
    return moved


def collide_tiles(rows, width, read, rate, write):
    tiles = width // 128

    def body(step, carry):
        r = pl.multiple_of((step // tiles) * 8, 8)
        c = pl.multiple_of((step % tiles) * 128, 128)
        at = (pl.ds(r, 8), pl.ds(c, 128))
        post = collide([read(i, at) for i in range(Q)], rate(at))
        for i in range(Q):
            write(i, at, post[i])
        return carry

    lax.fori_loop(0, (rows // 8) * tiles, body, 0, unroll=4)


def emit_halo(slot, edge, post_ref, fluid_ref, ys_ref, xs_ref):
    rows, width = fluid_ref.shape[1:]
    lane = lax.broadcasted_iota(jnp.int32, (rows, 128), 1)
    mine = lane // edge == slot
    for side, first in ((0, width - 128), (1, 0)):
        turn = lax.rem(slot * edge + (edge if side == 0 else 0), 128)
        for n in range(6):
            if n < 5:
                tile = post_ref[Y_SENT[side][n], slot, :, first:first + 128]
            else:
                tile = fluid_ref[slot, :, first:first + 128].astype(jnp.float32)
            ys_ref[side, n] = jnp.where(mine, pltpu.roll(tile, turn, 1), ys_ref[side, n])
    for side, row in ((0, rows - 1), (1, 0)):
        for n in range(5):
            xs_ref[side, slot, n:n + 1, :] = post_ref[X_SENT[side][n], slot, row:row + 1, :]
        xs_ref[side, slot, 5:6, :] = fluid_ref[slot, row:row + 1, :].astype(jnp.float32)
        xs_ref[side, slot, 6:8, :] = jnp.zeros((2, width), jnp.float32)


def emit_corners(rows, ys_ref, cs_ref):
    for k, i in enumerate(CORNERS):
        cx, cy, _z = VELOCITIES[i]
        row = rows - 1 if cx == 1 else 0
        ys = SIDE[cy]
        cs_ref[k, 0:1, :] = ys_ref[ys, Y_SENT[ys].index(i), row:row + 1, :]
        cs_ref[k, 1:2, :] = ys_ref[ys, 5, row:row + 1, :]
        cs_ref[k, 2:8, :] = jnp.zeros((6, 128), jnp.float32)


def stream_slot(slot, edge, slots, mask_ref, post_ref, halo, write):
    below, above = jnp.maximum(slot - 1, 0), jnp.minimum(slot + 1, slots - 1)
    write(0, post_ref[0, slot])
    for i in range(1, Q):
        cz = VELOCITIES[i][2]
        own = post_ref[i, slot]
        value = arrive(
            i, slot, edge, slots, own, post_ref[i, below] if cz == 1 else None,
            post_ref[i, above] if cz == -1 else None, *halo, False)
        mask = mask_ref[slot]
        stay = jnp.where(mask > 0, post_ref[OPPOSITE[i], slot], own)
        write(i, jnp.where((mask & (1 << i)) != 0, value, stay))


def make_mask(slot, edge, slots, fluid_ref, halo, mask_ref):
    rows, width = fluid_ref.shape[1:]
    row = lax.broadcasted_iota(jnp.int32, (rows, width), 0)
    lane = lax.broadcasted_iota(jnp.int32, (rows, width), 1)
    depth = lane % edge
    z, b = lax.axis_index("bz"), lax.axis_index("bxy")
    at_end = (b == 0, b == lax.axis_size("bxy") - 1, z == 0, z == lax.axis_size("bz") - 1)
    fluid = fluid_ref[slot].astype(jnp.float32)
    below = fluid_ref[jnp.maximum(slot - 1, 0)].astype(jnp.float32)
    above = fluid_ref[jnp.minimum(slot + 1, slots - 1)].astype(jnp.float32)
    bits = jnp.ones((rows, width), jnp.int32)
    for i in range(1, Q):
        cx, cy, cz = VELOCITIES[i]
        source = arrive(i, slot, edge, slots, fluid, below if cz == 1 else None,
                        above if cz == -1 else None, *halo, True)
        bit = jnp.where(source > 0.5, 1 << i, 0)
        if cx:
            edge_row = 0 if cx == 1 else rows - 1
            bit = jnp.where((row == edge_row) & at_end[0 if cx == 1 else 1], 0, bit)
        if cy:
            outer = lane < edge if cy == 1 else lane >= width - edge
            bit = jnp.where(outer & at_end[2 if cy == 1 else 3], 0, bit)
        if cz:
            final = 0 if cz == 1 else slots - 1
            face = 0 if cz == 1 else edge - 1
            bit = jnp.where((depth == face) & (slot == final), 0, bit)
        bits = bits | bit
    mask_ref[slot] = jnp.where(fluid_ref[slot] > 0, bits, 0)


def pack_shell(step, i, edge, value, hz, hx, hy):
    rows, width = value.shape
    for axis, c in enumerate(VELOCITIES[i]):
        if not c:
            continue
        n = TURNS[axis].index(i) + step * len(TURNS[axis])
        if axis == 0:
            row = 0 if c == 1 else rows - 1
            hx[n:n + 1, :] = value[row:row + 1, :]
        elif axis == 1:
            per = 128 // edge
            t, g = n // per, n % per
            tile = value[:, :128] if c == 1 else value[:, width - 128:]
            shift = (g * edge - (0 if c == 1 else 128 - edge)) % 128
            tile = pltpu.roll(tile, shift, 1) if shift else tile
            if g:
                lane = lax.broadcasted_iota(jnp.int32, tile.shape, 1)
                tile = jnp.where(lane >= g * edge, tile, hy[:, t * 128:(t + 1) * 128])
            hy[:, t * 128:(t + 1) * 128] = tile
        else:
            depth = lax.broadcasted_iota(jnp.int32, value.shape, 1) % edge
            shift = (n - (0 if c == 1 else edge - 1)) % width
            turned = pltpu.roll(value, shift, 1) if shift else value
            hz[...] = turned if n == 0 else jnp.where(depth == n, turned, hz[...])


def patch_shell(step, i, edge, value, hz, hx, hy):
    rows, width = value.shape
    for axis, c in enumerate(VELOCITIES[i]):
        if not c:
            continue
        n = TURNS[axis].index(i) + step * len(TURNS[axis])
        if axis == 0:
            row = 0 if c == 1 else rows - 1
            index = lax.broadcasted_iota(jnp.int32, value.shape, 0)
            value = jnp.where(index == row, jnp.broadcast_to(hx[n:n + 1, :], value.shape), value)
        elif axis == 1:
            per = 128 // edge
            t, g = n // per, n % per
            shift = ((0 if c == 1 else 128 - edge) - g * edge) % 128
            tile = hy[:, t * 128:(t + 1) * 128]
            tile = pltpu.roll(tile, shift, 1) if shift else tile
            lane = lax.broadcasted_iota(jnp.int32, tile.shape, 1)
            if c == 1:
                value = jnp.concatenate([jnp.where(lane < edge, tile, value[:, :128]), value[:, 128:]], axis=1)
            else:
                value = jnp.concatenate(
                    [value[:, :-128], jnp.where(lane >= 128 - edge, tile, value[:, -128:])], axis=1)
        else:
            depth = lax.broadcasted_iota(jnp.int32, value.shape, 1) % edge
            face = 0 if c == 1 else edge - 1
            shift = (face - n) % width
            turned = pltpu.roll(hz[...], shift, 1) if shift else hz[...]
            value = jnp.where(depth == face, turned, value)
    return value


def pulled(i, edge, here):
    cx, cy, cz = VELOCITIES[i]
    lanes = (cy * edge + cz) % here.shape[1]
    here = pltpu.roll(here, lanes, 1) if lanes else here
    return pltpu.roll(here, cx % here.shape[0], 0) if cx else here


def redo_block(edge, f, hz, hx, hy, mask_ref, next_ref):
    rows, width = f.shape[1:]
    fluid = jnp.where(f[Q] > 0.0, 1.0, 0.0)
    bits = jnp.ones((rows, width), jnp.int32)
    for i in range(1, Q):
        bits = bits | jnp.where(pulled(i, edge, fluid) > 0.5, 1 << i, 0)
    mask_ref[...] = jnp.where(f[Q] > 0.0, bits, 0)

    def put(i, at, value):
        f[(i,) + at] = value

    def stream(step):
        next_ref[0] = f[0]
        for i in range(1, Q):
            own = f[i]
            mask = mask_ref[...]
            stay = jnp.where(mask > 0, f[OPPOSITE[i]], own)
            value = jnp.where((mask & (1 << i)) != 0, pulled(i, edge, own), stay)
            next_ref[i] = patch_shell(step, i, edge, value, hz, hx, hy)

    def rate(at):
        return f[(Q,) + at]

    collide_tiles(rows, width, lambda i, at: f[(i,) + at], rate, put)
    stream(0)
    collide_tiles(rows, width, lambda i, at: next_ref[(i,) + at], rate, put)
    stream(1)


def choose(picks, values):
    taken = []
    for pick in picks:
        out = values[0]
        for j in range(1, len(values)):
            out = jnp.where(pick == j, values[j], out)
        taken.append(out)
    return taken


def cuts_of(n):
    half = (n + 1) // 2
    cuts = (0, half // 2, half, half + (n - half + 1) // 2, n)
    return [slice(cuts[k], cuts[k + 1]) for k in range(4)]


EARLY = cuts_of(Q + 1)
LATE = cuts_of(Q)
PIECES = 11


def solve_kernel(edge, pdfs, relax_ref, fluid_ref, goal_ref, own_out, left_out, right_out, table_ref,
                 a_ref, b_ref, next_ref, mask_ref, ys1, xs1, cs1, yr1, xr1, cr1, ys2, xs2, cs2, yr2, xr2, cr2,
                 hz, hx, hy, early_s, hz_s, hx_s, hy_s, late_s, early_r, hz_r, hx_r, hy_r,
                 early_p, hz_p, hx_p, hy_p, late_p, redo_ref, redo_mask, note_s, note_r, note_m,
                 load_sem, out_sem, halo_send, halo_recv, note_send, note_recv, note_sem, send_sem, recv_sem):
    slots, rows, width = fluid_ref.shape
    nz, nb = lax.axis_size("bz"), lax.axis_size("bxy")
    z, b = lax.axis_index("bz"), lax.axis_index("bxy")

    loads = [pltpu.make_async_copy(pdfs.at[slice(s.start, min(s.stop, Q))], a_ref.at[slice(s.start, min(s.stop, Q))],
                                   load_sem.at[n]) for n, s in enumerate(EARLY)]
    for load in loads:
        load.start()

    across = math.isqrt(nb // 2)
    row = 2 * across
    bends = across == 2 and nb == 2 * row
    cut = row - 1 if bends else nb
    low, high = cut + 1 - row, cut + row
    no = b < 0
    goes_right, goes_left = (b < nb - 1) & (b != cut), (b > 0) & (b != cut + 1)
    at_cut, past_cut, is_low, is_high = (
        (b == cut, b == cut + 1, b == low, b == high) if bends else (no, no, no, no))

    def there(dz, db):
        exists = None
        for at, step, count in ((z, dz, nz), (b, db, nb)):
            if step:
                inside = at < count - 1 if step == 1 else at > 0
                exists = inside if exists is None else exists & inside
        return exists

    ways = [(1, 0), (-1, 0), (0, 1), (0, -1)] + [(VELOCITIES[i][1], VELOCITIES[i][0]) for i in CORNERS]
    meets = [(there(dz, db), (z + dz, b + db)) for dz, db in ways]
    if bends:
        for who in (at_cut, past_cut):
            meets += [(who, (z, low)), (who, (z, high))]
        for who in (is_low, is_high):
            meets += [(who, (z, cut)), (who, (z, cut + 1))]
    barrier = pltpu.get_barrier_semaphore()
    count = 0
    for who, peer in meets:
        count = count + who.astype(jnp.int32)

        @pl.when(who)
        def _():
            pl.semaphore_signal(barrier, inc=1, device_id=peer, device_id_type=MESH)

    pl.semaphore_wait(barrier, count)

    goal = [goal_ref[0, 0, j] for j in range(slots)]
    base = b * slots

    def flag(t):
        return t.astype(jnp.int32)

    def nth(hits, n):
        before, found = jnp.int32(0), jnp.int32(0)
        for j in range(slots):
            found = found + jnp.where(hits[j] & (before == n), j, 0)
            before = before + flag(hits[j])
        return found

    to_right = [g >= base + slots for g in goal]
    to_left = [g < base for g in goal]
    first_pick = (nth(to_right, 0), nth(to_left, 0))
    second_pick = (nth(to_right, 1), nth(to_left, 1))

    at_row = lax.broadcasted_iota(jnp.int32, note_s.shape, 0)
    note = jnp.zeros(note_s.shape, jnp.int32)
    for j in range(slots):
        note = jnp.where(at_row == j, goal[j], note)
    note_s[...] = note

    def note_copy(n):
        db = 1 if n == 0 else -1
        return remote(note_s, note_r.at[n], note_send.at[n], note_recv.at[n], (z, b + db))

    for n, db in ((0, 1), (1, -1)):
        @pl.when(there(0, db))
        def _():
            note_copy(n).start()

    pieces = [(early_s.at[0, s], early_s.at[1, s], early_r.at[0, s], early_r.at[1, s], early_p.at[s], n < 2)
              for n, s in enumerate(EARLY)]
    for s, r, p, first in ((hz_s, hz_r, hz_p, True), (hx_s, hx_r, hx_p, False), (hy_s, hy_r, hy_p, False)):
        pieces.append((s.at[0], s.at[1], r.at[0], r.at[1], p, first))
    pieces += [(late_s.at[0, s], late_s.at[1, s], left_out.at[1, s], right_out.at[1, s], late_p.at[s], n >= 2)
               for n, s in enumerate(LATE)]

    def send_near(p):
        to_r, to_l, from_l, from_r, passing, first = pieces[p]

        @pl.when(goes_right)
        def _():
            remote(to_r, from_l, send_sem.at[0, p], recv_sem.at[0, p], (z, b + 1)).start()

        @pl.when(goes_left)
        def _():
            remote(to_l, from_r, send_sem.at[1, p], recv_sem.at[1, p], (z, b - 1)).start()

    def send_bent(p):
        to_r, to_l, from_l, from_r, passing, first = pieces[p]
        if bends:
            @pl.when(at_cut)
            def _():
                remote(to_r, passing, send_sem.at[0, p], recv_sem.at[2, p], (z, low if first else high)).start()

            @pl.when(past_cut)
            def _():
                remote(to_l, passing, send_sem.at[1, p], recv_sem.at[2, p], (z, high if first else low)).start()

    def forward(p):
        to_r, to_l, from_l, from_r, passing, first = pieces[p]
        if bends:
            for who, ahead in ((is_low, True), (is_high, False)):
                @pl.when(who)
                def _():
                    remote(to_r, passing, send_sem.at[2, p], recv_sem.at[2, p], (z, cut)).wait_recv()
                    if first == ahead:
                        remote(passing, from_l, send_sem.at[2, p], recv_sem.at[0, p], (z, cut + 1)).start()
                    else:
                        remote(passing, from_r, send_sem.at[2, p], recv_sem.at[1, p], (z, cut)).start()

    def arrived(p):
        to_r, to_l, from_l, from_r, passing, first = pieces[p]

        @pl.when(b > 0)
        def _():
            remote(to_r, from_l, send_sem.at[0, p], recv_sem.at[0, p], (z, b - 1)).wait_recv()

        @pl.when(b < nb - 1)
        def _():
            remote(to_l, from_r, send_sem.at[1, p], recv_sem.at[1, p], (z, b + 1)).wait_recv()

    def sent(p):
        to_r, to_l, from_l, from_r, passing, first = pieces[p]

        @pl.when(b < nb - 1)
        def _():
            remote(to_r, from_l, send_sem.at[0, p], recv_sem.at[0, p], (z, b + 1)).wait_send()

        @pl.when(b > 0)
        def _():
            remote(to_l, from_r, send_sem.at[1, p], recv_sem.at[1, p], (z, b - 1)).wait_send()

        if bends:
            @pl.when(is_low | is_high)
            def _():
                remote(passing, from_l, send_sem.at[2, p], recv_sem.at[0, p], (z, cut)).wait_send()

    for n, s in enumerate(EARLY):
        loads[n].wait()

        def gather(i, carry):
            early_s[0, i], early_s[1, i] = choose(first_pick, [a_ref[i, j] for j in range(slots)])
            return carry

        lax.fori_loop(s.start, min(s.stop, Q), gather, 0)
        if s.stop == Q + 1:
            early_s[0, Q], early_s[1, Q] = choose(
                first_pick, [jnp.where(fluid_ref[j] > 0, relax_ref[j], 0.0) for j in range(slots)])
        if n == 0:
            send_near(0)
        if n == 2:
            send_bent(2)

    def rate_of(slot):
        return lambda at: jnp.where(fluid_ref[(slot,) + at] > 0, relax_ref[(slot,) + at], 0.0)

    def first_step(slot, carry):
        def put(i, at, value):
            a_ref[(i, slot) + at] = value

        collide_tiles(rows, width, lambda i, at: a_ref[(i, slot) + at], rate_of(slot), put)
        emit_halo(slot, edge, a_ref, fluid_ref, ys1, xs1)
        return carry

    def routes(step):
        ys, xs, cs, yr, xr, cr = ((ys1, xs1, cs1, yr1, xr1, cr1), (ys2, xs2, cs2, yr2, xr2, cr2))[step]
        ends = [(ys.at[0], yr.at[0]), (ys.at[1], yr.at[1]), (xs.at[0], xr.at[0]), (xs.at[1], xr.at[1])]
        ends += [(cs.at[k], cr.at[k]) for k in range(4)]
        return [(src, dst, dz, db, step * 8 + n) for n, ((src, dst), (dz, db)) in enumerate(zip(ends, ways))]

    def exchange(step):
        for src, dst, dz, db, n in routes(step):
            @pl.when(there(dz, db))
            def _():
                remote(src, dst, halo_send.at[n], halo_recv.at[n], (z + dz, b + db)).start()

    def await_halo(step):
        for src, dst, dz, db, n in routes(step):
            @pl.when(there(-dz, -db))
            def _():
                remote(src, dst, halo_send.at[n], halo_recv.at[n], (z - dz, b - db)).wait_recv()

    ys1[...] = jnp.zeros(ys1.shape, jnp.float32)
    ys2[...] = jnp.zeros(ys2.shape, jnp.float32)
    lax.fori_loop(0, slots, first_step, 0)
    emit_corners(rows, ys1, cs1)
    exchange(0)
    send_near(1)
    send_near(2)
    send_bent(3)
    send_bent(0)
    await_halo(0)
    forward(2)

    def middle_step(slot, carry):
        halo = (yr1, xr1, cr1)
        make_mask(slot, edge, slots, fluid_ref, halo, mask_ref)

        def write(i, value):
            next_ref[i] = value
            pack_shell(0, i, edge, value, hz.at[slot], hx.at[slot], hy.at[slot])

        stream_slot(slot, edge, slots, mask_ref, a_ref, halo, write)

        def put(i, at, value):
            b_ref[(i, slot) + at] = value

        collide_tiles(rows, width, lambda i, at: next_ref[(i,) + at], rate_of(slot), put)
        emit_halo(slot, edge, b_ref, fluid_ref, ys2, xs2)
        return carry

    lax.fori_loop(0, slots, middle_step, 0)
    emit_corners(rows, ys2, cs2)
    exchange(1)
    send_near(3)
    send_bent(1)
    forward(3)
    await_halo(1)

    def last_step(slot, carry):
        def write(i, value):
            a_ref[i, slot] = value
            pack_shell(1, i, edge, value, hz.at[slot], hx.at[slot], hy.at[slot])

        stream_slot(slot, edge, slots, mask_ref, b_ref, (yr2, xr2, cr2), write)
        return carry

    lax.fori_loop(0, slots, last_step, 0)
    keep = pltpu.make_async_copy(a_ref, own_out, out_sem.at[2])
    keep.start()
    for shell, staged in ((hz, hz_s), (hx, hx_s), (hy, hy_s)):
        staged[0], staged[1] = choose(first_pick, [shell[j] for j in range(slots)])
    for p in (5, 6, 4):
        send_near(p)
        send_bent(p)
    for n, s in enumerate(LATE):
        def gather(i, carry):
            late_s[0, i], late_s[1, i] = choose(second_pick, [a_ref[i, j] for j in range(slots)])
            return carry

        lax.fori_loop(s.start, s.stop, gather, 0)
        send_near(7 + n)
        send_bent(7 + n)

    for p in (0, 5, 6, 1, 4, 7, 8):
        forward(p)
    for p in range(7):
        arrived(p)

    def redo(side, carry):
        redo_block(edge, early_r.at[side], hz_r.at[side], hx_r.at[side], hy_r.at[side], redo_mask, redo_ref.at[side])
        return carry

    lax.fori_loop(jnp.where(b > 0, 0, 1), jnp.where(b < nb - 1, 2, 1), redo, 0)
    redone = [(b > 0, pltpu.make_async_copy(redo_ref.at[0], left_out.at[0], out_sem.at[0])),
              (b < nb - 1, pltpu.make_async_copy(redo_ref.at[1], right_out.at[0], out_sem.at[1]))]
    for who, copy in redone:
        @pl.when(who)
        def _():
            copy.start()

    for p in (9, 10):
        forward(p)

    for n, db in ((0, 1), (1, -1)):
        @pl.when(there(0, -db))
        def _():
            remote(note_s, note_r.at[n], note_send.at[n], note_recv.at[n], (z, b - db)).wait_recv()

        @pl.when(there(0, db))
        def _():
            note_copy(n).wait_send()

    fetch = pltpu.make_async_copy(note_r, note_m, note_sem.at[0])
    fetch.start()
    fetch.wait()
    kind = [jnp.int32(0)] * slots
    index = [jnp.int32(k) for k in range(slots)]
    for k in range(slots):
        for j in range(slots):
            index[k] = jnp.where(goal[j] == base + k, j, index[k])
    for source, valid in ((1, b > 0), (2, b < nb - 1)):
        rank = jnp.int32(0)
        for j in range(slots):
            value = note_m[source - 1, j, 0]
            for k in range(slots):
                hit = valid & (value == base + k)
                kind[k] = jnp.where(hit, source, kind[k])
                index[k] = jnp.where(hit, rank, index[k])
            rank = rank + flag(valid & (value >= base) & (value < base + slots))
    for source in range(3):
        held = jnp.int32(0)
        for k in range(slots):
            held = jnp.where(kind[k] == source, index[k], held)
            table_ref[source, k] = held
    for k in range(slots):
        table_ref[3, k] = kind[k]

    for step in range(2):
        for src, dst, dz, db, n in routes(step):
            @pl.when(there(dz, db))
            def _():
                remote(src, dst, halo_send.at[n], halo_recv.at[n], (z + dz, b + db)).wait_send()

    for p in range(7):
        sent(p)
    keep.wait()
    for who, copy in redone:
        @pl.when(who)
        def _():
            copy.wait()

    for p in range(7, PIECES):
        sent(p)
        arrived(p)


def solve(pdfs, relax, fluid, targets):
    q, slots, rows, width = pdfs.shape
    edge = rows
    f32, i32 = jnp.float32, jnp.int32
    hbm = pl.BlockSpec(memory_space=pl.ANY)
    vmem = pl.BlockSpec(memory_space=pltpu.VMEM)
    smem = pl.BlockSpec(memory_space=pltpu.SMEM)
    per = 128 // edge
    turns = 2 * len(TURNS[0])
    x_rows = -(-turns // 8) * 8
    y_lanes = -(-turns // per) * 128
    ys, xs, cs = (2, 6, rows, 128), (2, slots, 8, width), (4, 8, 128)

    def shells(lead):
        return [pltpu.VMEM(lead + s, f32) for s in ((rows, width), (x_rows, width), (rows, y_lanes))]

    halo = [pltpu.VMEM(s, f32) for s in (ys, xs, cs)]
    dma = pltpu.SemaphoreType.DMA
    scratch = [pltpu.VMEM(pdfs.shape, f32), pltpu.VMEM(pdfs.shape, f32), pltpu.VMEM((q, rows, width), f32),
               pltpu.VMEM(fluid.shape, i32)] + halo * 4
    scratch += shells((slots,))
    scratch += [pltpu.VMEM((2, q + 1, rows, width), f32)] + shells((2,)) + [pltpu.VMEM((2, q, rows, width), f32)]
    scratch += [pltpu.VMEM((2, q + 1, rows, width), f32)] + shells((2,))
    scratch += [pltpu.VMEM((q + 1, rows, width), f32)] + shells(()) + [pltpu.VMEM((q, rows, width), f32)]
    scratch += [pltpu.VMEM((2, q, rows, width), f32), pltpu.VMEM((rows, width), i32)]
    scratch += [pltpu.VMEM((8, 128), i32), pltpu.VMEM((2, 8, 128), i32), pltpu.SMEM((2, 8, 128), i32)]
    scratch += [dma((4,)), dma((3,)), dma((16,)), dma((16,)), dma((2,)), dma((2,)), dma((1,)),
                dma((3, PIECES)), dma((3, PIECES))]
    got = jax.ShapeDtypeStruct((2, q, rows, width), f32)
    return pl.pallas_call(
        functools.partial(solve_kernel, edge),
        out_shape=[jax.ShapeDtypeStruct(pdfs.shape, f32), got, got, jax.ShapeDtypeStruct((4, slots), i32)],
        in_specs=[hbm, vmem, vmem, smem], out_specs=[hbm, hbm, hbm, smem], scratch_shapes=scratch,
        compiler_params=pltpu.CompilerParams(collective_id=0, has_side_effects=True, vmem_limit_bytes=VMEM_LIMIT),
        name="solve",
    )(pdfs, relax, fluid, targets)


def place_kernel(table_ref, final_ref, left_ref, right_ref, out_ref):
    kind = table_ref[3, pl.program_id(0)]

    @pl.when(kind == 0)
    def _():
        out_ref[...] = final_ref[...]

    @pl.when(kind == 1)
    def _():
        out_ref[:, 0] = left_ref[0]

    @pl.when(kind == 2)
    def _():
        out_ref[:, 0] = right_ref[0]


def place(final, left, right, table):
    q, blocks, rows, width = final.shape
    block = (q, 1, rows, width)

    def taken(kind):
        return pl.BlockSpec((1, q, rows, width), lambda k, table: (table[kind, k], 0, 0, 0))

    return pl.pallas_call(
        place_kernel,
        out_shape=jax.ShapeDtypeStruct(final.shape, final.dtype),
        grid_spec=pltpu.PrefetchScalarGridSpec(
            num_scalar_prefetch=1, grid=(blocks,),
            in_specs=[pl.BlockSpec(block, lambda k, table: (0, table[0, k], 0, 0)), taken(1), taken(2)],
            out_specs=pl.BlockSpec(block, lambda k, table: (0, k, 0, 0))),
        compiler_params=pltpu.CompilerParams(vmem_limit_bytes=VMEM_LIMIT),
        name="place",
    )(table, final, left, right)


def on_device(pdfs, relax, fluid, targets):
    own, left, right, table = solve(pdfs, relax, fluid, targets)
    return place(own, left, right, table)


def solution(mesh):
    placed = (
        P(None, None, "bxy", "bz"),
        P(None, "bxy", "bz"),
        P(None, "bxy", "bz"),
        P("bz", "bxy", None),
    )
    return jax.shard_map(
        on_device, mesh=mesh, in_specs=placed, out_specs=P(None, None, "bxy", "bz"), check_vma=False
    )
```

```python
import functools
import math

import jax
import jax.numpy as jnp
from jax import lax
from jax.experimental import pallas as pl
from jax.experimental.pallas import tpu as pltpu
from jax.sharding import PartitionSpec as P

MESH = pl.DeviceIdType.MESH
VELOCITIES = (
    (0, 0, 0), (1, 0, 0), (-1, 0, 0), (0, 1, 0), (0, -1, 0), (0, 0, 1), (0, 0, -1),
    (1, 1, 0), (-1, -1, 0), (1, -1, 0), (-1, 1, 0), (1, 0, 1), (-1, 0, -1),
    (1, 0, -1), (-1, 0, 1), (0, 1, 1), (0, -1, -1), (0, 1, -1), (0, -1, 1),
)
OPPOSITE = (0, 2, 1, 4, 3, 6, 5, 8, 7, 10, 9, 12, 11, 14, 13, 16, 15, 18, 17)
Q = 19
TURNS = tuple(tuple(i for i in range(Q) if VELOCITIES[i][axis]) for axis in range(3))
Y_SENT = tuple(tuple(i for i in range(Q) if VELOCITIES[i][1] == c) for c in (1, -1))
X_SENT = tuple(tuple(i for i in range(Q) if VELOCITIES[i][0] == c) for c in (1, -1))
CORNERS = (7, 8, 9, 10)
SIDE = {1: 0, -1: 1}
VMEM_LIMIT = 60 * 1024 * 1024


def collide(f, rate):
    pair = {i: (f[i] + f[i + 1], f[i] - f[i + 1]) for i in range(1, Q, 2)}
    density = f[0]
    for i in range(1, Q, 2):
        density = density + pair[i][0]
    scale = 3.0 / density
    flow = []
    for axis in range(3):
        total = None
        for i in range(1, Q, 2):
            c = VELOCITIES[i][axis]
            if c:
                d = pair[i][1]
                total = d if total is None else (total + d if c == 1 else total - d)
        flow.append(total * scale)
    base = 1.0 - (flow[0] * flow[0] + flow[1] * flow[1] + flow[2] * flow[2]) * (1.0 / 6.0)
    keep = 1.0 - rate
    drive = rate * density
    post = [None] * Q
    post[0] = keep * f[0] + (drive * (1.0 / 3.0)) * base
    near, far = drive * (1.0 / 18.0), drive * (1.0 / 36.0)
    for i in range(1, Q, 2):
        along = None
        for axis in range(3):
            c = VELOCITIES[i][axis]
            if c:
                along = flow[axis] if along is None else (along + flow[axis] if c == 1 else along - flow[axis])
        even = base + 0.5 * (along * along)
        weight = near if i < 7 else far
        post[i] = keep * f[i] + weight * (even + along)
        post[i + 1] = keep * f[i + 1] + weight * (even - along)
    return post


def remote(src, dst, send_sem, recv_sem, device):
    return pltpu.make_async_remote_copy(
        src_ref=src, dst_ref=dst, send_sem=send_sem, recv_sem=recv_sem, device_id=device, device_id_type=MESH)


def lane_shift(velocity, slot, edge, here, below, above, beside):
    _cx, cy, cz = velocity
    width = here.shape[1]
    step = cy * edge + cz
    moved = here if step == 0 else pltpu.roll(here, step % width, 1)
    if cz:
        depth = lax.broadcasted_iota(jnp.int32, here.shape, 1) % edge
        other, face = (below, 0) if cz == 1 else (above, edge - 1)
        carry = step - cz * edge
        wrapped = other if carry == 0 else pltpu.roll(other, carry % width, 1)
        moved = jnp.where(depth == face, wrapped, moved)
    if cy:
        lane = lax.broadcasted_iota(jnp.int32, (here.shape[0], 128), 1)
        offset = 128 if cy == 1 else 256 - edge
        outside = pltpu.roll(beside, lax.rem(offset + cz + 128 - slot * edge, 128), 1)
        if cy == 1:
            moved = jnp.concatenate([jnp.where(lane < edge, outside, moved[:, :128]), moved[:, 128:]], axis=1)
        else:
            moved = jnp.concatenate(
                [moved[:, :-128], jnp.where(lane >= 128 - edge, outside, moved[:, -128:])], axis=1)
    return moved


def arrive(i, slot, edge, slots, here, below, above, yr_ref, xr_ref, cr_ref, fluid):
    velocity = cx, cy, cz = VELOCITIES[i]
    beside = None
    if cy:
        side = SIDE[cy]
        beside = yr_ref[side, 5 if fluid else Y_SENT[side].index(i)]
    moved = lane_shift(velocity, slot, edge, here, below, above, beside)
    if cx:
        side = SIDE[cx]
        row = 5 if fluid else X_SENT[side].index(i)
        rows = moved.shape[0]

        def plane(s):
            return jnp.broadcast_to(xr_ref[side, s, row:row + 1, :], (8, moved.shape[1]))

        corner = None
        if cy:
            k = CORNERS.index(i)
            n = 1 if fluid else 0
            corner = jnp.broadcast_to(cr_ref[k, n:n + 1, :], (8, 128))
        entering = lane_shift(
            velocity, slot, edge, plane(slot), plane(jnp.maximum(slot - 1, 0)) if cz == 1 else None,
            plane(jnp.minimum(slot + 1, slots - 1)) if cz == -1 else None, corner)
        index = lax.broadcasted_iota(jnp.int32, (8, moved.shape[1]), 0)
        moved = pltpu.roll(moved, cx % rows, 0)
        if cx == 1:
            moved = jnp.concatenate([jnp.where(index == 0, entering, moved[:8]), moved[8:]], axis=0)
        else:
            moved = jnp.concatenate([moved[:-8], jnp.where(index == 7, entering, moved[-8:])], axis=0)
    return moved


def collide_tiles(rows, width, read, rate, write):
    tiles = width // 128

    def body(step, carry):
        r = pl.multiple_of((step // tiles) * 8, 8)
        c = pl.multiple_of((step % tiles) * 128, 128)
        at = (pl.ds(r, 8), pl.ds(c, 128))
        post = collide([read(i, at) for i in range(Q)], rate(at))
        for i in range(Q):
            write(i, at, post[i])
        return carry

    lax.fori_loop(0, (rows // 8) * tiles, body, 0, unroll=4)


def emit_halo(slot, edge, post_ref, fluid_ref, ys_ref, xs_ref):
    rows, width = fluid_ref.shape[1:]
    lane = lax.broadcasted_iota(jnp.int32, (rows, 128), 1)
    mine = lane // edge == slot
    for side, first in ((0, width - 128), (1, 0)):
        turn = lax.rem(slot * edge + (edge if side == 0 else 0), 128)
        for n in range(6):
            if n < 5:
                tile = post_ref[Y_SENT[side][n], slot, :, first:first + 128]
            else:
                tile = fluid_ref[slot, :, first:first + 128].astype(jnp.float32)
            ys_ref[side, n] = jnp.where(mine, pltpu.roll(tile, turn, 1), ys_ref[side, n])
    for side, row in ((0, rows - 1), (1, 0)):
        for n in range(5):
            xs_ref[side, slot, n:n + 1, :] = post_ref[X_SENT[side][n], slot, row:row + 1, :]
        xs_ref[side, slot, 5:6, :] = fluid_ref[slot, row:row + 1, :].astype(jnp.float32)
        xs_ref[side, slot, 6:8, :] = jnp.zeros((2, width), jnp.float32)


def emit_corners(rows, ys_ref, cs_ref):
    for k, i in enumerate(CORNERS):
        cx, cy, _z = VELOCITIES[i]
        row = rows - 1 if cx == 1 else 0
        ys = SIDE[cy]
        cs_ref[k, 0:1, :] = ys_ref[ys, Y_SENT[ys].index(i), row:row + 1, :]
        cs_ref[k, 1:2, :] = ys_ref[ys, 5, row:row + 1, :]
        cs_ref[k, 2:8, :] = jnp.zeros((6, 128), jnp.float32)


def stream_slot(slot, edge, slots, mask_ref, post_ref, halo, write):
    below, above = jnp.maximum(slot - 1, 0), jnp.minimum(slot + 1, slots - 1)
    write(0, post_ref[0, slot])
    for i in range(1, Q):
        cz = VELOCITIES[i][2]
        own = post_ref[i, slot]
        value = arrive(
            i, slot, edge, slots, own, post_ref[i, below] if cz == 1 else None,
            post_ref[i, above] if cz == -1 else None, *halo, False)
        mask = mask_ref[slot]
        stay = jnp.where(mask > 0, post_ref[OPPOSITE[i], slot], own)
        write(i, jnp.where((mask & (1 << i)) != 0, value, stay))


def make_mask(slot, edge, slots, fluid_ref, halo, mask_ref):
    rows, width = fluid_ref.shape[1:]
    row = lax.broadcasted_iota(jnp.int32, (rows, width), 0)
    lane = lax.broadcasted_iota(jnp.int32, (rows, width), 1)
    depth = lane % edge
    z, b = lax.axis_index("bz"), lax.axis_index("bxy")
    at_end = (b == 0, b == lax.axis_size("bxy") - 1, z == 0, z == lax.axis_size("bz") - 1)
    fluid = fluid_ref[slot].astype(jnp.float32)
    below = fluid_ref[jnp.maximum(slot - 1, 0)].astype(jnp.float32)
    above = fluid_ref[jnp.minimum(slot + 1, slots - 1)].astype(jnp.float32)
    bits = jnp.ones((rows, width), jnp.int32)
    for i in range(1, Q):
        cx, cy, cz = VELOCITIES[i]
        source = arrive(i, slot, edge, slots, fluid, below if cz == 1 else None,
                        above if cz == -1 else None, *halo, True)
        bit = jnp.where(source > 0.5, 1 << i, 0)
        if cx:
            edge_row = 0 if cx == 1 else rows - 1
            bit = jnp.where((row == edge_row) & at_end[0 if cx == 1 else 1], 0, bit)
        if cy:
            outer = lane < edge if cy == 1 else lane >= width - edge
            bit = jnp.where(outer & at_end[2 if cy == 1 else 3], 0, bit)
        if cz:
            final = 0 if cz == 1 else slots - 1
            face = 0 if cz == 1 else edge - 1
            bit = jnp.where((depth == face) & (slot == final), 0, bit)
        bits = bits | bit
    mask_ref[slot] = jnp.where(fluid_ref[slot] > 0, bits, 0)


def pack_shell(step, i, edge, value, hz, hx, hy):
    rows, width = value.shape
    for axis, c in enumerate(VELOCITIES[i]):
        if not c:
            continue
        n = TURNS[axis].index(i) + step * len(TURNS[axis])
        if axis == 0:
            row = 0 if c == 1 else rows - 1
            hx[n:n + 1, :] = value[row:row + 1, :]
        elif axis == 1:
            per = 128 // edge
            t, g = n // per, n % per
            tile = value[:, :128] if c == 1 else value[:, width - 128:]
            shift = (g * edge - (0 if c == 1 else 128 - edge)) % 128
            tile = pltpu.roll(tile, shift, 1) if shift else tile
            if g:
                lane = lax.broadcasted_iota(jnp.int32, tile.shape, 1)
                tile = jnp.where(lane >= g * edge, tile, hy[:, t * 128:(t + 1) * 128])
            hy[:, t * 128:(t + 1) * 128] = tile
        else:
            depth = lax.broadcasted_iota(jnp.int32, value.shape, 1) % edge
            shift = (n - (0 if c == 1 else edge - 1)) % width
            turned = pltpu.roll(value, shift, 1) if shift else value
            hz[...] = turned if n == 0 else jnp.where(depth == n, turned, hz[...])


def patch_shell(step, i, edge, value, hz, hx, hy):
    rows, width = value.shape
    for axis, c in enumerate(VELOCITIES[i]):
        if not c:
            continue
        n = TURNS[axis].index(i) + step * len(TURNS[axis])
        if axis == 0:
            row = 0 if c == 1 else rows - 1
            index = lax.broadcasted_iota(jnp.int32, value.shape, 0)
            value = jnp.where(index == row, jnp.broadcast_to(hx[n:n + 1, :], value.shape), value)
        elif axis == 1:
            per = 128 // edge
            t, g = n // per, n % per
            shift = ((0 if c == 1 else 128 - edge) - g * edge) % 128
            tile = hy[:, t * 128:(t + 1) * 128]
            tile = pltpu.roll(tile, shift, 1) if shift else tile
            lane = lax.broadcasted_iota(jnp.int32, tile.shape, 1)
            if c == 1:
                value = jnp.concatenate([jnp.where(lane < edge, tile, value[:, :128]), value[:, 128:]], axis=1)
            else:
                value = jnp.concatenate(
                    [value[:, :-128], jnp.where(lane >= 128 - edge, tile, value[:, -128:])], axis=1)
        else:
            depth = lax.broadcasted_iota(jnp.int32, value.shape, 1) % edge
            face = 0 if c == 1 else edge - 1
            shift = (face - n) % width
            turned = pltpu.roll(hz[...], shift, 1) if shift else hz[...]
            value = jnp.where(depth == face, turned, value)
    return value


def pulled(i, edge, here):
    cx, cy, cz = VELOCITIES[i]
    lanes = (cy * edge + cz) % here.shape[1]
    here = pltpu.roll(here, lanes, 1) if lanes else here
    return pltpu.roll(here, cx % here.shape[0], 0) if cx else here


def redo_block(edge, f, hz, hx, hy, mask_ref, next_ref):
    rows, width = f.shape[1:]
    fluid = jnp.where(f[Q] > 0.0, 1.0, 0.0)
    bits = jnp.ones((rows, width), jnp.int32)
    for i in range(1, Q):
        bits = bits | jnp.where(pulled(i, edge, fluid) > 0.5, 1 << i, 0)
    mask_ref[...] = jnp.where(f[Q] > 0.0, bits, 0)

    def put(i, at, value):
        f[(i,) + at] = value

    def stream(step):
        next_ref[0] = f[0]
        for i in range(1, Q):
            own = f[i]
            mask = mask_ref[...]
            stay = jnp.where(mask > 0, f[OPPOSITE[i]], own)
            value = jnp.where((mask & (1 << i)) != 0, pulled(i, edge, own), stay)
            next_ref[i] = patch_shell(step, i, edge, value, hz, hx, hy)

    def rate(at):
        return f[(Q,) + at]

    collide_tiles(rows, width, lambda i, at: f[(i,) + at], rate, put)
    stream(0)
    collide_tiles(rows, width, lambda i, at: next_ref[(i,) + at], rate, put)
    stream(1)


def choose(picks, values):
    taken = []
    for pick in picks:
        out = values[0]
        for j in range(1, len(values)):
            out = jnp.where(pick == j, values[j], out)
        taken.append(out)
    return taken


def cuts_of(n):
    half = (n + 1) // 2
    cuts = (0, half // 2, half, half + (n - half + 1) // 2, n)
    return [slice(cuts[k], cuts[k + 1]) for k in range(4)]


EARLY = cuts_of(Q + 1)
LATE = cuts_of(Q)
PIECES = 11


def solve_kernel(edge, pdfs, relax_ref, fluid_ref, goal_ref, a_ref, got, table_ref,
                 b_ref, next_ref, mask_ref, ys1, xs1, cs1, yr1, xr1, cr1, ys2, xs2, cs2, yr2, xr2, cr2,
                 hz, hx, hy, early_s, hz_s, hx_s, hy_s, late_s, early_r, hz_r, hx_r, hy_r,
                 early_p, hz_p, hx_p, hy_p, late_p, redo_mask, note_s, note_r, note_m,
                 load_sem, halo_send, halo_recv, note_send, note_recv, note_sem, send_sem, recv_sem):
    slots, rows, width = fluid_ref.shape
    nz, nb = lax.axis_size("bz"), lax.axis_size("bxy")
    z, b = lax.axis_index("bz"), lax.axis_index("bxy")

    loads = [pltpu.make_async_copy(pdfs.at[slice(s.start, min(s.stop, Q))], a_ref.at[slice(s.start, min(s.stop, Q))],
                                   load_sem.at[n]) for n, s in enumerate(EARLY)]
    for load in loads:
        load.start()

    across = math.isqrt(nb // 2)
    row = 2 * across
    bends = across == 2 and nb == 2 * row
    cut = row - 1 if bends else nb
    low, high = cut + 1 - row, cut + row
    no = b < 0
    goes_right, goes_left = (b < nb - 1) & (b != cut), (b > 0) & (b != cut + 1)
    at_cut, past_cut, is_low, is_high = (
        (b == cut, b == cut + 1, b == low, b == high) if bends else (no, no, no, no))

    def there(dz, db):
        exists = None
        for at, step, count in ((z, dz, nz), (b, db, nb)):
            if step:
                inside = at < count - 1 if step == 1 else at > 0
                exists = inside if exists is None else exists & inside
        return exists

    ways = [(1, 0), (-1, 0), (0, 1), (0, -1)] + [(VELOCITIES[i][1], VELOCITIES[i][0]) for i in CORNERS]
    meets = [(there(dz, db), (z + dz, b + db)) for dz, db in ways]
    if bends:
        for who in (at_cut, past_cut):
            meets += [(who, (z, low)), (who, (z, high))]
        for who in (is_low, is_high):
            meets += [(who, (z, cut)), (who, (z, cut + 1))]
    barrier = pltpu.get_barrier_semaphore()
    count = 0
    for who, peer in meets:
        count = count + who.astype(jnp.int32)

        @pl.when(who)
        def _():
            pl.semaphore_signal(barrier, inc=1, device_id=peer, device_id_type=MESH)

    pl.semaphore_wait(barrier, count)

    goal = [goal_ref[0, 0, j] for j in range(slots)]
    base = b * slots

    def flag(t):
        return t.astype(jnp.int32)

    def nth(hits, n):
        before, found = jnp.int32(0), jnp.int32(0)
        for j in range(slots):
            found = found + jnp.where(hits[j] & (before == n), j, 0)
            before = before + flag(hits[j])
        return found

    to_right = [g >= base + slots for g in goal]
    to_left = [g < base for g in goal]
    first_pick = (nth(to_right, 0), nth(to_left, 0))
    second_pick = (nth(to_right, 1), nth(to_left, 1))

    at_row = lax.broadcasted_iota(jnp.int32, note_s.shape, 0)
    note = jnp.zeros(note_s.shape, jnp.int32)
    for j in range(slots):
        note = jnp.where(at_row == j, goal[j], note)
    note_s[...] = note

    def note_copy(n):
        db = 1 if n == 0 else -1
        return remote(note_s, note_r.at[n], note_send.at[n], note_recv.at[n], (z, b + db))

    for n, db in ((0, 1), (1, -1)):
        @pl.when(there(0, db))
        def _():
            note_copy(n).start()

    pieces = [(early_s.at[0, s], early_s.at[1, s], early_r.at[0, s], early_r.at[1, s], early_p.at[s], n < 2)
              for n, s in enumerate(EARLY)]
    for s, r, p, first in ((hz_s, hz_r, hz_p, True), (hx_s, hx_r, hx_p, False), (hy_s, hy_r, hy_p, False)):
        pieces.append((s.at[0], s.at[1], r.at[0], r.at[1], p, first))
    pieces += [(late_s.at[0, s], late_s.at[1, s], got.at[0, 1, s], got.at[1, 1, s], late_p.at[s], n >= 2)
               for n, s in enumerate(LATE)]

    def send_near(p):
        to_r, to_l, from_l, from_r, passing, first = pieces[p]

        @pl.when(goes_right)
        def _():
            remote(to_r, from_l, send_sem.at[0, p], recv_sem.at[0, p], (z, b + 1)).start()

        @pl.when(goes_left)
        def _():
            remote(to_l, from_r, send_sem.at[1, p], recv_sem.at[1, p], (z, b - 1)).start()

    def send_bent(p):
        to_r, to_l, from_l, from_r, passing, first = pieces[p]
        if bends:
            @pl.when(at_cut)
            def _():
                remote(to_r, passing, send_sem.at[0, p], recv_sem.at[2, p], (z, low if first else high)).start()

            @pl.when(past_cut)
            def _():
                remote(to_l, passing, send_sem.at[1, p], recv_sem.at[2, p], (z, high if first else low)).start()

    def forward(p):
        to_r, to_l, from_l, from_r, passing, first = pieces[p]
        if bends:
            for who, ahead in ((is_low, True), (is_high, False)):
                @pl.when(who)
                def _():
                    remote(to_r, passing, send_sem.at[2, p], recv_sem.at[2, p], (z, cut)).wait_recv()
                    if first == ahead:
                        remote(passing, from_l, send_sem.at[2, p], recv_sem.at[0, p], (z, cut + 1)).start()
                    else:
                        remote(passing, from_r, send_sem.at[2, p], recv_sem.at[1, p], (z, cut)).start()

    def arrived(p):
        to_r, to_l, from_l, from_r, passing, first = pieces[p]

        @pl.when(b > 0)
        def _():
            remote(to_r, from_l, send_sem.at[0, p], recv_sem.at[0, p], (z, b - 1)).wait_recv()

        @pl.when(b < nb - 1)
        def _():
            remote(to_l, from_r, send_sem.at[1, p], recv_sem.at[1, p], (z, b + 1)).wait_recv()

    def sent(p):
        to_r, to_l, from_l, from_r, passing, first = pieces[p]

        @pl.when(b < nb - 1)
        def _():
            remote(to_r, from_l, send_sem.at[0, p], recv_sem.at[0, p], (z, b + 1)).wait_send()

        @pl.when(b > 0)
        def _():
            remote(to_l, from_r, send_sem.at[1, p], recv_sem.at[1, p], (z, b - 1)).wait_send()

        if bends:
            @pl.when(is_low | is_high)
            def _():
                remote(passing, from_l, send_sem.at[2, p], recv_sem.at[0, p], (z, cut)).wait_send()

    for n, s in enumerate(EARLY):
        loads[n].wait()

        def gather(i, carry):
            early_s[0, i], early_s[1, i] = choose(first_pick, [a_ref[i, j] for j in range(slots)])
            return carry

        lax.fori_loop(s.start, min(s.stop, Q), gather, 0)
        if s.stop == Q + 1:
            early_s[0, Q], early_s[1, Q] = choose(
                first_pick, [jnp.where(fluid_ref[j] > 0, relax_ref[j], 0.0) for j in range(slots)])
        if n == 0:
            send_near(0)
        if n == 2:
            send_bent(2)

    def rate_of(slot):
        return lambda at: jnp.where(fluid_ref[(slot,) + at] > 0, relax_ref[(slot,) + at], 0.0)

    def first_step(slot, carry):
        def put(i, at, value):
            a_ref[(i, slot) + at] = value

        collide_tiles(rows, width, lambda i, at: a_ref[(i, slot) + at], rate_of(slot), put)
        emit_halo(slot, edge, a_ref, fluid_ref, ys1, xs1)
        return carry

    def routes(step):
        ys, xs, cs, yr, xr, cr = ((ys1, xs1, cs1, yr1, xr1, cr1), (ys2, xs2, cs2, yr2, xr2, cr2))[step]
        ends = [(ys.at[0], yr.at[0]), (ys.at[1], yr.at[1]), (xs.at[0], xr.at[0]), (xs.at[1], xr.at[1])]
        ends += [(cs.at[k], cr.at[k]) for k in range(4)]
        return [(src, dst, dz, db, step * 8 + n) for n, ((src, dst), (dz, db)) in enumerate(zip(ends, ways))]

    def exchange(step):
        for src, dst, dz, db, n in routes(step):
            @pl.when(there(dz, db))
            def _():
                remote(src, dst, halo_send.at[n], halo_recv.at[n], (z + dz, b + db)).start()

    def await_halo(step):
        for src, dst, dz, db, n in routes(step):
            @pl.when(there(-dz, -db))
            def _():
                remote(src, dst, halo_send.at[n], halo_recv.at[n], (z - dz, b - db)).wait_recv()

    ys1[...] = jnp.zeros(ys1.shape, jnp.float32)
    ys2[...] = jnp.zeros(ys2.shape, jnp.float32)
    lax.fori_loop(0, slots, first_step, 0)
    emit_corners(rows, ys1, cs1)
    exchange(0)
    send_near(1)
    send_near(2)
    send_bent(3)
    send_bent(0)
    await_halo(0)
    forward(2)

    def middle_step(slot, carry):
        halo = (yr1, xr1, cr1)
        make_mask(slot, edge, slots, fluid_ref, halo, mask_ref)

        def write(i, value):
            next_ref[i] = value
            pack_shell(0, i, edge, value, hz.at[slot], hx.at[slot], hy.at[slot])

        stream_slot(slot, edge, slots, mask_ref, a_ref, halo, write)

        def put(i, at, value):
            b_ref[(i, slot) + at] = value

        collide_tiles(rows, width, lambda i, at: next_ref[(i,) + at], rate_of(slot), put)
        emit_halo(slot, edge, b_ref, fluid_ref, ys2, xs2)
        return carry

    lax.fori_loop(0, slots, middle_step, 0)
    emit_corners(rows, ys2, cs2)
    exchange(1)
    send_near(3)
    send_bent(1)
    forward(3)
    await_halo(1)

    def last_step(slot, carry):
        def write(i, value):
            a_ref[i, slot] = value
            pack_shell(1, i, edge, value, hz.at[slot], hx.at[slot], hy.at[slot])

        stream_slot(slot, edge, slots, mask_ref, b_ref, (yr2, xr2, cr2), write)
        return carry

    lax.fori_loop(0, slots, last_step, 0)
    for shell, staged in ((hz, hz_s), (hx, hx_s), (hy, hy_s)):
        staged[0], staged[1] = choose(first_pick, [shell[j] for j in range(slots)])
    for p in (5, 6, 4):
        send_near(p)
        send_bent(p)
    for n, s in enumerate(LATE):
        def gather(i, carry):
            late_s[0, i], late_s[1, i] = choose(second_pick, [a_ref[i, j] for j in range(slots)])
            return carry

        lax.fori_loop(s.start, s.stop, gather, 0)
        send_near(7 + n)
        send_bent(7 + n)

    for p in (0, 5, 6, 1, 4, 7, 8):
        forward(p)
    for p in range(7):
        arrived(p)

    def redo(side, carry):
        redo_block(edge, early_r.at[side], hz_r.at[side], hx_r.at[side], hy_r.at[side], redo_mask, got.at[side, 0])
        return carry

    lax.fori_loop(jnp.where(b > 0, 0, 1), jnp.where(b < nb - 1, 2, 1), redo, 0)
    for p in (9, 10):
        forward(p)

    for n, db in ((0, 1), (1, -1)):
        @pl.when(there(0, -db))
        def _():
            remote(note_s, note_r.at[n], note_send.at[n], note_recv.at[n], (z, b - db)).wait_recv()

        @pl.when(there(0, db))
        def _():
            note_copy(n).wait_send()

    fetch = pltpu.make_async_copy(note_r, note_m, note_sem.at[0])
    fetch.start()
    fetch.wait()
    kind = [jnp.int32(0)] * slots
    index = [jnp.int32(k) for k in range(slots)]
    for k in range(slots):
        for j in range(slots):
            index[k] = jnp.where(goal[j] == base + k, j, index[k])
    for source, valid in ((1, b > 0), (2, b < nb - 1)):
        rank = jnp.int32(0)
        for j in range(slots):
            value = note_m[source - 1, j, 0]
            for k in range(slots):
                hit = valid & (value == base + k)
                kind[k] = jnp.where(hit, source, kind[k])
                index[k] = jnp.where(hit, rank, index[k])
            rank = rank + flag(valid & (value >= base) & (value < base + slots))
    for source in range(3):
        held = jnp.int32(0)
        for k in range(slots):
            held = jnp.where(kind[k] == source, index[k], held)
            table_ref[source, k] = held
    for k in range(slots):
        table_ref[3, k] = kind[k]

    for step in range(2):
        for src, dst, dz, db, n in routes(step):
            @pl.when(there(dz, db))
            def _():
                remote(src, dst, halo_send.at[n], halo_recv.at[n], (z + dz, b + db)).wait_send()

    for p in range(7):
        sent(p)
    for p in range(7, PIECES):
        sent(p)
        arrived(p)


def solve(pdfs, relax, fluid, targets):
    q, slots, rows, width = pdfs.shape
    edge = rows
    f32, i32 = jnp.float32, jnp.int32
    hbm = pl.BlockSpec(memory_space=pl.ANY)
    vmem = pl.BlockSpec(memory_space=pltpu.VMEM)
    smem = pl.BlockSpec(memory_space=pltpu.SMEM)
    per = 128 // edge
    turns = 2 * len(TURNS[0])
    x_rows = -(-turns // 8) * 8
    y_lanes = -(-turns // per) * 128
    ys, xs, cs = (2, 6, rows, 128), (2, slots, 8, width), (4, 8, 128)

    def shells(lead):
        return [pltpu.VMEM(lead + s, f32) for s in ((rows, width), (x_rows, width), (rows, y_lanes))]

    halo = [pltpu.VMEM(s, f32) for s in (ys, xs, cs)]
    dma = pltpu.SemaphoreType.DMA
    scratch = [pltpu.VMEM(pdfs.shape, f32), pltpu.VMEM((q, rows, width), f32),
               pltpu.VMEM(fluid.shape, i32)] + halo * 4
    scratch += shells((slots,))
    scratch += [pltpu.VMEM((2, q + 1, rows, width), f32)] + shells((2,)) + [pltpu.VMEM((2, q, rows, width), f32)]
    scratch += [pltpu.VMEM((2, q + 1, rows, width), f32)] + shells((2,))
    scratch += [pltpu.VMEM((q + 1, rows, width), f32)] + shells(()) + [pltpu.VMEM((q, rows, width), f32)]
    scratch += [pltpu.VMEM((rows, width), i32)]
    scratch += [pltpu.VMEM((8, 128), i32), pltpu.VMEM((2, 8, 128), i32), pltpu.SMEM((2, 8, 128), i32)]
    scratch += [dma((4,)), dma((16,)), dma((16,)), dma((2,)), dma((2,)), dma((1,)),
                dma((3, PIECES)), dma((3, PIECES))]
    return pl.pallas_call(
        functools.partial(solve_kernel, edge),
        out_shape=[pltpu.VMEM(pdfs.shape, f32), pltpu.VMEM((2, 2, q, rows, width), f32),
                   jax.ShapeDtypeStruct((4, slots), i32)],
        in_specs=[hbm, vmem, vmem, smem], out_specs=[vmem, vmem, smem], scratch_shapes=scratch,
        compiler_params=pltpu.CompilerParams(collective_id=0, has_side_effects=True, vmem_limit_bytes=40 * 1024 * 1024),
        name="solve",
    )(pdfs, relax, fluid, targets)


def place_kernel(table_ref, own, got, out, sem):
    slots = out.shape[1]
    for k in range(slots):
        for kind in range(3):
            @pl.when(table_ref[3, k] == kind)
            def _():
                at = table_ref[kind, k]
                src = own.at[:, at] if kind == 0 else got.at[kind - 1, at]
                pltpu.make_async_copy(src, out.at[:, k], sem.at[k]).start()

    for k in range(slots):
        pltpu.make_async_copy(own.at[:, k], out.at[:, k], sem.at[k]).wait()


def place(own, got, table):
    hbm = pl.BlockSpec(memory_space=pl.ANY)
    smem = pl.BlockSpec(memory_space=pltpu.SMEM)
    return pl.pallas_call(
        place_kernel, out_shape=jax.ShapeDtypeStruct(own.shape, own.dtype),
        in_specs=[smem, hbm, hbm], out_specs=hbm, scratch_shapes=[pltpu.SemaphoreType.DMA((own.shape[1],))],
        compiler_params=pltpu.CompilerParams(vmem_limit_bytes=1024 * 1024), name="place",
    )(table, own, got)


def on_device(pdfs, relax, fluid, targets):
    own, got, table = solve(pdfs, relax, fluid, targets)
    return place(own, got, table)


def solution(mesh):
    placed = (
        P(None, None, "bxy", "bz"),
        P(None, "bxy", "bz"),
        P(None, "bxy", "bz"),
        P("bz", "bxy", None),
    )
    return jax.shard_map(
        on_device, mesh=mesh, in_specs=placed, out_specs=P(None, None, "bxy", "bz"), check_vma=False
    )
```

```python
import functools
import math

import jax
import jax.numpy as jnp
from jax import lax
from jax.experimental import pallas as pl
from jax.experimental.pallas import tpu as pltpu
from jax.sharding import PartitionSpec as P

MESH = pl.DeviceIdType.MESH
VELOCITIES = (
    (0, 0, 0), (1, 0, 0), (-1, 0, 0), (0, 1, 0), (0, -1, 0), (0, 0, 1), (0, 0, -1),
    (1, 1, 0), (-1, -1, 0), (1, -1, 0), (-1, 1, 0), (1, 0, 1), (-1, 0, -1),
    (1, 0, -1), (-1, 0, 1), (0, 1, 1), (0, -1, -1), (0, 1, -1), (0, -1, 1),
)
OPPOSITE = (0, 2, 1, 4, 3, 6, 5, 8, 7, 10, 9, 12, 11, 14, 13, 16, 15, 18, 17)
Q = 19
TURNS = tuple(tuple(i for i in range(Q) if VELOCITIES[i][axis]) for axis in range(3))
Y_SENT = tuple(tuple(i for i in range(Q) if VELOCITIES[i][1] == c) for c in (1, -1))
X_SENT = tuple(tuple(i for i in range(Q) if VELOCITIES[i][0] == c) for c in (1, -1))
CORNERS = (7, 8, 9, 10)
SIDE = {1: 0, -1: 1}
VMEM_LIMIT = 60 * 1024 * 1024


def collide(f, rate):
    pair = {i: (f[i] + f[i + 1], f[i] - f[i + 1]) for i in range(1, Q, 2)}
    density = f[0]
    for i in range(1, Q, 2):
        density = density + pair[i][0]
    scale = 3.0 / density
    flow = []
    for axis in range(3):
        total = None
        for i in range(1, Q, 2):
            c = VELOCITIES[i][axis]
            if c:
                d = pair[i][1]
                total = d if total is None else (total + d if c == 1 else total - d)
        flow.append(total * scale)
    base = 1.0 - (flow[0] * flow[0] + flow[1] * flow[1] + flow[2] * flow[2]) * (1.0 / 6.0)
    keep = 1.0 - rate
    drive = rate * density
    post = [None] * Q
    post[0] = keep * f[0] + (drive * (1.0 / 3.0)) * base
    near, far = drive * (1.0 / 18.0), drive * (1.0 / 36.0)
    for i in range(1, Q, 2):
        along = None
        for axis in range(3):
            c = VELOCITIES[i][axis]
            if c:
                along = flow[axis] if along is None else (along + flow[axis] if c == 1 else along - flow[axis])
        even = base + 0.5 * (along * along)
        weight = near if i < 7 else far
        post[i] = keep * f[i] + weight * (even + along)
        post[i + 1] = keep * f[i + 1] + weight * (even - along)
    return post


def remote(src, dst, send_sem, recv_sem, device):
    return pltpu.make_async_remote_copy(
        src_ref=src, dst_ref=dst, send_sem=send_sem, recv_sem=recv_sem, device_id=device, device_id_type=MESH)


def lane_shift(velocity, slot, edge, here, below, above, beside):
    _cx, cy, cz = velocity
    width = here.shape[1]
    step = cy * edge + cz
    moved = here if step == 0 else pltpu.roll(here, step % width, 1)
    if cz:
        depth = lax.broadcasted_iota(jnp.int32, here.shape, 1) % edge
        other, face = (below, 0) if cz == 1 else (above, edge - 1)
        carry = step - cz * edge
        wrapped = other if carry == 0 else pltpu.roll(other, carry % width, 1)
        moved = jnp.where(depth == face, wrapped, moved)
    if cy:
        lane = lax.broadcasted_iota(jnp.int32, (here.shape[0], 128), 1)
        offset = 128 if cy == 1 else 256 - edge
        outside = pltpu.roll(beside, lax.rem(offset + cz + 128 - slot * edge, 128), 1)
        if cy == 1:
            moved = jnp.concatenate([jnp.where(lane < edge, outside, moved[:, :128]), moved[:, 128:]], axis=1)
        else:
            moved = jnp.concatenate(
                [moved[:, :-128], jnp.where(lane >= 128 - edge, outside, moved[:, -128:])], axis=1)
    return moved


def arrive(i, slot, edge, slots, here, below, above, yr_ref, xr_ref, cr_ref, fluid):
    velocity = cx, cy, cz = VELOCITIES[i]
    beside = None
    if cy:
        side = SIDE[cy]
        beside = yr_ref[side, 5 if fluid else Y_SENT[side].index(i)]
    moved = lane_shift(velocity, slot, edge, here, below, above, beside)
    if cx:
        side = SIDE[cx]
        row = 5 if fluid else X_SENT[side].index(i)
        rows = moved.shape[0]

        def plane(s):
            return jnp.broadcast_to(xr_ref[side, pl.ds(row * slots + s, 1), :], (8, moved.shape[1]))

        corner = None
        if cy:
            k = CORNERS.index(i)
            n = 1 if fluid else 0
            corner = jnp.broadcast_to(cr_ref[k, n:n + 1, :], (8, 128))
        entering = lane_shift(
            velocity, slot, edge, plane(slot), plane(jnp.maximum(slot - 1, 0)) if cz == 1 else None,
            plane(jnp.minimum(slot + 1, slots - 1)) if cz == -1 else None, corner)
        index = lax.broadcasted_iota(jnp.int32, (8, moved.shape[1]), 0)
        moved = pltpu.roll(moved, cx % rows, 0)
        if cx == 1:
            moved = jnp.concatenate([jnp.where(index == 0, entering, moved[:8]), moved[8:]], axis=0)
        else:
            moved = jnp.concatenate([moved[:-8], jnp.where(index == 7, entering, moved[-8:])], axis=0)
    return moved


def collide_tiles(rows, width, read, rate, write):
    tiles = width // 128

    def body(step, carry):
        r = pl.multiple_of((step // tiles) * 8, 8)
        c = pl.multiple_of((step % tiles) * 128, 128)
        at = (pl.ds(r, 8), pl.ds(c, 128))
        post = collide([read(i, at) for i in range(Q)], rate(at))
        for i in range(Q):
            write(i, at, post[i])
        return carry

    lax.fori_loop(0, (rows // 8) * tiles, body, 0, unroll=4)


def emit_halo(slot, edge, post_ref, fluid_ref, ys_ref, xs_ref):
    slots, rows, width = fluid_ref.shape
    lane = lax.broadcasted_iota(jnp.int32, (rows, 128), 1)
    mine = lane // edge == slot
    for side, first in ((0, width - 128), (1, 0)):
        turn = lax.rem(slot * edge + (edge if side == 0 else 0), 128)
        for n in range(6):
            if n < 5:
                tile = post_ref[Y_SENT[side][n], slot, :, first:first + 128]
            else:
                tile = fluid_ref[slot, :, first:first + 128].astype(jnp.float32)
            ys_ref[side, n] = jnp.where(mine, pltpu.roll(tile, turn, 1), ys_ref[side, n])
    for side, row in ((0, rows - 1), (1, 0)):
        for n in range(5):
            xs_ref[side, pl.ds(n * slots + slot, 1), :] = post_ref[X_SENT[side][n], slot, row:row + 1, :]
        xs_ref[side, pl.ds(5 * slots + slot, 1), :] = fluid_ref[slot, row:row + 1, :].astype(jnp.float32)


def emit_corners(rows, ys_ref, cs_ref):
    for k, i in enumerate(CORNERS):
        cx, cy, _z = VELOCITIES[i]
        row = rows - 1 if cx == 1 else 0
        ys = SIDE[cy]
        cs_ref[k, 0:1, :] = ys_ref[ys, Y_SENT[ys].index(i), row:row + 1, :]
        cs_ref[k, 1:2, :] = ys_ref[ys, 5, row:row + 1, :]
        cs_ref[k, 2:8, :] = jnp.zeros((6, 128), jnp.float32)


def stream_slot(slot, edge, slots, mask_ref, post_ref, halo, write):
    below, above = jnp.maximum(slot - 1, 0), jnp.minimum(slot + 1, slots - 1)
    write(0, post_ref[0, slot])
    for i in range(1, Q):
        cz = VELOCITIES[i][2]
        own = post_ref[i, slot]
        value = arrive(
            i, slot, edge, slots, own, post_ref[i, below] if cz == 1 else None,
            post_ref[i, above] if cz == -1 else None, *halo, False)
        mask = mask_ref[slot]
        stay = jnp.where(mask > 0, post_ref[OPPOSITE[i], slot], own)
        write(i, jnp.where((mask & (1 << i)) != 0, value, stay))


def make_mask(slot, edge, slots, fluid_ref, halo, mask_ref):
    rows, width = fluid_ref.shape[1:]
    row = lax.broadcasted_iota(jnp.int32, (rows, width), 0)
    lane = lax.broadcasted_iota(jnp.int32, (rows, width), 1)
    depth = lane % edge
    z, b = lax.axis_index("bz"), lax.axis_index("bxy")
    at_end = (b == 0, b == lax.axis_size("bxy") - 1, z == 0, z == lax.axis_size("bz") - 1)
    fluid = fluid_ref[slot].astype(jnp.float32)
    below = fluid_ref[jnp.maximum(slot - 1, 0)].astype(jnp.float32)
    above = fluid_ref[jnp.minimum(slot + 1, slots - 1)].astype(jnp.float32)
    bits = jnp.ones((rows, width), jnp.int32)
    for i in range(1, Q):
        cx, cy, cz = VELOCITIES[i]
        source = arrive(i, slot, edge, slots, fluid, below if cz == 1 else None,
                        above if cz == -1 else None, *halo, True)
        bit = jnp.where(source > 0.5, 1 << i, 0)
        if cx:
            edge_row = 0 if cx == 1 else rows - 1
            bit = jnp.where((row == edge_row) & at_end[0 if cx == 1 else 1], 0, bit)
        if cy:
            outer = lane < edge if cy == 1 else lane >= width - edge
            bit = jnp.where(outer & at_end[2 if cy == 1 else 3], 0, bit)
        if cz:
            final = 0 if cz == 1 else slots - 1
            face = 0 if cz == 1 else edge - 1
            bit = jnp.where((depth == face) & (slot == final), 0, bit)
        bits = bits | bit
    mask_ref[slot] = jnp.where(fluid_ref[slot] > 0, bits, 0)


def pack_shell(step, i, edge, value, hz, hx, hy):
    rows, width = value.shape
    for axis, c in enumerate(VELOCITIES[i]):
        if not c:
            continue
        n = TURNS[axis].index(i) + step * len(TURNS[axis])
        if axis == 0:
            row = 0 if c == 1 else rows - 1
            hx[n:n + 1, :] = value[row:row + 1, :]
        elif axis == 1:
            per = 128 // edge
            t, g = n // per, n % per
            tile = value[:, :128] if c == 1 else value[:, width - 128:]
            shift = (g * edge - (0 if c == 1 else 128 - edge)) % 128
            tile = pltpu.roll(tile, shift, 1) if shift else tile
            if g:
                lane = lax.broadcasted_iota(jnp.int32, tile.shape, 1)
                tile = jnp.where(lane >= g * edge, tile, hy[:, t * 128:(t + 1) * 128])
            hy[:, t * 128:(t + 1) * 128] = tile
        else:
            depth = lax.broadcasted_iota(jnp.int32, value.shape, 1) % edge
            shift = (n - (0 if c == 1 else edge - 1)) % width
            turned = pltpu.roll(value, shift, 1) if shift else value
            hz[...] = turned if n == 0 else jnp.where(depth == n, turned, hz[...])


def patch_shell(step, i, edge, value, hz, hx, hy):
    rows, width = value.shape
    for axis, c in enumerate(VELOCITIES[i]):
        if not c:
            continue
        n = TURNS[axis].index(i) + step * len(TURNS[axis])
        if axis == 0:
            row = 0 if c == 1 else rows - 1
            index = lax.broadcasted_iota(jnp.int32, value.shape, 0)
            value = jnp.where(index == row, jnp.broadcast_to(hx[n:n + 1, :], value.shape), value)
        elif axis == 1:
            per = 128 // edge
            t, g = n // per, n % per
            shift = ((0 if c == 1 else 128 - edge) - g * edge) % 128
            tile = hy[:, t * 128:(t + 1) * 128]
            tile = pltpu.roll(tile, shift, 1) if shift else tile
            lane = lax.broadcasted_iota(jnp.int32, tile.shape, 1)
            if c == 1:
                value = jnp.concatenate([jnp.where(lane < edge, tile, value[:, :128]), value[:, 128:]], axis=1)
            else:
                value = jnp.concatenate(
                    [value[:, :-128], jnp.where(lane >= 128 - edge, tile, value[:, -128:])], axis=1)
        else:
            depth = lax.broadcasted_iota(jnp.int32, value.shape, 1) % edge
            face = 0 if c == 1 else edge - 1
            shift = (face - n) % width
            turned = pltpu.roll(hz[...], shift, 1) if shift else hz[...]
            value = jnp.where(depth == face, turned, value)
    return value


def pulled(i, edge, here):
    cx, cy, cz = VELOCITIES[i]
    lanes = (cy * edge + cz) % here.shape[1]
    here = pltpu.roll(here, lanes, 1) if lanes else here
    return pltpu.roll(here, cx % here.shape[0], 0) if cx else here


def redo_block(edge, f, hz, hx, hy, mask_ref, next_ref):
    rows, width = f.shape[1:]
    fluid = jnp.where(f[Q] > 0.0, 1.0, 0.0)
    bits = jnp.ones((rows, width), jnp.int32)
    for i in range(1, Q):
        bits = bits | jnp.where(pulled(i, edge, fluid) > 0.5, 1 << i, 0)
    mask_ref[...] = jnp.where(f[Q] > 0.0, bits, 0)

    def put(i, at, value):
        f[(i,) + at] = value

    def stream(step):
        next_ref[0] = f[0]
        for i in range(1, Q):
            own = f[i]
            mask = mask_ref[...]
            stay = jnp.where(mask > 0, f[OPPOSITE[i]], own)
            value = jnp.where((mask & (1 << i)) != 0, pulled(i, edge, own), stay)
            next_ref[i] = patch_shell(step, i, edge, value, hz, hx, hy)

    def rate(at):
        return f[(Q,) + at]

    collide_tiles(rows, width, lambda i, at: f[(i,) + at], rate, put)
    stream(0)
    collide_tiles(rows, width, lambda i, at: next_ref[(i,) + at], rate, put)
    stream(1)


def choose(picks, values):
    taken = []
    for pick in picks:
        out = values[0]
        for j in range(1, len(values)):
            out = jnp.where(pick == j, values[j], out)
        taken.append(out)
    return taken


def cuts_of(n):
    half = (n + 1) // 2
    cuts = (0, half // 2, half, half + (n - half + 1) // 2, n)
    return [slice(cuts[k], cuts[k + 1]) for k in range(4)]


EARLY = cuts_of(Q + 1)
LATE = cuts_of(Q)
PIECES = 11


def solve_kernel(edge, pdfs, relax, fluid, goal_ref, a_ref, got, table_ref,
                 relax_ref, fluid_ref, b_ref, next_ref, mask_ref, ys1, xs1, cs1, yr1, xr1, cr1, ys2, xs2, cs2, yr2, xr2, cr2,
                 hz, hx, hy, early_s, hz_s, hx_s, hy_s, late_s, early_r, hz_r, hx_r, hy_r,
                 early_p, hz_p, hx_p, hy_p, late_p, redo_mask, note_s, note_r, note_m,
                 load_sem, halo_send, halo_recv, note_send, note_recv, note_sem, send_sem, recv_sem):
    slots, rows, width = fluid_ref.shape
    nz, nb = lax.axis_size("bz"), lax.axis_size("bxy")
    z, b = lax.axis_index("bz"), lax.axis_index("bxy")

    loads = [pltpu.make_async_copy(pdfs.at[slice(s.start, min(s.stop, Q))], a_ref.at[slice(s.start, min(s.stop, Q))],
                                   load_sem.at[n]) for n, s in enumerate(EARLY)]
    side_loads = [pltpu.make_async_copy(relax, relax_ref, load_sem.at[4]),
                  pltpu.make_async_copy(fluid, fluid_ref, load_sem.at[5])]
    for load in loads + side_loads:
        load.start()

    across = math.isqrt(nb // 2)
    row = 2 * across
    bends = across == 2 and nb == 2 * row
    cut = row - 1 if bends else nb
    low, high = cut + 1 - row, cut + row
    no = b < 0
    goes_right, goes_left = (b < nb - 1) & (b != cut), (b > 0) & (b != cut + 1)
    at_cut, past_cut, is_low, is_high = (
        (b == cut, b == cut + 1, b == low, b == high) if bends else (no, no, no, no))

    def there(dz, db):
        exists = None
        for at, step, count in ((z, dz, nz), (b, db, nb)):
            if step:
                inside = at < count - 1 if step == 1 else at > 0
                exists = inside if exists is None else exists & inside
        return exists

    ways = [(1, 0), (-1, 0), (0, 1), (0, -1)] + [(VELOCITIES[i][1], VELOCITIES[i][0]) for i in CORNERS]
    meets = [(there(dz, db), (z + dz, b + db)) for dz, db in ways]
    if bends:
        for who in (at_cut, past_cut):
            meets += [(who, (z, low)), (who, (z, high))]
        for who in (is_low, is_high):
            meets += [(who, (z, cut)), (who, (z, cut + 1))]
    barrier = pltpu.get_barrier_semaphore()
    count = 0
    for who, peer in meets:
        count = count + who.astype(jnp.int32)

        @pl.when(who)
        def _():
            pl.semaphore_signal(barrier, inc=1, device_id=peer, device_id_type=MESH)

    pl.semaphore_wait(barrier, count)

    goal = [goal_ref[0, 0, j] for j in range(slots)]
    base = b * slots

    def flag(t):
        return t.astype(jnp.int32)

    def nth(hits, n):
        before, found = jnp.int32(0), jnp.int32(0)
        for j in range(slots):
            found = found + jnp.where(hits[j] & (before == n), j, 0)
            before = before + flag(hits[j])
        return found

    to_right = [g >= base + slots for g in goal]
    to_left = [g < base for g in goal]
    first_pick = (nth(to_right, 0), nth(to_left, 0))
    second_pick = (nth(to_right, 1), nth(to_left, 1))

    at_row = lax.broadcasted_iota(jnp.int32, note_s.shape, 0)
    note = jnp.zeros(note_s.shape, jnp.int32)
    for j in range(slots):
        note = jnp.where(at_row == j, goal[j], note)
    note_s[...] = note

    def note_copy(n):
        db = 1 if n == 0 else -1
        return remote(note_s, note_r.at[n], note_send.at[n], note_recv.at[n], (z, b + db))

    for n, db in ((0, 1), (1, -1)):
        @pl.when(there(0, db))
        def _():
            note_copy(n).start()

    pieces = [(early_s.at[0, s], early_s.at[1, s], early_r.at[0, s], early_r.at[1, s], early_p.at[s], n < 2)
              for n, s in enumerate(EARLY)]
    for s, r, p, first in ((hz_s, hz_r, hz_p, True), (hx_s, hx_r, hx_p, False), (hy_s, hy_r, hy_p, False)):
        pieces.append((s.at[0], s.at[1], r.at[0], r.at[1], p, first))
    pieces += [(late_s.at[0, s], late_s.at[1, s], got.at[0, 1, s], got.at[1, 1, s], late_p.at[s], n >= 2)
               for n, s in enumerate(LATE)]

    def send_near(p):
        to_r, to_l, from_l, from_r, passing, first = pieces[p]

        @pl.when(goes_right)
        def _():
            remote(to_r, from_l, send_sem.at[0, p], recv_sem.at[0, p], (z, b + 1)).start()

        @pl.when(goes_left)
        def _():
            remote(to_l, from_r, send_sem.at[1, p], recv_sem.at[1, p], (z, b - 1)).start()

    def send_bent(p):
        to_r, to_l, from_l, from_r, passing, first = pieces[p]
        if bends:
            @pl.when(at_cut)
            def _():
                remote(to_r, passing, send_sem.at[0, p], recv_sem.at[2, p], (z, low if first else high)).start()

            @pl.when(past_cut)
            def _():
                remote(to_l, passing, send_sem.at[1, p], recv_sem.at[2, p], (z, high if first else low)).start()

    def forward(p):
        to_r, to_l, from_l, from_r, passing, first = pieces[p]
        if bends:
            for who, ahead in ((is_low, True), (is_high, False)):
                @pl.when(who)
                def _():
                    remote(to_r, passing, send_sem.at[2, p], recv_sem.at[2, p], (z, cut)).wait_recv()
                    if first == ahead:
                        remote(passing, from_l, send_sem.at[2, p], recv_sem.at[0, p], (z, cut + 1)).start()
                    else:
                        remote(passing, from_r, send_sem.at[2, p], recv_sem.at[1, p], (z, cut)).start()

    def arrived(p):
        to_r, to_l, from_l, from_r, passing, first = pieces[p]

        @pl.when(b > 0)
        def _():
            remote(to_r, from_l, send_sem.at[0, p], recv_sem.at[0, p], (z, b - 1)).wait_recv()

        @pl.when(b < nb - 1)
        def _():
            remote(to_l, from_r, send_sem.at[1, p], recv_sem.at[1, p], (z, b + 1)).wait_recv()

    def sent(p):
        to_r, to_l, from_l, from_r, passing, first = pieces[p]

        @pl.when(b < nb - 1)
        def _():
            remote(to_r, from_l, send_sem.at[0, p], recv_sem.at[0, p], (z, b + 1)).wait_send()

        @pl.when(b > 0)
        def _():
            remote(to_l, from_r, send_sem.at[1, p], recv_sem.at[1, p], (z, b - 1)).wait_send()

        if bends:
            @pl.when(is_low | is_high)
            def _():
                remote(passing, from_l, send_sem.at[2, p], recv_sem.at[0, p], (z, cut)).wait_send()

    for n, s in enumerate(EARLY):
        loads[n].wait()

        def gather(i, carry):
            early_s[0, i], early_s[1, i] = choose(first_pick, [a_ref[i, j] for j in range(slots)])
            return carry

        lax.fori_loop(s.start, min(s.stop, Q), gather, 0)
        if s.stop == Q + 1:
            for load in side_loads:
                load.wait()
            early_s[0, Q], early_s[1, Q] = choose(
                first_pick, [jnp.where(fluid_ref[j] > 0, relax_ref[j], 0.0) for j in range(slots)])
        if n == 0:
            send_near(0)
        if n == 2:
            send_bent(2)

    def rate_of(slot):
        return lambda at: jnp.where(fluid_ref[(slot,) + at] > 0, relax_ref[(slot,) + at], 0.0)

    def first_step(slot, carry):
        def put(i, at, value):
            a_ref[(i, slot) + at] = value

        collide_tiles(rows, width, lambda i, at: a_ref[(i, slot) + at], rate_of(slot), put)
        emit_halo(slot, edge, a_ref, fluid_ref, ys1, xs1)
        return carry

    def routes(step):
        ys, xs, cs, yr, xr, cr = ((ys1, xs1, cs1, yr1, xr1, cr1), (ys2, xs2, cs2, yr2, xr2, cr2))[step]
        ends = [(ys.at[0], yr.at[0]), (ys.at[1], yr.at[1]), (xs.at[0], xr.at[0]), (xs.at[1], xr.at[1])]
        ends += [(cs.at[k], cr.at[k]) for k in range(4)]
        return [(src, dst, dz, db, step * 8 + n) for n, ((src, dst), (dz, db)) in enumerate(zip(ends, ways))]

    def exchange(step):
        for src, dst, dz, db, n in routes(step):
            @pl.when(there(dz, db))
            def _():
                remote(src, dst, halo_send.at[n], halo_recv.at[n], (z + dz, b + db)).start()

    def await_halo(step):
        for src, dst, dz, db, n in routes(step):
            @pl.when(there(-dz, -db))
            def _():
                remote(src, dst, halo_send.at[n], halo_recv.at[n], (z - dz, b - db)).wait_recv()

    ys1[...] = jnp.zeros(ys1.shape, jnp.float32)
    ys2[...] = jnp.zeros(ys2.shape, jnp.float32)
    lax.fori_loop(0, slots, first_step, 0)
    emit_corners(rows, ys1, cs1)
    exchange(0)
    send_near(1)
    send_near(2)
    send_bent(3)
    send_bent(0)
    await_halo(0)
    forward(2)

    def middle_step(slot, carry):
        halo = (yr1, xr1, cr1)
        make_mask(slot, edge, slots, fluid_ref, halo, mask_ref)

        def write(i, value):
            next_ref[i] = value
            pack_shell(0, i, edge, value, hz.at[slot], hx.at[slot], hy.at[slot])

        stream_slot(slot, edge, slots, mask_ref, a_ref, halo, write)

        def put(i, at, value):
            b_ref[(i, slot) + at] = value

        collide_tiles(rows, width, lambda i, at: next_ref[(i,) + at], rate_of(slot), put)
        emit_halo(slot, edge, b_ref, fluid_ref, ys2, xs2)
        return carry

    lax.fori_loop(0, slots, middle_step, 0)
    emit_corners(rows, ys2, cs2)
    exchange(1)
    send_near(3)
    send_bent(1)
    forward(3)
    await_halo(1)

    def last_step(slot, carry):
        def write(i, value):
            a_ref[i, slot] = value
            pack_shell(1, i, edge, value, hz.at[slot], hx.at[slot], hy.at[slot])

        stream_slot(slot, edge, slots, mask_ref, b_ref, (yr2, xr2, cr2), write)
        return carry

    lax.fori_loop(0, slots, last_step, 0)
    for shell, staged in ((hz, hz_s), (hx, hx_s), (hy, hy_s)):
        staged[0], staged[1] = choose(first_pick, [shell[j] for j in range(slots)])
    for p in (5, 6, 4):
        send_near(p)
        send_bent(p)
    for n, s in enumerate(LATE):
        def gather(i, carry):
            late_s[0, i], late_s[1, i] = choose(second_pick, [a_ref[i, j] for j in range(slots)])
            return carry

        lax.fori_loop(s.start, s.stop, gather, 0)
        send_near(7 + n)
        send_bent(7 + n)

    for p in (0, 5, 6, 1, 4, 7, 8):
        forward(p)
    for p in range(7):
        arrived(p)

    def redo(side, carry):
        redo_block(edge, early_r.at[side], hz_r.at[side], hx_r.at[side], hy_r.at[side], redo_mask, got.at[side, 0])
        return carry

    lax.fori_loop(jnp.where(b > 0, 0, 1), jnp.where(b < nb - 1, 2, 1), redo, 0)
    for p in (9, 10):
        forward(p)

    for n, db in ((0, 1), (1, -1)):
        @pl.when(there(0, -db))
        def _():
            remote(note_s, note_r.at[n], note_send.at[n], note_recv.at[n], (z, b - db)).wait_recv()

        @pl.when(there(0, db))
        def _():
            note_copy(n).wait_send()

    fetch = pltpu.make_async_copy(note_r, note_m, note_sem.at[0])
    fetch.start()
    fetch.wait()
    kind = [jnp.int32(0)] * slots
    index = [jnp.int32(k) for k in range(slots)]
    for k in range(slots):
        for j in range(slots):
            index[k] = jnp.where(goal[j] == base + k, j, index[k])
    for source, valid in ((1, b > 0), (2, b < nb - 1)):
        rank = jnp.int32(0)
        for j in range(slots):
            value = note_m[source - 1, j, 0]
            for k in range(slots):
                hit = valid & (value == base + k)
                kind[k] = jnp.where(hit, source, kind[k])
                index[k] = jnp.where(hit, rank, index[k])
            rank = rank + flag(valid & (value >= base) & (value < base + slots))
    line = lax.broadcasted_iota(jnp.int32, table_ref.shape, 0)
    entry = lax.broadcasted_iota(jnp.int32, table_ref.shape, 1)
    table = jnp.zeros(table_ref.shape, jnp.int32)
    for k in range(slots):
        table = jnp.where(entry == k, jnp.where(line == 0, kind[k], index[k]), table)
    table_ref[...] = table

    for step in range(2):
        for src, dst, dz, db, n in routes(step):
            @pl.when(there(dz, db))
            def _():
                remote(src, dst, halo_send.at[n], halo_recv.at[n], (z + dz, b + db)).wait_send()

    for p in range(7):
        sent(p)
    for p in range(7, PIECES):
        sent(p)
        arrived(p)


def solve(pdfs, relax, fluid, targets):
    q, slots, rows, width = pdfs.shape
    edge = rows
    f32, i32 = jnp.float32, jnp.int32
    hbm = pl.BlockSpec(memory_space=pl.ANY)
    vmem = pl.BlockSpec(memory_space=pltpu.VMEM)
    smem = pl.BlockSpec(memory_space=pltpu.SMEM)
    per = 128 // edge
    turns = 2 * len(TURNS[0])
    x_rows = -(-turns // 8) * 8
    y_lanes = -(-turns // per) * 128
    ys, xs, cs = (2, 6, rows, 128), (2, -(-6 * slots // 8) * 8, width), (4, 8, 128)

    def shells(lead):
        return [pltpu.VMEM(lead + s, f32) for s in ((rows, width), (x_rows, width), (rows, y_lanes))]

    halo = [pltpu.VMEM(s, f32) for s in (ys, xs, cs)]
    dma = pltpu.SemaphoreType.DMA
    scratch = [pltpu.VMEM(relax.shape, f32), pltpu.VMEM(fluid.shape, i32), pltpu.VMEM(pdfs.shape, f32), pltpu.VMEM((q, rows, width), f32),
               pltpu.VMEM(fluid.shape, i32)] + halo * 4
    scratch += shells((slots,))
    scratch += [pltpu.VMEM((2, q + 1, rows, width), f32)] + shells((2,)) + [pltpu.VMEM((2, q, rows, width), f32)]
    scratch += [pltpu.VMEM((2, q + 1, rows, width), f32)] + shells((2,))
    scratch += [pltpu.VMEM((q + 1, rows, width), f32)] + shells(()) + [pltpu.VMEM((q, rows, width), f32)]
    scratch += [pltpu.VMEM((rows, width), i32)]
    scratch += [pltpu.VMEM((8, 128), i32), pltpu.VMEM((2, 8, 128), i32), pltpu.SMEM((2, 8, 128), i32)]
    scratch += [dma((6,)), dma((16,)), dma((16,)), dma((2,)), dma((2,)), dma((1,)),
                dma((3, PIECES)), dma((3, PIECES))]
    return pl.pallas_call(
        functools.partial(solve_kernel, edge),
        out_shape=[pltpu.VMEM(pdfs.shape, f32), pltpu.VMEM((2, 2, q, rows, width), f32),
                   pltpu.VMEM((8, 128), i32)],
        in_specs=[hbm, hbm, hbm, smem], out_specs=[vmem, vmem, vmem], scratch_shapes=scratch,
        compiler_params=pltpu.CompilerParams(collective_id=0, has_side_effects=True, vmem_limit_bytes=40 * 1024 * 1024),
        name="solve",
    )(pdfs, relax, fluid, targets)


def place_kernel(table_ref, own, got, out, sem):
    slots = out.shape[1]
    for k in range(slots):
        for kind in range(3):
            @pl.when(table_ref[0, k] == kind)
            def _():
                at = table_ref[1, k]
                for n, s in enumerate(LATE):
                    src = own.at[s, at] if kind == 0 else got.at[kind - 1, at, s]
                    pltpu.make_async_copy(src, out.at[s, k], sem.at[k, n]).start()

    for k in range(slots):
        for n, s in enumerate(LATE):
            pltpu.make_async_copy(own.at[s, k], out.at[s, k], sem.at[k, n]).wait()


def place(own, got, table):
    hbm = pl.BlockSpec(memory_space=pl.ANY)
    smem = pl.BlockSpec(memory_space=pltpu.SMEM)
    return pl.pallas_call(
        place_kernel, out_shape=jax.ShapeDtypeStruct(own.shape, own.dtype),
        in_specs=[smem, hbm, hbm], out_specs=hbm, scratch_shapes=[pltpu.SemaphoreType.DMA((own.shape[1], len(LATE)))],
        compiler_params=pltpu.CompilerParams(vmem_limit_bytes=1024 * 1024), name="place",
    )(table, own, got)


def on_device(pdfs, relax, fluid, targets):
    own, got, table = solve(pdfs, relax, fluid, targets)
    return place(own, got, table)


def solution(mesh):
    placed = (
        P(None, None, "bxy", "bz"),
        P(None, "bxy", "bz"),
        P(None, "bxy", "bz"),
        P("bz", "bxy", None),
    )
    return jax.shard_map(
        on_device, mesh=mesh, in_specs=placed, out_specs=P(None, None, "bxy", "bz"), check_vma=False
    )
```

```python
import functools
import math

import jax
import jax.numpy as jnp
from jax import lax
from jax.experimental import pallas as pl
from jax.experimental.pallas import tpu as pltpu
from jax.sharding import PartitionSpec as P

MESH = pl.DeviceIdType.MESH
VELOCITIES = (
    (0, 0, 0), (1, 0, 0), (-1, 0, 0), (0, 1, 0), (0, -1, 0), (0, 0, 1), (0, 0, -1),
    (1, 1, 0), (-1, -1, 0), (1, -1, 0), (-1, 1, 0), (1, 0, 1), (-1, 0, -1),
    (1, 0, -1), (-1, 0, 1), (0, 1, 1), (0, -1, -1), (0, 1, -1), (0, -1, 1),
)
OPPOSITE = (0, 2, 1, 4, 3, 6, 5, 8, 7, 10, 9, 12, 11, 14, 13, 16, 15, 18, 17)
Q = 19
TURNS = tuple(tuple(i for i in range(Q) if VELOCITIES[i][axis]) for axis in range(3))
Y_SENT = tuple(tuple(i for i in range(Q) if VELOCITIES[i][1] == c) for c in (1, -1))
X_SENT = tuple(tuple(i for i in range(Q) if VELOCITIES[i][0] == c) for c in (1, -1))
CORNERS = (7, 8, 9, 10)
SIDE = {1: 0, -1: 1}
VMEM_LIMIT = 60 * 1024 * 1024


def collide(f, rate):
    pair = {i: (f[i] + f[i + 1], f[i] - f[i + 1]) for i in range(1, Q, 2)}
    density = f[0]
    for i in range(1, Q, 2):
        density = density + pair[i][0]
    scale = 3.0 / density
    flow = []
    for axis in range(3):
        total = None
        for i in range(1, Q, 2):
            c = VELOCITIES[i][axis]
            if c:
                d = pair[i][1]
                total = d if total is None else (total + d if c == 1 else total - d)
        flow.append(total * scale)
    base = 1.0 - (flow[0] * flow[0] + flow[1] * flow[1] + flow[2] * flow[2]) * (1.0 / 6.0)
    keep = 1.0 - rate
    drive = rate * density
    post = [None] * Q
    post[0] = keep * f[0] + (drive * (1.0 / 3.0)) * base
    near, far = drive * (1.0 / 18.0), drive * (1.0 / 36.0)
    for i in range(1, Q, 2):
        along = None
        for axis in range(3):
            c = VELOCITIES[i][axis]
            if c:
                along = flow[axis] if along is None else (along + flow[axis] if c == 1 else along - flow[axis])
        even = base + 0.5 * (along * along)
        weight = near if i < 7 else far
        post[i] = keep * f[i] + weight * (even + along)
        post[i + 1] = keep * f[i + 1] + weight * (even - along)
    return post


def remote(src, dst, send_sem, recv_sem, device):
    return pltpu.make_async_remote_copy(
        src_ref=src, dst_ref=dst, send_sem=send_sem, recv_sem=recv_sem, device_id=device, device_id_type=MESH)


def lane_shift(velocity, slot, edge, here, below, above, beside):
    _cx, cy, cz = velocity
    width = here.shape[1]
    step = cy * edge + cz
    moved = here if step == 0 else pltpu.roll(here, step % width, 1)
    if cz:
        depth = lax.broadcasted_iota(jnp.int32, here.shape, 1) % edge
        other, face = (below, 0) if cz == 1 else (above, edge - 1)
        carry = step - cz * edge
        wrapped = other if carry == 0 else pltpu.roll(other, carry % width, 1)
        moved = jnp.where(depth == face, wrapped, moved)
    if cy:
        lane = lax.broadcasted_iota(jnp.int32, (here.shape[0], 128), 1)
        offset = 128 if cy == 1 else 256 - edge
        outside = pltpu.roll(beside, lax.rem(offset + cz + 128 - slot * edge, 128), 1)
        if cy == 1:
            moved = jnp.concatenate([jnp.where(lane < edge, outside, moved[:, :128]), moved[:, 128:]], axis=1)
        else:
            moved = jnp.concatenate(
                [moved[:, :-128], jnp.where(lane >= 128 - edge, outside, moved[:, -128:])], axis=1)
    return moved


def arrive(i, slot, edge, slots, here, below, above, yr_ref, xr_ref, cr_ref, fluid):
    velocity = cx, cy, cz = VELOCITIES[i]
    beside = None
    if cy:
        side = SIDE[cy]
        beside = yr_ref[side, 5 if fluid else Y_SENT[side].index(i)]
    moved = lane_shift(velocity, slot, edge, here, below, above, beside)
    if cx:
        side = SIDE[cx]
        row = 5 if fluid else X_SENT[side].index(i)
        rows = moved.shape[0]

        def plane(s):
            return jnp.broadcast_to(xr_ref[side, pl.ds(row * slots + s, 1), :], (8, moved.shape[1]))

        corner = None
        if cy:
            k = CORNERS.index(i)
            n = 1 if fluid else 0
            corner = jnp.broadcast_to(cr_ref[k, n:n + 1, :], (8, 128))
        entering = lane_shift(
            velocity, slot, edge, plane(slot), plane(jnp.maximum(slot - 1, 0)) if cz == 1 else None,
            plane(jnp.minimum(slot + 1, slots - 1)) if cz == -1 else None, corner)
        index = lax.broadcasted_iota(jnp.int32, (8, moved.shape[1]), 0)
        moved = pltpu.roll(moved, cx % rows, 0)
        if cx == 1:
            moved = jnp.concatenate([jnp.where(index == 0, entering, moved[:8]), moved[8:]], axis=0)
        else:
            moved = jnp.concatenate([moved[:-8], jnp.where(index == 7, entering, moved[-8:])], axis=0)
    return moved


def collide_tiles(rows, width, read, rate, write):
    tiles = width // 128

    def body(step, carry):
        r = pl.multiple_of((step // tiles) * 8, 8)
        c = pl.multiple_of((step % tiles) * 128, 128)
        at = (pl.ds(r, 8), pl.ds(c, 128))
        post = collide([read(i, at) for i in range(Q)], rate(at))
        for i in range(Q):
            write(i, at, post[i])
        return carry

    lax.fori_loop(0, (rows // 8) * tiles, body, 0, unroll=4)


def emit_halo(slot, edge, post_ref, fluid_ref, ys_ref, xs_ref):
    slots, rows, width = fluid_ref.shape
    lane = lax.broadcasted_iota(jnp.int32, (rows, 128), 1)
    mine = lane // edge == slot
    for side, first in ((0, width - 128), (1, 0)):
        turn = lax.rem(slot * edge + (edge if side == 0 else 0), 128)
        for n in range(6):
            if n < 5:
                tile = post_ref[Y_SENT[side][n], slot, :, first:first + 128]
            else:
                tile = fluid_ref[slot, :, first:first + 128].astype(jnp.float32)
            ys_ref[side, n] = jnp.where(mine, pltpu.roll(tile, turn, 1), ys_ref[side, n])
    for side, row in ((0, rows - 1), (1, 0)):
        for n in range(5):
            xs_ref[side, pl.ds(n * slots + slot, 1), :] = post_ref[X_SENT[side][n], slot, row:row + 1, :]
        xs_ref[side, pl.ds(5 * slots + slot, 1), :] = fluid_ref[slot, row:row + 1, :].astype(jnp.float32)


def emit_corners(rows, ys_ref, cs_ref):
    for k, i in enumerate(CORNERS):
        cx, cy, _z = VELOCITIES[i]
        row = rows - 1 if cx == 1 else 0
        ys = SIDE[cy]
        cs_ref[k, 0:1, :] = ys_ref[ys, Y_SENT[ys].index(i), row:row + 1, :]
        cs_ref[k, 1:2, :] = ys_ref[ys, 5, row:row + 1, :]
        cs_ref[k, 2:8, :] = jnp.zeros((6, 128), jnp.float32)


def stream_slot(slot, edge, slots, mask_ref, post_ref, halo, write):
    below, above = jnp.maximum(slot - 1, 0), jnp.minimum(slot + 1, slots - 1)
    write(0, post_ref[0, slot])
    for i in range(1, Q):
        cz = VELOCITIES[i][2]
        own = post_ref[i, slot]
        value = arrive(
            i, slot, edge, slots, own, post_ref[i, below] if cz == 1 else None,
            post_ref[i, above] if cz == -1 else None, *halo, False)
        mask = mask_ref[slot]
        stay = jnp.where(mask > 0, post_ref[OPPOSITE[i], slot], own)
        write(i, jnp.where((mask & (1 << i)) != 0, value, stay))


def make_mask(slot, edge, slots, fluid_ref, halo, mask_ref):
    rows, width = fluid_ref.shape[1:]
    row = lax.broadcasted_iota(jnp.int32, (rows, width), 0)
    lane = lax.broadcasted_iota(jnp.int32, (rows, width), 1)
    depth = lane % edge
    z, b = lax.axis_index("bz"), lax.axis_index("bxy")
    at_end = (b == 0, b == lax.axis_size("bxy") - 1, z == 0, z == lax.axis_size("bz") - 1)
    fluid = fluid_ref[slot].astype(jnp.float32)
    below = fluid_ref[jnp.maximum(slot - 1, 0)].astype(jnp.float32)
    above = fluid_ref[jnp.minimum(slot + 1, slots - 1)].astype(jnp.float32)
    bits = jnp.ones((rows, width), jnp.int32)
    for i in range(1, Q):
        cx, cy, cz = VELOCITIES[i]
        source = arrive(i, slot, edge, slots, fluid, below if cz == 1 else None,
                        above if cz == -1 else None, *halo, True)
        bit = jnp.where(source > 0.5, 1 << i, 0)
        if cx:
            edge_row = 0 if cx == 1 else rows - 1
            bit = jnp.where((row == edge_row) & at_end[0 if cx == 1 else 1], 0, bit)
        if cy:
            outer = lane < edge if cy == 1 else lane >= width - edge
            bit = jnp.where(outer & at_end[2 if cy == 1 else 3], 0, bit)
        if cz:
            final = 0 if cz == 1 else slots - 1
            face = 0 if cz == 1 else edge - 1
            bit = jnp.where((depth == face) & (slot == final), 0, bit)
        bits = bits | bit
    mask_ref[slot] = jnp.where(fluid_ref[slot] > 0, bits, 0)


def pack_shell(step, i, edge, values, hz, hx, hy):
    value = values[i]
    rows, width = value.shape
    for axis, c in enumerate(VELOCITIES[i]):
        if not c:
            continue
        n = TURNS[axis].index(i) + step * len(TURNS[axis])
        if axis == 0:
            row = 0 if c == 1 else rows - 1
            hx[n:n + 1, :] = value[row:row + 1, :]
        elif axis == 1:
            per = 128 // edge
            t, g = n // per, n % per
            tile = value[:, :128] if c == 1 else value[:, width - 128:]
            shift = (g * edge - (0 if c == 1 else 128 - edge)) % 128
            tile = pltpu.roll(tile, shift, 1) if shift else tile
            if g:
                lane = lax.broadcasted_iota(jnp.int32, tile.shape, 1)
                tile = jnp.where(lane >= g * edge, tile, hy[:, t * 128:(t + 1) * 128])
            hy[:, t * 128:(t + 1) * 128] = tile
        elif n % 2:
            depth = lax.broadcasted_iota(jnp.int32, value.shape, 1) % edge
            pair = (values[i - 1], value) if c == -1 else (value, values[i - 1])
            both = jnp.where(depth == 0, pair[0], pair[1])
            if n > 1:
                both = jnp.where(depth // 2 == n // 2, pltpu.roll(both, n, 1), hz[...])
            hz[...] = both


def patch_shell(step, i, edge, value, hz, hx, hy):
    rows, width = value.shape
    for axis, c in enumerate(VELOCITIES[i]):
        if not c:
            continue
        n = TURNS[axis].index(i) + step * len(TURNS[axis])
        if axis == 0:
            row = 0 if c == 1 else rows - 1
            index = lax.broadcasted_iota(jnp.int32, value.shape, 0)
            value = jnp.where(index == row, jnp.broadcast_to(hx[n:n + 1, :], value.shape), value)
        elif axis == 1:
            per = 128 // edge
            t, g = n // per, n % per
            shift = ((0 if c == 1 else 128 - edge) - g * edge) % 128
            tile = hy[:, t * 128:(t + 1) * 128]
            tile = pltpu.roll(tile, shift, 1) if shift else tile
            lane = lax.broadcasted_iota(jnp.int32, tile.shape, 1)
            if c == 1:
                value = jnp.concatenate([jnp.where(lane < edge, tile, value[:, :128]), value[:, 128:]], axis=1)
            else:
                value = jnp.concatenate(
                    [value[:, :-128], jnp.where(lane >= 128 - edge, tile, value[:, -128:])], axis=1)
        else:
            depth = lax.broadcasted_iota(jnp.int32, value.shape, 1) % edge
            face = 0 if c == 1 else edge - 1
            turned = pltpu.roll(hz[...], width - (n | 1), 1) if n > 1 else hz[...]
            value = jnp.where(depth == face, turned, value)
    return value


def pulled(i, edge, here):
    cx, cy, cz = VELOCITIES[i]
    lanes = (cy * edge + cz) % here.shape[1]
    here = pltpu.roll(here, lanes, 1) if lanes else here
    return pltpu.roll(here, cx % here.shape[0], 0) if cx else here


def redo_block(edge, f, hz, hx, hy, mask_ref, next_ref):
    rows, width = f.shape[1:]
    fluid = jnp.where(f[Q] > 0.0, 1.0, 0.0)
    bits = jnp.ones((rows, width), jnp.int32)
    for i in range(1, Q):
        bits = bits | jnp.where(pulled(i, edge, fluid) > 0.5, 1 << i, 0)
    mask_ref[...] = jnp.where(f[Q] > 0.0, bits, 0)

    def put(i, at, value):
        f[(i,) + at] = value

    def stream(step):
        next_ref[0] = f[0]
        for i in range(1, Q):
            own = f[i]
            mask = mask_ref[...]
            stay = jnp.where(mask > 0, f[OPPOSITE[i]], own)
            value = jnp.where((mask & (1 << i)) != 0, pulled(i, edge, own), stay)
            next_ref[i] = patch_shell(step, i, edge, value, hz, hx, hy)

    def rate(at):
        return f[(Q,) + at]

    collide_tiles(rows, width, lambda i, at: f[(i,) + at], rate, put)
    stream(0)
    collide_tiles(rows, width, lambda i, at: next_ref[(i,) + at], rate, put)
    stream(1)


def choose(picks, values):
    taken = []
    for pick in picks:
        out = values[0]
        for j in range(1, len(values)):
            out = jnp.where(pick == j, values[j], out)
        taken.append(out)
    return taken


def cuts_of(n):
    half = (n + 1) // 2
    cuts = (0, half // 2, half, half + (n - half + 1) // 2, n)
    return [slice(cuts[k], cuts[k + 1]) for k in range(4)]


EARLY = cuts_of(Q + 1)
LATE = cuts_of(Q)
PIECES = 11


def solve_kernel(edge, pdfs, relax, fluid, goal_ref, a_ref, got, table_ref,
                 relax_ref, fluid_ref, b_ref, next_ref, mask_ref, ys1, xs1, cs1, yr1, xr1, cr1, ys2, xs2, cs2, yr2, xr2, cr2,
                 hz, hx, hy, early_s, hz_s, hx_s, hy_s, late_s, early_r, hz_r, hx_r, hy_r,
                 early_p, hz_p, hx_p, hy_p, late_p, redo_mask, note_s, note_r, note_m,
                 load_sem, row_sem, halo_send, halo_recv, note_send, note_recv, note_sem, send_sem, recv_sem):
    slots, rows, width = fluid_ref.shape
    nz, nb = lax.axis_size("bz"), lax.axis_size("bxy")
    z, b = lax.axis_index("bz"), lax.axis_index("bxy")

    loads = [pltpu.make_async_copy(pdfs.at[slice(s.start, min(s.stop, Q))], a_ref.at[slice(s.start, min(s.stop, Q))],
                                   load_sem.at[n]) for n, s in enumerate(EARLY)]
    side_loads = [pltpu.make_async_copy(relax, relax_ref, load_sem.at[4]),
                  pltpu.make_async_copy(fluid, fluid_ref, load_sem.at[5])]
    for load in loads + side_loads:
        load.start()

    across = math.isqrt(nb // 2)
    row = 2 * across
    bends = across == 2 and nb == 2 * row
    cut = row - 1 if bends else nb
    low, high = cut + 1 - row, cut + row
    no = b < 0
    goes_right, goes_left = (b < nb - 1) & (b != cut), (b > 0) & (b != cut + 1)
    at_cut, past_cut, is_low, is_high = (
        (b == cut, b == cut + 1, b == low, b == high) if bends else (no, no, no, no))

    def there(dz, db):
        exists = None
        for at, step, count in ((z, dz, nz), (b, db, nb)):
            if step:
                inside = at < count - 1 if step == 1 else at > 0
                exists = inside if exists is None else exists & inside
        return exists

    ways = [(1, 0), (-1, 0), (0, 1), (0, -1)] + [(VELOCITIES[i][1], VELOCITIES[i][0]) for i in CORNERS]
    meets = [(there(dz, db), (z + dz, b + db)) for dz, db in ways[:4]]
    if bends:
        for who in (at_cut, past_cut):
            meets += [(who, (z, low)), (who, (z, high))]
        for who in (is_low, is_high):
            meets += [(who, (z, cut)), (who, (z, cut + 1))]
    barrier = pltpu.get_barrier_semaphore()
    count = 0
    for who, peer in meets:
        count = count + who.astype(jnp.int32)

        @pl.when(who)
        def _():
            pl.semaphore_signal(barrier, inc=1, device_id=peer, device_id_type=MESH)

    pl.semaphore_wait(barrier, count)
    rows_met = 0
    for dz, db in ways[:2]:
        rows_met = rows_met + there(dz, db).astype(jnp.int32)

        @pl.when(there(dz, db))
        def _():
            pl.semaphore_signal(row_sem, inc=1, device_id=(z + dz, b + db), device_id_type=MESH)

    goal = [goal_ref[0, 0, j] for j in range(slots)]
    base = b * slots

    def flag(t):
        return t.astype(jnp.int32)

    def nth(hits, n):
        before, found = jnp.int32(0), jnp.int32(0)
        for j in range(slots):
            found = found + jnp.where(hits[j] & (before == n), j, 0)
            before = before + flag(hits[j])
        return found

    to_right = [g >= base + slots for g in goal]
    to_left = [g < base for g in goal]
    first_pick = (nth(to_right, 0), nth(to_left, 0))
    second_pick = (nth(to_right, 1), nth(to_left, 1))

    at_row = lax.broadcasted_iota(jnp.int32, note_s.shape, 0)
    note = jnp.zeros(note_s.shape, jnp.int32)
    for j in range(slots):
        note = jnp.where(at_row == j, goal[j], note)
    note_s[...] = note

    def note_copy(n):
        db = 1 if n == 0 else -1
        return remote(note_s, note_r.at[n], note_send.at[n], note_recv.at[n], (z, b + db))

    for n, db in ((0, 1), (1, -1)):
        @pl.when(there(0, db))
        def _():
            note_copy(n).start()

    pieces = [(early_s.at[0, s], early_s.at[1, s], early_r.at[0, s], early_r.at[1, s], early_p.at[s], n < 2)
              for n, s in enumerate(EARLY)]
    for s, r, p, first in ((hz_s, hz_r, hz_p, True), (hx_s, hx_r, hx_p, False), (hy_s, hy_r, hy_p, False)):
        pieces.append((s.at[0], s.at[1], r.at[0], r.at[1], p, first))
    pieces += [(late_s.at[0, s], late_s.at[1, s], got.at[0, 1, s], got.at[1, 1, s], late_p.at[s], n % 2 == 1)
               for n, s in enumerate(LATE)]

    def send_near(p):
        to_r, to_l, from_l, from_r, passing, first = pieces[p]

        @pl.when(goes_right)
        def _():
            remote(to_r, from_l, send_sem.at[0, p], recv_sem.at[0, p], (z, b + 1)).start()

        @pl.when(goes_left)
        def _():
            remote(to_l, from_r, send_sem.at[1, p], recv_sem.at[1, p], (z, b - 1)).start()

    def send_bent(p):
        to_r, to_l, from_l, from_r, passing, first = pieces[p]
        if bends:
            @pl.when(at_cut)
            def _():
                remote(to_r, passing, send_sem.at[0, p], recv_sem.at[2, p], (z, low if first else high)).start()

            @pl.when(past_cut)
            def _():
                remote(to_l, passing, send_sem.at[1, p], recv_sem.at[2, p], (z, high if first else low)).start()

    def forward(p):
        to_r, to_l, from_l, from_r, passing, first = pieces[p]
        if bends:
            for who, ahead in ((is_low, True), (is_high, False)):
                @pl.when(who)
                def _():
                    remote(to_r, passing, send_sem.at[2, p], recv_sem.at[2, p], (z, cut)).wait_recv()
                    if first == ahead:
                        remote(passing, from_l, send_sem.at[2, p], recv_sem.at[0, p], (z, cut + 1)).start()
                    else:
                        remote(passing, from_r, send_sem.at[2, p], recv_sem.at[1, p], (z, cut)).start()

    def arrived(p):
        to_r, to_l, from_l, from_r, passing, first = pieces[p]

        @pl.when(b > 0)
        def _():
            remote(to_r, from_l, send_sem.at[0, p], recv_sem.at[0, p], (z, b - 1)).wait_recv()

        @pl.when(b < nb - 1)
        def _():
            remote(to_l, from_r, send_sem.at[1, p], recv_sem.at[1, p], (z, b + 1)).wait_recv()

    def sent(p):
        to_r, to_l, from_l, from_r, passing, first = pieces[p]

        @pl.when(b < nb - 1)
        def _():
            remote(to_r, from_l, send_sem.at[0, p], recv_sem.at[0, p], (z, b + 1)).wait_send()

        @pl.when(b > 0)
        def _():
            remote(to_l, from_r, send_sem.at[1, p], recv_sem.at[1, p], (z, b - 1)).wait_send()

        if bends:
            @pl.when(is_low | is_high)
            def _():
                remote(passing, from_l, send_sem.at[2, p], recv_sem.at[0, p], (z, cut)).wait_send()

    for n, s in enumerate(EARLY):
        loads[n].wait()

        def gather(i, carry):
            early_s[0, i], early_s[1, i] = choose(first_pick, [a_ref[i, j] for j in range(slots)])
            return carry

        lax.fori_loop(s.start, min(s.stop, Q), gather, 0)
        if s.stop == Q + 1:
            for load in side_loads:
                load.wait()
            early_s[0, Q], early_s[1, Q] = choose(
                first_pick, [jnp.where(fluid_ref[j] > 0, relax_ref[j], 0.0) for j in range(slots)])
        if n == 0:
            send_near(0)
        if n == 2:
            send_bent(2)

    def rate_of(slot):
        return lambda at: jnp.where(fluid_ref[(slot,) + at] > 0, relax_ref[(slot,) + at], 0.0)

    def first_step(slot, carry):
        def put(i, at, value):
            a_ref[(i, slot) + at] = value

        collide_tiles(rows, width, lambda i, at: a_ref[(i, slot) + at], rate_of(slot), put)
        emit_halo(slot, edge, a_ref, fluid_ref, ys1, xs1)
        return carry

    def routes(step):
        ys, xs, cs, yr, xr, cr = ((ys1, xs1, cs1, yr1, xr1, cr1), (ys2, xs2, cs2, yr2, xr2, cr2))[step]
        ends = [(ys.at[0], yr.at[0]), (ys.at[1], yr.at[1]), (xs.at[0], xr.at[0]), (xs.at[1], xr.at[1])]
        ends += [(cs.at[k], cr.at[k]) for k in range(4)]
        return [(src, dst, dz, db, step * 8 + n) for n, ((src, dst), (dz, db)) in enumerate(zip(ends, ways))]

    def exchange(step):
        for src, dst, dz, db, n in routes(step):
            @pl.when(there(dz, db))
            def _():
                remote(src, dst, halo_send.at[n], halo_recv.at[n], (z + dz, b + db)).start()

    def await_halo(step):
        for src, dst, dz, db, n in routes(step):
            @pl.when(there(-dz, -db))
            def _():
                remote(src, dst, halo_send.at[n], halo_recv.at[n], (z - dz, b - db)).wait_recv()

    ys1[...] = jnp.zeros(ys1.shape, jnp.float32)
    ys2[...] = jnp.zeros(ys2.shape, jnp.float32)
    lax.fori_loop(0, slots, first_step, 0)
    emit_corners(rows, ys1, cs1)
    pl.semaphore_wait(row_sem, rows_met)
    exchange(0)
    send_near(1)
    send_near(2)
    send_bent(3)
    send_bent(0)
    await_halo(0)
    forward(2)

    def middle_step(slot, carry):
        halo = (yr1, xr1, cr1)
        make_mask(slot, edge, slots, fluid_ref, halo, mask_ref)

        values = {}

        def write(i, value):
            next_ref[i] = values[i] = value
            pack_shell(0, i, edge, values, hz.at[slot], hx.at[slot], hy.at[slot])

        stream_slot(slot, edge, slots, mask_ref, a_ref, halo, write)

        def put(i, at, value):
            b_ref[(i, slot) + at] = value

        collide_tiles(rows, width, lambda i, at: next_ref[(i,) + at], rate_of(slot), put)
        emit_halo(slot, edge, b_ref, fluid_ref, ys2, xs2)
        return carry

    lax.fori_loop(0, slots, middle_step, 0)
    emit_corners(rows, ys2, cs2)
    exchange(1)
    send_near(3)
    send_bent(1)
    forward(3)
    await_halo(1)

    def last_step(slot, carry):
        values = {}

        def write(i, value):
            a_ref[i, slot] = values[i] = value
            pack_shell(1, i, edge, values, hz.at[slot], hx.at[slot], hy.at[slot])

        stream_slot(slot, edge, slots, mask_ref, b_ref, (yr2, xr2, cr2), write)
        return carry

    lax.fori_loop(0, slots, last_step, 0)
    for shell, staged in ((hz, hz_s), (hx, hx_s), (hy, hy_s)):
        staged[0], staged[1] = choose(first_pick, [shell[j] for j in range(slots)])
    for p in (5, 6, 4):
        send_near(p)
        send_bent(p)
    for n, s in enumerate(LATE):
        def gather(i, carry):
            late_s[0, i], late_s[1, i] = choose(second_pick, [a_ref[i, j] for j in range(slots)])
            return carry

        lax.fori_loop(s.start, s.stop, gather, 0)
        send_near(7 + n)
        send_bent(7 + n)

    for p in (0, 5, 6, 1, 4, 7, 9):
        forward(p)
    for p in range(7):
        arrived(p)

    def redo(side, carry):
        redo_block(edge, early_r.at[side], hz_r.at[side], hx_r.at[side], hy_r.at[side], redo_mask, got.at[side, 0])
        return carry

    lax.fori_loop(jnp.where(b > 0, 0, 1), jnp.where(b < nb - 1, 2, 1), redo, 0)
    for p in (8, 10):
        forward(p)

    for n, db in ((0, 1), (1, -1)):
        @pl.when(there(0, -db))
        def _():
            remote(note_s, note_r.at[n], note_send.at[n], note_recv.at[n], (z, b - db)).wait_recv()

        @pl.when(there(0, db))
        def _():
            note_copy(n).wait_send()

    fetch = pltpu.make_async_copy(note_r, note_m, note_sem.at[0])
    fetch.start()
    fetch.wait()
    kind = [jnp.int32(0)] * slots
    index = [jnp.int32(k) for k in range(slots)]
    for k in range(slots):
        for j in range(slots):
            index[k] = jnp.where(goal[j] == base + k, j, index[k])
    for source, valid in ((1, b > 0), (2, b < nb - 1)):
        rank = jnp.int32(0)
        for j in range(slots):
            value = note_m[source - 1, j, 0]
            for k in range(slots):
                hit = valid & (value == base + k)
                kind[k] = jnp.where(hit, source, kind[k])
                index[k] = jnp.where(hit, rank, index[k])
            rank = rank + flag(valid & (value >= base) & (value < base + slots))
    line = lax.broadcasted_iota(jnp.int32, table_ref.shape, 0)
    entry = lax.broadcasted_iota(jnp.int32, table_ref.shape, 1)
    table = jnp.zeros(table_ref.shape, jnp.int32)
    for k in range(slots):
        table = jnp.where(entry == k, jnp.where(line == 0, kind[k], index[k]), table)
    table_ref[...] = table

    for step in range(2):
        for src, dst, dz, db, n in routes(step):
            @pl.when(there(dz, db))
            def _():
                remote(src, dst, halo_send.at[n], halo_recv.at[n], (z + dz, b + db)).wait_send()

    for p in range(7):
        sent(p)
    for p in range(7, PIECES):
        sent(p)
        arrived(p)


def solve(pdfs, relax, fluid, targets):
    q, slots, rows, width = pdfs.shape
    edge = rows
    f32, i32 = jnp.float32, jnp.int32
    hbm = pl.BlockSpec(memory_space=pl.ANY)
    vmem = pl.BlockSpec(memory_space=pltpu.VMEM)
    smem = pl.BlockSpec(memory_space=pltpu.SMEM)
    per = 128 // edge
    turns = 2 * len(TURNS[0])
    x_rows = -(-turns // 8) * 8
    y_lanes = -(-turns // per) * 128
    ys, xs, cs = (2, 6, rows, 128), (2, -(-6 * slots // 8) * 8, width), (4, 8, 128)

    def shells(lead):
        return [pltpu.VMEM(lead + s, f32) for s in ((rows, width), (x_rows, width), (rows, y_lanes))]

    halo = [pltpu.VMEM(s, f32) for s in (ys, xs, cs)]
    dma = pltpu.SemaphoreType.DMA
    scratch = [pltpu.VMEM(relax.shape, f32), pltpu.VMEM(fluid.shape, i32), pltpu.VMEM(pdfs.shape, f32), pltpu.VMEM((q, rows, width), f32),
               pltpu.VMEM(fluid.shape, i32)] + halo * 4
    scratch += shells((slots,))
    scratch += [pltpu.VMEM((2, q + 1, rows, width), f32)] + shells((2,)) + [pltpu.VMEM((2, q, rows, width), f32)]
    scratch += [pltpu.VMEM((2, q + 1, rows, width), f32)] + shells((2,))
    scratch += [pltpu.VMEM((q + 1, rows, width), f32)] + shells(()) + [pltpu.VMEM((q, rows, width), f32)]
    scratch += [pltpu.VMEM((rows, width), i32)]
    scratch += [pltpu.VMEM((8, 128), i32), pltpu.VMEM((2, 8, 128), i32), pltpu.SMEM((2, 8, 128), i32)]
    scratch += [dma((6,)), pltpu.SemaphoreType.REGULAR, dma((16,)), dma((16,)), dma((2,)), dma((2,)), dma((1,)),
                dma((3, PIECES)), dma((3, PIECES))]
    return pl.pallas_call(
        functools.partial(solve_kernel, edge),
        out_shape=[pltpu.VMEM(pdfs.shape, f32), pltpu.VMEM((2, 2, q, rows, width), f32),
                   pltpu.VMEM((8, 128), i32)],
        in_specs=[hbm, hbm, hbm, smem], out_specs=[vmem, vmem, vmem], scratch_shapes=scratch,
        compiler_params=pltpu.CompilerParams(collective_id=0, has_side_effects=True, vmem_limit_bytes=40 * 1024 * 1024),
        name="solve",
    )(pdfs, relax, fluid, targets)


def place_kernel(table_ref, own, got, out, sem):
    slots = out.shape[1]
    for k in range(slots):
        for kind in range(3):
            @pl.when(table_ref[0, k] == kind)
            def _():
                at = table_ref[1, k]
                for n, s in enumerate(LATE):
                    src = own.at[s, at] if kind == 0 else got.at[kind - 1, at, s]
                    pltpu.make_async_copy(src, out.at[s, k], sem.at[k, n]).start()

    for k in range(slots):
        for n, s in enumerate(LATE):
            pltpu.make_async_copy(own.at[s, k], out.at[s, k], sem.at[k, n]).wait()


def place(own, got, table):
    hbm = pl.BlockSpec(memory_space=pl.ANY)
    smem = pl.BlockSpec(memory_space=pltpu.SMEM)
    return pl.pallas_call(
        place_kernel, out_shape=jax.ShapeDtypeStruct(own.shape, own.dtype),
        in_specs=[smem, hbm, hbm], out_specs=hbm, scratch_shapes=[pltpu.SemaphoreType.DMA((own.shape[1], len(LATE)))],
        compiler_params=pltpu.CompilerParams(vmem_limit_bytes=1024 * 1024), name="place",
    )(table, own, got)


def on_device(pdfs, relax, fluid, targets):
    own, got, table = solve(pdfs, relax, fluid, targets)
    return place(own, got, table)


def solution(mesh):
    placed = (
        P(None, None, "bxy", "bz"),
        P(None, "bxy", "bz"),
        P(None, "bxy", "bz"),
        P("bz", "bxy", None),
    )
    return jax.shard_map(
        on_device, mesh=mesh, in_specs=placed, out_specs=P(None, None, "bxy", "bz"), check_vma=False
    )
```

```python
import functools
import math

import jax
import jax.numpy as jnp
from jax import lax
from jax.experimental import pallas as pl
from jax.experimental.pallas import tpu as pltpu
from jax.sharding import PartitionSpec as P

MESH = pl.DeviceIdType.MESH
VELOCITIES = (
    (0, 0, 0), (1, 0, 0), (-1, 0, 0), (0, 1, 0), (0, -1, 0), (0, 0, 1), (0, 0, -1),
    (1, 1, 0), (-1, -1, 0), (1, -1, 0), (-1, 1, 0), (1, 0, 1), (-1, 0, -1),
    (1, 0, -1), (-1, 0, 1), (0, 1, 1), (0, -1, -1), (0, 1, -1), (0, -1, 1),
)
OPPOSITE = (0, 2, 1, 4, 3, 6, 5, 8, 7, 10, 9, 12, 11, 14, 13, 16, 15, 18, 17)
Q = 19
TURNS = tuple(tuple(i for i in range(Q) if VELOCITIES[i][axis]) for axis in range(3))
Y_SENT = tuple(tuple(i for i in range(Q) if VELOCITIES[i][1] == c) for c in (1, -1))
X_SENT = tuple(tuple(i for i in range(Q) if VELOCITIES[i][0] == c) for c in (1, -1))
CORNERS = (7, 8, 9, 10)
SIDE = {1: 0, -1: 1}
VMEM_LIMIT = 60 * 1024 * 1024


def collide(f, rate):
    pair = {i: (f[i] + f[i + 1], f[i] - f[i + 1]) for i in range(1, Q, 2)}
    density = f[0]
    for i in range(1, Q, 2):
        density = density + pair[i][0]
    scale = 3.0 / density
    flow = []
    for axis in range(3):
        total = None
        for i in range(1, Q, 2):
            c = VELOCITIES[i][axis]
            if c:
                d = pair[i][1]
                total = d if total is None else (total + d if c == 1 else total - d)
        flow.append(total * scale)
    base = 1.0 - (flow[0] * flow[0] + flow[1] * flow[1] + flow[2] * flow[2]) * (1.0 / 6.0)
    keep = 1.0 - rate
    drive = rate * density
    post = [None] * Q
    post[0] = keep * f[0] + (drive * (1.0 / 3.0)) * base
    near, far = drive * (1.0 / 18.0), drive * (1.0 / 36.0)
    for i in range(1, Q, 2):
        along = None
        for axis in range(3):
            c = VELOCITIES[i][axis]
            if c:
                along = flow[axis] if along is None else (along + flow[axis] if c == 1 else along - flow[axis])
        even = base + 0.5 * (along * along)
        weight = near if i < 7 else far
        post[i] = keep * f[i] + weight * (even + along)
        post[i + 1] = keep * f[i + 1] + weight * (even - along)
    return post


def remote(src, dst, send_sem, recv_sem, device):
    return pltpu.make_async_remote_copy(
        src_ref=src, dst_ref=dst, send_sem=send_sem, recv_sem=recv_sem, device_id=device, device_id_type=MESH)


def lane_shift(velocity, slot, edge, here, below, above, beside):
    _cx, cy, cz = velocity
    width = here.shape[1]
    step = cy * edge + cz
    moved = here if step == 0 else pltpu.roll(here, step % width, 1)
    if cz:
        depth = lax.broadcasted_iota(jnp.int32, here.shape, 1) % edge
        other, face = (below, 0) if cz == 1 else (above, edge - 1)
        carry = step - cz * edge
        wrapped = other if carry == 0 else pltpu.roll(other, carry % width, 1)
        moved = jnp.where(depth == face, wrapped, moved)
    if cy:
        lane = lax.broadcasted_iota(jnp.int32, (here.shape[0], 128), 1)
        offset = 128 if cy == 1 else 256 - edge
        outside = pltpu.roll(beside, lax.rem(offset + cz + 128 - slot * edge, 128), 1)
        if cy == 1:
            moved = jnp.concatenate([jnp.where(lane < edge, outside, moved[:, :128]), moved[:, 128:]], axis=1)
        else:
            moved = jnp.concatenate(
                [moved[:, :-128], jnp.where(lane >= 128 - edge, outside, moved[:, -128:])], axis=1)
    return moved


def arrive(i, slot, edge, slots, here, below, above, yr_ref, xr_ref, cr_ref, fluid):
    velocity = cx, cy, cz = VELOCITIES[i]
    beside = None
    if cy:
        side = SIDE[cy]
        beside = yr_ref[side, 5 if fluid else Y_SENT[side].index(i)]
    moved = lane_shift(velocity, slot, edge, here, below, above, beside)
    if cx:
        side = SIDE[cx]
        row = 5 if fluid else X_SENT[side].index(i)
        rows = moved.shape[0]

        def plane(s):
            return jnp.broadcast_to(xr_ref[side, pl.ds(row * slots + s, 1), :], (8, moved.shape[1]))

        corner = None
        if cy:
            k = CORNERS.index(i)
            n = 1 if fluid else 0
            corner = jnp.broadcast_to(cr_ref[k, n:n + 1, :], (8, 128))
        entering = lane_shift(
            velocity, slot, edge, plane(slot), plane(jnp.maximum(slot - 1, 0)) if cz == 1 else None,
            plane(jnp.minimum(slot + 1, slots - 1)) if cz == -1 else None, corner)
        index = lax.broadcasted_iota(jnp.int32, (8, moved.shape[1]), 0)
        moved = pltpu.roll(moved, cx % rows, 0)
        if cx == 1:
            moved = jnp.concatenate([jnp.where(index == 0, entering, moved[:8]), moved[8:]], axis=0)
        else:
            moved = jnp.concatenate([moved[:-8], jnp.where(index == 7, entering, moved[-8:])], axis=0)
    return moved


def collide_tiles(rows, width, read, rate, write):
    tiles = width // 128

    def body(step, carry):
        r = pl.multiple_of((step // tiles) * 8, 8)
        c = pl.multiple_of((step % tiles) * 128, 128)
        at = (pl.ds(r, 8), pl.ds(c, 128))
        post = collide([read(i, at) for i in range(Q)], rate(at))
        for i in range(Q):
            write(i, at, post[i])
        return carry

    lax.fori_loop(0, (rows // 8) * tiles, body, 0, unroll=4)


def emit_halo(slot, edge, post_ref, fluid_ref, ys_ref, xs_ref):
    slots, rows, width = fluid_ref.shape
    lane = lax.broadcasted_iota(jnp.int32, (rows, 128), 1)
    mine = lane // edge == slot
    for side, first in ((0, width - 128), (1, 0)):
        turn = lax.rem(slot * edge + (edge if side == 0 else 0), 128)
        for n in range(6):
            if n < 5:
                tile = post_ref[Y_SENT[side][n], slot, :, first:first + 128]
            else:
                tile = fluid_ref[slot, :, first:first + 128].astype(jnp.float32)
            ys_ref[side, n] = jnp.where(mine, pltpu.roll(tile, turn, 1), ys_ref[side, n])
    for side, row in ((0, rows - 1), (1, 0)):
        for n in range(5):
            xs_ref[side, pl.ds(n * slots + slot, 1), :] = post_ref[X_SENT[side][n], slot, row:row + 1, :]
        xs_ref[side, pl.ds(5 * slots + slot, 1), :] = fluid_ref[slot, row:row + 1, :].astype(jnp.float32)


def emit_corners(rows, ys_ref, cs_ref):
    for k, i in enumerate(CORNERS):
        cx, cy, _z = VELOCITIES[i]
        row = rows - 1 if cx == 1 else 0
        ys = SIDE[cy]
        cs_ref[k, 0:1, :] = ys_ref[ys, Y_SENT[ys].index(i), row:row + 1, :]
        cs_ref[k, 1:2, :] = ys_ref[ys, 5, row:row + 1, :]
        cs_ref[k, 2:8, :] = jnp.zeros((6, 128), jnp.float32)


def stream_slot(slot, edge, slots, mask_ref, post_ref, halo, write):
    below, above = jnp.maximum(slot - 1, 0), jnp.minimum(slot + 1, slots - 1)
    write(0, post_ref[0, slot])
    for i in range(1, Q):
        cz = VELOCITIES[i][2]
        own = post_ref[i, slot]
        value = arrive(
            i, slot, edge, slots, own, post_ref[i, below] if cz == 1 else None,
            post_ref[i, above] if cz == -1 else None, *halo, False)
        mask = mask_ref[slot]
        stay = jnp.where(mask > 0, post_ref[OPPOSITE[i], slot], own)
        write(i, jnp.where((mask & (1 << i)) != 0, value, stay))


def make_mask(slot, edge, slots, fluid_ref, halo, mask_ref):
    rows, width = fluid_ref.shape[1:]
    row = lax.broadcasted_iota(jnp.int32, (rows, width), 0)
    lane = lax.broadcasted_iota(jnp.int32, (rows, width), 1)
    depth = lane % edge
    z, b = lax.axis_index("bz"), lax.axis_index("bxy")
    at_end = (b == 0, b == lax.axis_size("bxy") - 1, z == 0, z == lax.axis_size("bz") - 1)
    fluid = fluid_ref[slot].astype(jnp.float32)
    below = fluid_ref[jnp.maximum(slot - 1, 0)].astype(jnp.float32)
    above = fluid_ref[jnp.minimum(slot + 1, slots - 1)].astype(jnp.float32)
    bits = jnp.ones((rows, width), jnp.int32)
    for i in range(1, Q):
        cx, cy, cz = VELOCITIES[i]
        source = arrive(i, slot, edge, slots, fluid, below if cz == 1 else None,
                        above if cz == -1 else None, *halo, True)
        bit = jnp.where(source > 0.5, 1 << i, 0)
        if cx:
            edge_row = 0 if cx == 1 else rows - 1
            bit = jnp.where((row == edge_row) & at_end[0 if cx == 1 else 1], 0, bit)
        if cy:
            outer = lane < edge if cy == 1 else lane >= width - edge
            bit = jnp.where(outer & at_end[2 if cy == 1 else 3], 0, bit)
        if cz:
            final = 0 if cz == 1 else slots - 1
            face = 0 if cz == 1 else edge - 1
            bit = jnp.where((depth == face) & (slot == final), 0, bit)
        bits = bits | bit
    mask_ref[slot] = jnp.where(fluid_ref[slot] > 0, bits, 0)


def pack_shell(step, i, edge, values, hz, hx, hy):
    value = values[i]
    rows, width = value.shape
    for axis, c in enumerate(VELOCITIES[i]):
        if not c:
            continue
        n = TURNS[axis].index(i) + step * len(TURNS[axis])
        if axis == 0:
            row = 0 if c == 1 else rows - 1
            hx[n:n + 1, :] = value[row:row + 1, :]
        elif axis == 1:
            per = 128 // edge
            t, g = n // per, n % per
            tile = value[:, :128] if c == 1 else value[:, width - 128:]
            shift = (g * edge - (0 if c == 1 else 128 - edge)) % 128
            tile = pltpu.roll(tile, shift, 1) if shift else tile
            if g:
                lane = lax.broadcasted_iota(jnp.int32, tile.shape, 1)
                tile = jnp.where(lane >= g * edge, tile, hy[:, t * 128:(t + 1) * 128])
            hy[:, t * 128:(t + 1) * 128] = tile
        elif n % 2:
            depth = lax.broadcasted_iota(jnp.int32, value.shape, 1) % edge
            pair = (values[i - 1], value) if c == -1 else (value, values[i - 1])
            both = jnp.where(depth == 0, pair[0], pair[1])
            both = pltpu.roll(both, n, 1)
            hz[...] = jnp.where(depth // 2 == n // 2, both, hz[...]) if n > 1 else both


def fold(edge, whole):
    used = 2 * len(TURNS[2])
    free, left = edge - used, 2 * used - edge
    half = whole.shape[1] // 2
    depth = lax.broadcasted_iota(jnp.int32, whole.shape, 1)[:, :half] % edge
    far = whole[:, half:]
    near = jnp.where(depth < used, whole[:, :half], pltpu.roll(far, used, 1))
    far = pltpu.roll(far, half - free, 1)
    while left < edge:
        half = far.shape[1] // 2
        far = jnp.where(depth[:, :half] < left, far[:, :half], pltpu.roll(far[:, half:], left, 1))
        left *= 2
    return jnp.concatenate([near, far], axis=1)


def unfold(edge, folded, width):
    used = 2 * len(TURNS[2])
    free, left = edge - used, 2 * used - edge
    half = width // 2
    depth = lax.broadcasted_iota(jnp.int32, (folded.shape[0], half), 1) % edge
    near, far = folded[:, :half], folded[:, half:]
    size = edge
    while size > left:
        size //= 2
        far = jnp.concatenate([far, pltpu.roll(far, far.shape[1] - size, 1)], axis=1)
    far = pltpu.roll(far, free, 1)
    return jnp.concatenate([near, jnp.where(depth < free, pltpu.roll(near, half - used, 1), far)], axis=1)


def patch_shell(step, i, edge, value, hz, hx, hy):
    rows, width = value.shape
    for axis, c in enumerate(VELOCITIES[i]):
        if not c:
            continue
        n = TURNS[axis].index(i) + step * len(TURNS[axis])
        if axis == 0:
            row = 0 if c == 1 else rows - 1
            index = lax.broadcasted_iota(jnp.int32, value.shape, 0)
            value = jnp.where(index == row, jnp.broadcast_to(hx[n:n + 1, :], value.shape), value)
        elif axis == 1:
            per = 128 // edge
            t, g = n // per, n % per
            shift = ((0 if c == 1 else 128 - edge) - g * edge) % 128
            tile = hy[:, t * 128:(t + 1) * 128]
            tile = pltpu.roll(tile, shift, 1) if shift else tile
            lane = lax.broadcasted_iota(jnp.int32, tile.shape, 1)
            if c == 1:
                value = jnp.concatenate([jnp.where(lane < edge, tile, value[:, :128]), value[:, 128:]], axis=1)
            else:
                value = jnp.concatenate(
                    [value[:, :-128], jnp.where(lane >= 128 - edge, tile, value[:, -128:])], axis=1)
        else:
            depth = lax.broadcasted_iota(jnp.int32, value.shape, 1) % edge
            face = 0 if c == 1 else edge - 1
            turned = pltpu.roll(hz[...], width - (n | 1), 1)
            value = jnp.where(depth == face, turned, value)
    return value


def pulled(i, edge, here):
    cx, cy, cz = VELOCITIES[i]
    lanes = (cy * edge + cz) % here.shape[1]
    here = pltpu.roll(here, lanes, 1) if lanes else here
    return pltpu.roll(here, cx % here.shape[0], 0) if cx else here


def redo_block(edge, f, hz, hx, hy, mask_ref, next_ref):
    rows, width = f.shape[1:]
    fluid = jnp.where(f[Q] > 0.0, 1.0, 0.0)
    bits = jnp.ones((rows, width), jnp.int32)
    for i in range(1, Q):
        bits = bits | jnp.where(pulled(i, edge, fluid) > 0.5, 1 << i, 0)
    mask_ref[...] = jnp.where(f[Q] > 0.0, bits, 0)

    def put(i, at, value):
        f[(i,) + at] = value

    def stream(step):
        next_ref[0] = f[0]
        for i in range(1, Q):
            own = f[i]
            mask = mask_ref[...]
            stay = jnp.where(mask > 0, f[OPPOSITE[i]], own)
            value = jnp.where((mask & (1 << i)) != 0, pulled(i, edge, own), stay)
            next_ref[i] = patch_shell(step, i, edge, value, hz, hx, hy)

    def rate(at):
        return f[(Q,) + at]

    collide_tiles(rows, width, lambda i, at: f[(i,) + at], rate, put)
    stream(0)
    collide_tiles(rows, width, lambda i, at: next_ref[(i,) + at], rate, put)
    stream(1)


def choose(picks, values):
    taken = []
    for pick in picks:
        out = values[0]
        for j in range(1, len(values)):
            out = jnp.where(pick == j, values[j], out)
        taken.append(out)
    return taken


def cuts_of(n):
    half = (n + 1) // 2
    cuts = (0, half // 2, half, half + (n - half + 1) // 2, n)
    return [slice(cuts[k], cuts[k + 1]) for k in range(4)]


EARLY = cuts_of(Q + 1)
LATE = cuts_of(Q)
PIECES = 11


def solve_kernel(edge, pdfs, relax, fluid, goal_ref, a_ref, got, table_ref,
                 relax_ref, fluid_ref, b_ref, next_ref, mask_ref, ys1, xs1, cs1, yr1, xr1, cr1, ys2, xs2, cs2, yr2, xr2, cr2,
                 hz, hx, hy, early_s, hz_s, hx_s, hy_s, late_s, early_r, hz_r, hx_r, hy_r,
                 early_p, hz_p, hx_p, hy_p, late_p, redo_mask, note_s, note_r, note_m,
                 load_sem, row_sem, halo_send, halo_recv, note_send, note_recv, note_sem, send_sem, recv_sem):
    slots, rows, width = fluid_ref.shape
    nz, nb = lax.axis_size("bz"), lax.axis_size("bxy")
    z, b = lax.axis_index("bz"), lax.axis_index("bxy")

    loads = [pltpu.make_async_copy(pdfs.at[slice(s.start, min(s.stop, Q))], a_ref.at[slice(s.start, min(s.stop, Q))],
                                   load_sem.at[n]) for n, s in enumerate(EARLY)]
    side_loads = [pltpu.make_async_copy(relax, relax_ref, load_sem.at[4]),
                  pltpu.make_async_copy(fluid, fluid_ref, load_sem.at[5])]
    for load in loads + side_loads:
        load.start()

    across = math.isqrt(nb // 2)
    row = 2 * across
    bends = across == 2 and nb == 2 * row
    cut = row - 1 if bends else nb
    low, high = cut + 1 - row, cut + row
    no = b < 0
    goes_right, goes_left = (b < nb - 1) & (b != cut), (b > 0) & (b != cut + 1)
    at_cut, past_cut, is_low, is_high = (
        (b == cut, b == cut + 1, b == low, b == high) if bends else (no, no, no, no))

    def there(dz, db):
        exists = None
        for at, step, count in ((z, dz, nz), (b, db, nb)):
            if step:
                inside = at < count - 1 if step == 1 else at > 0
                exists = inside if exists is None else exists & inside
        return exists

    ways = [(1, 0), (-1, 0), (0, 1), (0, -1)] + [(VELOCITIES[i][1], VELOCITIES[i][0]) for i in CORNERS]
    meets = [(there(dz, db), (z + dz, b + db)) for dz, db in ways[:4]]
    if bends:
        for who in (at_cut, past_cut):
            meets += [(who, (z, low)), (who, (z, high))]
        for who in (is_low, is_high):
            meets += [(who, (z, cut)), (who, (z, cut + 1))]
    barrier = pltpu.get_barrier_semaphore()
    count = 0
    for who, peer in meets:
        count = count + who.astype(jnp.int32)

        @pl.when(who)
        def _():
            pl.semaphore_signal(barrier, inc=1, device_id=peer, device_id_type=MESH)

    pl.semaphore_wait(barrier, count)
    rows_met = 0
    for dz, db in ways[:2]:
        rows_met = rows_met + there(dz, db).astype(jnp.int32)

        @pl.when(there(dz, db))
        def _():
            pl.semaphore_signal(row_sem, inc=1, device_id=(z + dz, b + db), device_id_type=MESH)

    goal = [goal_ref[0, 0, j] for j in range(slots)]
    base = b * slots

    def flag(t):
        return t.astype(jnp.int32)

    def nth(hits, n):
        before, found = jnp.int32(0), jnp.int32(0)
        for j in range(slots):
            found = found + jnp.where(hits[j] & (before == n), j, 0)
            before = before + flag(hits[j])
        return found

    to_right = [g >= base + slots for g in goal]
    to_left = [g < base for g in goal]
    first_pick = (nth(to_right, 0), nth(to_left, 0))
    second_pick = (nth(to_right, 1), nth(to_left, 1))

    at_row = lax.broadcasted_iota(jnp.int32, note_s.shape, 0)
    note = jnp.zeros(note_s.shape, jnp.int32)
    for j in range(slots):
        note = jnp.where(at_row == j, goal[j], note)
    note_s[...] = note

    def note_copy(n):
        db = 1 if n == 0 else -1
        return remote(note_s, note_r.at[n], note_send.at[n], note_recv.at[n], (z, b + db))

    for n, db in ((0, 1), (1, -1)):
        @pl.when(there(0, db))
        def _():
            note_copy(n).start()

    pieces = [(early_s.at[0, s], early_s.at[1, s], early_r.at[0, s], early_r.at[1, s], early_p.at[s], n < 2)
              for n, s in enumerate(EARLY)]
    for s, r, p, first in ((hz_s, hz_r, hz_p, True), (hx_s, hx_r, hx_p, False), (hy_s, hy_r, hy_p, False)):
        pieces.append((s.at[0], s.at[1], r.at[0], r.at[1], p, first))
    pieces += [(late_s.at[0, s], late_s.at[1, s], got.at[0, 1, s], got.at[1, 1, s], late_p.at[s], n % 2 == 1)
               for n, s in enumerate(LATE)]

    def send_near(p):
        to_r, to_l, from_l, from_r, passing, first = pieces[p]

        @pl.when(goes_right)
        def _():
            remote(to_r, from_l, send_sem.at[0, p], recv_sem.at[0, p], (z, b + 1)).start()

        @pl.when(goes_left)
        def _():
            remote(to_l, from_r, send_sem.at[1, p], recv_sem.at[1, p], (z, b - 1)).start()

    def send_bent(p):
        to_r, to_l, from_l, from_r, passing, first = pieces[p]
        if bends:
            @pl.when(at_cut)
            def _():
                remote(to_r, passing, send_sem.at[0, p], recv_sem.at[2, p], (z, low if first else high)).start()

            @pl.when(past_cut)
            def _():
                remote(to_l, passing, send_sem.at[1, p], recv_sem.at[2, p], (z, high if first else low)).start()

    def forward(p):
        to_r, to_l, from_l, from_r, passing, first = pieces[p]
        if bends:
            for who, ahead in ((is_low, True), (is_high, False)):
                @pl.when(who)
                def _():
                    remote(to_r, passing, send_sem.at[2, p], recv_sem.at[2, p], (z, cut)).wait_recv()
                    if first == ahead:
                        remote(passing, from_l, send_sem.at[2, p], recv_sem.at[0, p], (z, cut + 1)).start()
                    else:
                        remote(passing, from_r, send_sem.at[2, p], recv_sem.at[1, p], (z, cut)).start()

    def arrived(p):
        to_r, to_l, from_l, from_r, passing, first = pieces[p]

        @pl.when(b > 0)
        def _():
            remote(to_r, from_l, send_sem.at[0, p], recv_sem.at[0, p], (z, b - 1)).wait_recv()

        @pl.when(b < nb - 1)
        def _():
            remote(to_l, from_r, send_sem.at[1, p], recv_sem.at[1, p], (z, b + 1)).wait_recv()

    def sent(p):
        to_r, to_l, from_l, from_r, passing, first = pieces[p]

        @pl.when(b < nb - 1)
        def _():
            remote(to_r, from_l, send_sem.at[0, p], recv_sem.at[0, p], (z, b + 1)).wait_send()

        @pl.when(b > 0)
        def _():
            remote(to_l, from_r, send_sem.at[1, p], recv_sem.at[1, p], (z, b - 1)).wait_send()

        if bends:
            @pl.when(is_low | is_high)
            def _():
                remote(passing, from_l, send_sem.at[2, p], recv_sem.at[0, p], (z, cut)).wait_send()

    for n, s in enumerate(EARLY):
        loads[n].wait()

        def gather(i, carry):
            early_s[0, i], early_s[1, i] = choose(first_pick, [a_ref[i, j] for j in range(slots)])
            return carry

        lax.fori_loop(s.start, min(s.stop, Q), gather, 0)
        if s.stop == Q + 1:
            for load in side_loads:
                load.wait()
            early_s[0, Q], early_s[1, Q] = choose(
                first_pick, [jnp.where(fluid_ref[j] > 0, relax_ref[j], 0.0) for j in range(slots)])
        if n == 0:
            send_near(0)
        if n == 2:
            send_bent(2)

    def rate_of(slot):
        return lambda at: jnp.where(fluid_ref[(slot,) + at] > 0, relax_ref[(slot,) + at], 0.0)

    def first_step(slot, carry):
        def put(i, at, value):
            a_ref[(i, slot) + at] = value

        collide_tiles(rows, width, lambda i, at: a_ref[(i, slot) + at], rate_of(slot), put)
        emit_halo(slot, edge, a_ref, fluid_ref, ys1, xs1)
        return carry

    def routes(step):
        ys, xs, cs, yr, xr, cr = ((ys1, xs1, cs1, yr1, xr1, cr1), (ys2, xs2, cs2, yr2, xr2, cr2))[step]
        ends = [(ys.at[0], yr.at[0]), (ys.at[1], yr.at[1]), (xs.at[0], xr.at[0]), (xs.at[1], xr.at[1])]
        ends += [(cs.at[k], cr.at[k]) for k in range(4)]
        return [(src, dst, dz, db, step * 8 + n) for n, ((src, dst), (dz, db)) in enumerate(zip(ends, ways))]

    def exchange(step):
        for src, dst, dz, db, n in routes(step):
            @pl.when(there(dz, db))
            def _():
                remote(src, dst, halo_send.at[n], halo_recv.at[n], (z + dz, b + db)).start()

    def await_halo(step):
        for src, dst, dz, db, n in routes(step):
            @pl.when(there(-dz, -db))
            def _():
                remote(src, dst, halo_send.at[n], halo_recv.at[n], (z - dz, b - db)).wait_recv()

    ys1[...] = jnp.zeros(ys1.shape, jnp.float32)
    ys2[...] = jnp.zeros(ys2.shape, jnp.float32)
    lax.fori_loop(0, slots, first_step, 0)
    emit_corners(rows, ys1, cs1)
    pl.semaphore_wait(row_sem, rows_met)
    exchange(0)
    send_near(1)
    send_near(2)
    send_bent(3)
    send_bent(0)
    await_halo(0)
    forward(2)

    def middle_step(slot, carry):
        halo = (yr1, xr1, cr1)
        make_mask(slot, edge, slots, fluid_ref, halo, mask_ref)

        values = {}

        def write(i, value):
            next_ref[i] = values[i] = value
            pack_shell(0, i, edge, values, hz.at[slot], hx.at[slot], hy.at[slot])

        stream_slot(slot, edge, slots, mask_ref, a_ref, halo, write)

        def put(i, at, value):
            b_ref[(i, slot) + at] = value

        collide_tiles(rows, width, lambda i, at: next_ref[(i,) + at], rate_of(slot), put)
        emit_halo(slot, edge, b_ref, fluid_ref, ys2, xs2)
        return carry

    lax.fori_loop(0, slots, middle_step, 0)
    emit_corners(rows, ys2, cs2)
    exchange(1)
    send_near(3)
    send_bent(1)
    forward(3)
    await_halo(1)

    def last_step(slot, carry):
        values = {}

        def write(i, value):
            a_ref[i, slot] = values[i] = value
            pack_shell(1, i, edge, values, hz.at[slot], hx.at[slot], hy.at[slot])

        stream_slot(slot, edge, slots, mask_ref, b_ref, (yr2, xr2, cr2), write)
        return carry

    lax.fori_loop(0, slots, last_step, 0)
    for shell, staged in ((hx, hx_s), (hy, hy_s)):
        staged[0], staged[1] = choose(first_pick, [shell[j] for j in range(slots)])
    for side, whole in enumerate(choose(first_pick, [hz[j] for j in range(slots)])):
        hz_s[side] = fold(edge, whole)
    for p in (5, 6, 4):
        send_near(p)
        send_bent(p)
    for n, s in enumerate(LATE):
        def gather(i, carry):
            late_s[0, i], late_s[1, i] = choose(second_pick, [a_ref[i, j] for j in range(slots)])
            return carry

        lax.fori_loop(s.start, s.stop, gather, 0)
        send_near(7 + n)
        send_bent(7 + n)

    for p in (0, 5, 6, 1, 4, 7, 9):
        forward(p)
    for p in range(7):
        arrived(p)

    def redo(side, carry):
        hz[0] = unfold(edge, hz_r[side], width)
        redo_block(edge, early_r.at[side], hz.at[0], hx_r.at[side], hy_r.at[side], redo_mask, got.at[side, 0])
        return carry

    lax.fori_loop(jnp.where(b > 0, 0, 1), jnp.where(b < nb - 1, 2, 1), redo, 0)
    for p in (8, 10):
        forward(p)

    for n, db in ((0, 1), (1, -1)):
        @pl.when(there(0, -db))
        def _():
            remote(note_s, note_r.at[n], note_send.at[n], note_recv.at[n], (z, b - db)).wait_recv()

        @pl.when(there(0, db))
        def _():
            note_copy(n).wait_send()

    fetch = pltpu.make_async_copy(note_r, note_m, note_sem.at[0])
    fetch.start()
    fetch.wait()
    kind = [jnp.int32(0)] * slots
    index = [jnp.int32(k) for k in range(slots)]
    for k in range(slots):
        for j in range(slots):
            index[k] = jnp.where(goal[j] == base + k, j, index[k])
    for source, valid in ((1, b > 0), (2, b < nb - 1)):
        rank = jnp.int32(0)
        for j in range(slots):
            value = note_m[source - 1, j, 0]
            for k in range(slots):
                hit = valid & (value == base + k)
                kind[k] = jnp.where(hit, source, kind[k])
                index[k] = jnp.where(hit, rank, index[k])
            rank = rank + flag(valid & (value >= base) & (value < base + slots))
    line = lax.broadcasted_iota(jnp.int32, table_ref.shape, 0)
    entry = lax.broadcasted_iota(jnp.int32, table_ref.shape, 1)
    table = jnp.zeros(table_ref.shape, jnp.int32)
    for k in range(slots):
        table = jnp.where(entry == k, jnp.where(line == 0, kind[k], index[k]), table)
    table_ref[...] = table

    for step in range(2):
        for src, dst, dz, db, n in routes(step):
            @pl.when(there(dz, db))
            def _():
                remote(src, dst, halo_send.at[n], halo_recv.at[n], (z + dz, b + db)).wait_send()

    for p in range(7):
        sent(p)
    for p in range(7, PIECES):
        sent(p)
        arrived(p)


def solve(pdfs, relax, fluid, targets):
    q, slots, rows, width = pdfs.shape
    edge = rows
    f32, i32 = jnp.float32, jnp.int32
    hbm = pl.BlockSpec(memory_space=pl.ANY)
    vmem = pl.BlockSpec(memory_space=pltpu.VMEM)
    smem = pl.BlockSpec(memory_space=pltpu.SMEM)
    per = 128 // edge
    turns = 2 * len(TURNS[0])
    x_rows = -(-turns // 8) * 8
    y_lanes = -(-turns // per) * 128
    ys, xs, cs = (2, 6, rows, 128), (2, -(-6 * slots // 8) * 8, width), (4, 8, 128)

    z_lanes = 2 * len(TURNS[2]) * (width // edge)

    def shells(lead, lanes=z_lanes):
        return [pltpu.VMEM(lead + s, f32) for s in ((rows, lanes), (x_rows, width), (rows, y_lanes))]

    halo = [pltpu.VMEM(s, f32) for s in (ys, xs, cs)]
    dma = pltpu.SemaphoreType.DMA
    scratch = [pltpu.VMEM(relax.shape, f32), pltpu.VMEM(fluid.shape, i32), pltpu.VMEM(pdfs.shape, f32), pltpu.VMEM((q, rows, width), f32),
               pltpu.VMEM(fluid.shape, i32)] + halo * 4
    scratch += shells((slots,), width)
    scratch += [pltpu.VMEM((2, q + 1, rows, width), f32)] + shells((2,)) + [pltpu.VMEM((2, q, rows, width), f32)]
    scratch += [pltpu.VMEM((2, q + 1, rows, width), f32)] + shells((2,))
    scratch += [pltpu.VMEM((q + 1, rows, width), f32)] + shells(()) + [pltpu.VMEM((q, rows, width), f32)]
    scratch += [pltpu.VMEM((rows, width), i32)]
    scratch += [pltpu.VMEM((8, 128), i32), pltpu.VMEM((2, 8, 128), i32), pltpu.SMEM((2, 8, 128), i32)]
    scratch += [dma((6,)), pltpu.SemaphoreType.REGULAR, dma((16,)), dma((16,)), dma((2,)), dma((2,)), dma((1,)),
                dma((3, PIECES)), dma((3, PIECES))]
    return pl.pallas_call(
        functools.partial(solve_kernel, edge),
        out_shape=[pltpu.VMEM(pdfs.shape, f32), pltpu.VMEM((2, 2, q, rows, width), f32),
                   pltpu.VMEM((8, 128), i32)],
        in_specs=[hbm, hbm, hbm, smem], out_specs=[vmem, vmem, vmem], scratch_shapes=scratch,
        compiler_params=pltpu.CompilerParams(collective_id=0, has_side_effects=True, vmem_limit_bytes=40 * 1024 * 1024),
        name="solve",
    )(pdfs, relax, fluid, targets)


def place_kernel(table_ref, own, got, out, sem):
    slots = out.shape[1]
    for k in range(slots):
        for kind in range(3):
            @pl.when(table_ref[0, k] == kind)
            def _():
                at = table_ref[1, k]
                for n, s in enumerate(LATE):
                    src = own.at[s, at] if kind == 0 else got.at[kind - 1, at, s]
                    pltpu.make_async_copy(src, out.at[s, k], sem.at[k, n]).start()

    for k in range(slots):
        for n, s in enumerate(LATE):
            pltpu.make_async_copy(own.at[s, k], out.at[s, k], sem.at[k, n]).wait()


def place(own, got, table):
    hbm = pl.BlockSpec(memory_space=pl.ANY)
    smem = pl.BlockSpec(memory_space=pltpu.SMEM)
    return pl.pallas_call(
        place_kernel, out_shape=jax.ShapeDtypeStruct(own.shape, own.dtype),
        in_specs=[smem, hbm, hbm], out_specs=hbm, scratch_shapes=[pltpu.SemaphoreType.DMA((own.shape[1], len(LATE)))],
        compiler_params=pltpu.CompilerParams(vmem_limit_bytes=1024 * 1024), name="place",
    )(table, own, got)


def on_device(pdfs, relax, fluid, targets):
    own, got, table = solve(pdfs, relax, fluid, targets)
    return place(own, got, table)


def solution(mesh):
    placed = (
        P(None, None, "bxy", "bz"),
        P(None, "bxy", "bz"),
        P(None, "bxy", "bz"),
        P("bz", "bxy", None),
    )
    return jax.shard_map(
        on_device, mesh=mesh, in_specs=placed, out_specs=P(None, None, "bxy", "bz"), check_vma=False
    )
```

```python
import functools
import math

import jax
import jax.numpy as jnp
from jax import lax
from jax.experimental import pallas as pl
from jax.experimental.pallas import tpu as pltpu
from jax.sharding import PartitionSpec as P

MESH = pl.DeviceIdType.MESH
VELOCITIES = (
    (0, 0, 0), (1, 0, 0), (-1, 0, 0), (0, 1, 0), (0, -1, 0), (0, 0, 1), (0, 0, -1),
    (1, 1, 0), (-1, -1, 0), (1, -1, 0), (-1, 1, 0), (1, 0, 1), (-1, 0, -1),
    (1, 0, -1), (-1, 0, 1), (0, 1, 1), (0, -1, -1), (0, 1, -1), (0, -1, 1),
)
OPPOSITE = (0, 2, 1, 4, 3, 6, 5, 8, 7, 10, 9, 12, 11, 14, 13, 16, 15, 18, 17)
Q = 19
TURNS = tuple(tuple(i for i in range(Q) if VELOCITIES[i][axis]) for axis in range(3))
Y_SENT = tuple(tuple(i for i in range(Q) if VELOCITIES[i][1] == c) for c in (1, -1))
X_SENT = tuple(tuple(i for i in range(Q) if VELOCITIES[i][0] == c) for c in (1, -1))
CORNERS = (7, 8, 9, 10)
SIDE = {1: 0, -1: 1}
VMEM_LIMIT = 60 * 1024 * 1024


def collide(f, rate):
    pair = {i: (f[i] + f[i + 1], f[i] - f[i + 1]) for i in range(1, Q, 2)}
    density = f[0]
    for i in range(1, Q, 2):
        density = density + pair[i][0]
    scale = 3.0 / density
    flow = []
    for axis in range(3):
        total = None
        for i in range(1, Q, 2):
            c = VELOCITIES[i][axis]
            if c:
                d = pair[i][1]
                total = d if total is None else (total + d if c == 1 else total - d)
        flow.append(total * scale)
    base = 1.0 - (flow[0] * flow[0] + flow[1] * flow[1] + flow[2] * flow[2]) * (1.0 / 6.0)
    keep = 1.0 - rate
    drive = rate * density
    post = [None] * Q
    post[0] = keep * f[0] + (drive * (1.0 / 3.0)) * base
    near, far = drive * (1.0 / 18.0), drive * (1.0 / 36.0)
    for i in range(1, Q, 2):
        along = None
        for axis in range(3):
            c = VELOCITIES[i][axis]
            if c:
                along = flow[axis] if along is None else (along + flow[axis] if c == 1 else along - flow[axis])
        even = base + 0.5 * (along * along)
        weight = near if i < 7 else far
        post[i] = keep * f[i] + weight * (even + along)
        post[i + 1] = keep * f[i + 1] + weight * (even - along)
    return post


def remote(src, dst, send_sem, recv_sem, device):
    return pltpu.make_async_remote_copy(
        src_ref=src, dst_ref=dst, send_sem=send_sem, recv_sem=recv_sem, device_id=device, device_id_type=MESH)


def lane_shift(velocity, slot, edge, here, below, above, beside):
    _cx, cy, cz = velocity
    width = here.shape[1]
    step = cy * edge + cz
    moved = here if step == 0 else pltpu.roll(here, step % width, 1)
    if cz:
        depth = lax.broadcasted_iota(jnp.int32, here.shape, 1) % edge
        other, face = (below, 0) if cz == 1 else (above, edge - 1)
        carry = step - cz * edge
        wrapped = other if carry == 0 else pltpu.roll(other, carry % width, 1)
        moved = jnp.where(depth == face, wrapped, moved)
    if cy:
        lane = lax.broadcasted_iota(jnp.int32, (here.shape[0], 128), 1)
        offset = 128 if cy == 1 else 256 - edge
        outside = pltpu.roll(beside, lax.rem(offset + cz + 128 - slot * edge, 128), 1)
        if cy == 1:
            moved = jnp.concatenate([jnp.where(lane < edge, outside, moved[:, :128]), moved[:, 128:]], axis=1)
        else:
            moved = jnp.concatenate(
                [moved[:, :-128], jnp.where(lane >= 128 - edge, outside, moved[:, -128:])], axis=1)
    return moved


def arrive(i, slot, edge, slots, here, below, above, yr_ref, xr_ref, cr_ref, fluid):
    velocity = cx, cy, cz = VELOCITIES[i]
    beside = None
    if cy:
        side = SIDE[cy]
        beside = yr_ref[side, 5 if fluid else Y_SENT[side].index(i)]
    moved = lane_shift(velocity, slot, edge, here, below, above, beside)
    if cx:
        side = SIDE[cx]
        row = 5 if fluid else X_SENT[side].index(i)
        rows = moved.shape[0]

        def plane(s):
            return jnp.broadcast_to(xr_ref[side, pl.ds(row * slots + s, 1), :], (8, moved.shape[1]))

        corner = None
        if cy:
            k = CORNERS.index(i)
            n = 1 if fluid else 0
            corner = jnp.broadcast_to(cr_ref[k, n:n + 1, :], (8, 128))
        entering = lane_shift(
            velocity, slot, edge, plane(slot), plane(jnp.maximum(slot - 1, 0)) if cz == 1 else None,
            plane(jnp.minimum(slot + 1, slots - 1)) if cz == -1 else None, corner)
        index = lax.broadcasted_iota(jnp.int32, (8, moved.shape[1]), 0)
        moved = pltpu.roll(moved, cx % rows, 0)
        if cx == 1:
            moved = jnp.concatenate([jnp.where(index == 0, entering, moved[:8]), moved[8:]], axis=0)
        else:
            moved = jnp.concatenate([moved[:-8], jnp.where(index == 7, entering, moved[-8:])], axis=0)
    return moved


def collide_tiles(rows, width, read, rate, write):
    tiles = width // 128

    def body(step, carry):
        r = pl.multiple_of((step // tiles) * 8, 8)
        c = pl.multiple_of((step % tiles) * 128, 128)
        at = (pl.ds(r, 8), pl.ds(c, 128))
        post = collide([read(i, at) for i in range(Q)], rate(at))
        for i in range(Q):
            write(i, at, post[i])
        return carry

    lax.fori_loop(0, (rows // 8) * tiles, body, 0, unroll=4)


def emit_halo(slot, edge, post_ref, fluid_ref, ys_ref, xs_ref):
    slots, rows, width = fluid_ref.shape
    lane = lax.broadcasted_iota(jnp.int32, (rows, 128), 1)
    mine = lane // edge == slot
    for side, first in ((0, width - 128), (1, 0)):
        turn = lax.rem(slot * edge + (edge if side == 0 else 0), 128)
        for n in range(6):
            if n < 5:
                tile = post_ref[Y_SENT[side][n], slot, :, first:first + 128]
            else:
                tile = fluid_ref[slot, :, first:first + 128].astype(jnp.float32)
            ys_ref[side, n] = jnp.where(mine, pltpu.roll(tile, turn, 1), ys_ref[side, n])
    for side, row in ((0, rows - 1), (1, 0)):
        for n in range(5):
            xs_ref[side, pl.ds(n * slots + slot, 1), :] = post_ref[X_SENT[side][n], slot, row:row + 1, :]
        xs_ref[side, pl.ds(5 * slots + slot, 1), :] = fluid_ref[slot, row:row + 1, :].astype(jnp.float32)


def emit_corners(rows, ys_ref, cs_ref):
    for k, i in enumerate(CORNERS):
        cx, cy, _z = VELOCITIES[i]
        row = rows - 1 if cx == 1 else 0
        ys = SIDE[cy]
        cs_ref[k, 0:1, :] = ys_ref[ys, Y_SENT[ys].index(i), row:row + 1, :]
        cs_ref[k, 1:2, :] = ys_ref[ys, 5, row:row + 1, :]
        cs_ref[k, 2:8, :] = jnp.zeros((6, 128), jnp.float32)


def stream_slot(slot, edge, slots, mask_ref, post_ref, halo, write):
    below, above = jnp.maximum(slot - 1, 0), jnp.minimum(slot + 1, slots - 1)
    write(0, post_ref[0, slot])
    for i in range(1, Q):
        cz = VELOCITIES[i][2]
        own = post_ref[i, slot]
        value = arrive(
            i, slot, edge, slots, own, post_ref[i, below] if cz == 1 else None,
            post_ref[i, above] if cz == -1 else None, *halo, False)
        mask = mask_ref[slot]
        stay = jnp.where(mask > 0, post_ref[OPPOSITE[i], slot], own)
        write(i, jnp.where((mask & (1 << i)) != 0, value, stay))


def make_mask(slot, edge, slots, fluid_ref, halo, mask_ref):
    rows, width = fluid_ref.shape[1:]
    row = lax.broadcasted_iota(jnp.int32, (rows, width), 0)
    lane = lax.broadcasted_iota(jnp.int32, (rows, width), 1)
    depth = lane % edge
    z, b = lax.axis_index("bz"), lax.axis_index("bxy")
    at_end = (b == 0, b == lax.axis_size("bxy") - 1, z == 0, z == lax.axis_size("bz") - 1)
    fluid = fluid_ref[slot].astype(jnp.float32)
    below = fluid_ref[jnp.maximum(slot - 1, 0)].astype(jnp.float32)
    above = fluid_ref[jnp.minimum(slot + 1, slots - 1)].astype(jnp.float32)
    bits = jnp.ones((rows, width), jnp.int32)
    for i in range(1, Q):
        cx, cy, cz = VELOCITIES[i]
        source = arrive(i, slot, edge, slots, fluid, below if cz == 1 else None,
                        above if cz == -1 else None, *halo, True)
        bit = jnp.where(source > 0.5, 1 << i, 0)
        if cx:
            edge_row = 0 if cx == 1 else rows - 1
            bit = jnp.where((row == edge_row) & at_end[0 if cx == 1 else 1], 0, bit)
        if cy:
            outer = lane < edge if cy == 1 else lane >= width - edge
            bit = jnp.where(outer & at_end[2 if cy == 1 else 3], 0, bit)
        if cz:
            final = 0 if cz == 1 else slots - 1
            face = 0 if cz == 1 else edge - 1
            bit = jnp.where((depth == face) & (slot == final), 0, bit)
        bits = bits | bit
    mask_ref[slot] = jnp.where(fluid_ref[slot] > 0, bits, 0)


def pack_shell(step, i, edge, values, hz, hx, hy):
    value = values[i]
    rows, width = value.shape
    for axis, c in enumerate(VELOCITIES[i]):
        if not c:
            continue
        n = TURNS[axis].index(i) + step * len(TURNS[axis])
        if axis == 0:
            row = 0 if c == 1 else rows - 1
            hx[n:n + 1, :] = value[row:row + 1, :]
        elif axis == 1:
            per = 128 // edge
            t, g = n // per, n % per
            tile = value[:, :128] if c == 1 else value[:, width - 128:]
            shift = (g * edge - (0 if c == 1 else 128 - edge)) % 128
            tile = pltpu.roll(tile, shift, 1) if shift else tile
            if g:
                lane = lax.broadcasted_iota(jnp.int32, tile.shape, 1)
                tile = jnp.where(lane >= g * edge, tile, hy[:, t * 128:(t + 1) * 128])
            hy[:, t * 128:(t + 1) * 128] = tile
        elif n % 2:
            depth = lax.broadcasted_iota(jnp.int32, value.shape, 1) % edge
            pair = (values[i - 1], value) if c == -1 else (value, values[i - 1])
            both = jnp.where(depth == 0, pair[0], pair[1])
            both = pltpu.roll(both, n, 1)
            hz[...] = jnp.where(depth // 2 == n // 2, both, hz[...]) if n > 1 else both


def fold(edge, whole):
    used = 2 * len(TURNS[2])
    free, left = edge - used, 2 * used - edge
    half = whole.shape[1] // 2
    depth = lax.broadcasted_iota(jnp.int32, whole.shape, 1)[:, :half] % edge
    far = whole[:, half:]
    near = jnp.where(depth < used, whole[:, :half], pltpu.roll(far, used, 1))
    far = pltpu.roll(far, half - free, 1)
    while left < edge:
        half = far.shape[1] // 2
        far = jnp.where(depth[:, :half] < left, far[:, :half], pltpu.roll(far[:, half:], left, 1))
        left *= 2
    return jnp.concatenate([near, far], axis=1)


def unfold(edge, folded, width):
    used = 2 * len(TURNS[2])
    free, left = edge - used, 2 * used - edge
    half = width // 2
    depth = lax.broadcasted_iota(jnp.int32, (folded.shape[0], half), 1) % edge
    near, far = folded[:, :half], folded[:, half:]
    size = edge
    while size > left:
        size //= 2
        far = jnp.concatenate([far, pltpu.roll(far, far.shape[1] - size, 1)], axis=1)
    far = pltpu.roll(far, free, 1)
    return jnp.concatenate([near, jnp.where(depth < free, pltpu.roll(near, half - used, 1), far)], axis=1)


def patch_shell(step, i, edge, value, hz, hx, hy):
    rows, width = value.shape
    for axis, c in enumerate(VELOCITIES[i]):
        if not c:
            continue
        n = TURNS[axis].index(i) + step * len(TURNS[axis])
        if axis == 0:
            row = 0 if c == 1 else rows - 1
            index = lax.broadcasted_iota(jnp.int32, value.shape, 0)
            value = jnp.where(index == row, jnp.broadcast_to(hx[n:n + 1, :], value.shape), value)
        elif axis == 1:
            per = 128 // edge
            t, g = n // per, n % per
            shift = ((0 if c == 1 else 128 - edge) - g * edge) % 128
            tile = hy[:, t * 128:(t + 1) * 128]
            tile = pltpu.roll(tile, shift, 1) if shift else tile
            lane = lax.broadcasted_iota(jnp.int32, tile.shape, 1)
            if c == 1:
                value = jnp.concatenate([jnp.where(lane < edge, tile, value[:, :128]), value[:, 128:]], axis=1)
            else:
                value = jnp.concatenate(
                    [value[:, :-128], jnp.where(lane >= 128 - edge, tile, value[:, -128:])], axis=1)
        else:
            depth = lax.broadcasted_iota(jnp.int32, value.shape, 1) % edge
            face = 0 if c == 1 else edge - 1
            turned = pltpu.roll(hz[...], width - (n | 1), 1)
            value = jnp.where(depth == face, turned, value)
    return value


def pulled(i, edge, here):
    cx, cy, cz = VELOCITIES[i]
    lanes = (cy * edge + cz) % here.shape[1]
    here = pltpu.roll(here, lanes, 1) if lanes else here
    return pltpu.roll(here, cx % here.shape[0], 0) if cx else here


def redo_block(edge, f, hz, hx, hy, mask_ref, next_ref):
    rows, width = f.shape[1:]
    fluid = jnp.where(f[Q] > 0.0, 1.0, 0.0)
    bits = jnp.ones((rows, width), jnp.int32)
    for i in range(1, Q):
        bits = bits | jnp.where(pulled(i, edge, fluid) > 0.5, 1 << i, 0)
    mask_ref[...] = jnp.where(f[Q] > 0.0, bits, 0)

    def put(i, at, value):
        f[(i,) + at] = value

    def stream(step):
        next_ref[0] = f[0]
        for i in range(1, Q):
            own = f[i]
            mask = mask_ref[...]
            stay = jnp.where(mask > 0, f[OPPOSITE[i]], own)
            value = jnp.where((mask & (1 << i)) != 0, pulled(i, edge, own), stay)
            next_ref[i] = patch_shell(step, i, edge, value, hz, hx, hy)

    def rate(at):
        return f[(Q,) + at]

    collide_tiles(rows, width, lambda i, at: f[(i,) + at], rate, put)
    stream(0)
    collide_tiles(rows, width, lambda i, at: next_ref[(i,) + at], rate, put)
    stream(1)


def choose(picks, values):
    taken = []
    for pick in picks:
        out = values[0]
        for j in range(1, len(values)):
            out = jnp.where(pick == j, values[j], out)
        taken.append(out)
    return taken


def cuts_of(n):
    half = (n + 1) // 2
    cuts = (0, half // 2, half, half + (n - half + 1) // 2, n)
    return [slice(cuts[k], cuts[k + 1]) for k in range(4)]


EARLY = cuts_of(Q + 1)
LATE = cuts_of(Q)
PIECES = 11


def solve_kernel(edge, pdfs, relax, fluid, goal_ref, a_ref, got, table_ref,
                 relax_ref, fluid_ref, b_ref, next_ref, mask_ref, ys1, xs1, cs1, yr1, xr1, cr1, ys2, xs2, cs2, yr2, xr2, cr2,
                 hz, hx, hy, early_s, hz_s, hx_s, hy_s, late_s, early_r, hz_r, hx_r, hy_r,
                 early_p, hz_p, hx_p, hy_p, late_p, redo_mask, note_s, note_r, note_m,
                 load_sem, row_sem, halo_send, halo_recv, note_send, note_recv, note_sem, send_sem, recv_sem):
    slots, rows, width = fluid_ref.shape
    nz, nb = lax.axis_size("bz"), lax.axis_size("bxy")
    z, b = lax.axis_index("bz"), lax.axis_index("bxy")

    loads = [pltpu.make_async_copy(pdfs.at[slice(s.start, min(s.stop, Q))], a_ref.at[slice(s.start, min(s.stop, Q))],
                                   load_sem.at[n]) for n, s in enumerate(EARLY)]
    side_loads = [pltpu.make_async_copy(relax, relax_ref, load_sem.at[4]),
                  pltpu.make_async_copy(fluid, fluid_ref, load_sem.at[5])]
    for load in loads + side_loads:
        load.start()

    spare = [(n, t) for n in range(2 * len(TURNS[0]) - hx_s.shape[1]) for t in range(width // 128)]
    across = math.isqrt(nb // 2)
    row = 2 * across
    bends = across == 2 and nb == 2 * row
    cut = row - 1 if bends else nb
    low, high = cut + 1 - row, cut + row
    no = b < 0
    goes_right, goes_left = (b < nb - 1) & (b != cut), (b > 0) & (b != cut + 1)
    at_cut, past_cut, is_low, is_high = (
        (b == cut, b == cut + 1, b == low, b == high) if bends else (no, no, no, no))

    def there(dz, db):
        exists = None
        for at, step, count in ((z, dz, nz), (b, db, nb)):
            if step:
                inside = at < count - 1 if step == 1 else at > 0
                exists = inside if exists is None else exists & inside
        return exists

    ways = [(1, 0), (-1, 0), (0, 1), (0, -1)] + [(VELOCITIES[i][1], VELOCITIES[i][0]) for i in CORNERS]
    meets = [(there(dz, db), (z + dz, b + db)) for dz, db in ways[:4]]
    if bends:
        for who in (at_cut, past_cut):
            meets += [(who, (z, low)), (who, (z, high))]
        for who in (is_low, is_high):
            meets += [(who, (z, cut)), (who, (z, cut + 1))]
    barrier = pltpu.get_barrier_semaphore()
    count = 0
    for who, peer in meets:
        count = count + who.astype(jnp.int32)

        @pl.when(who)
        def _():
            pl.semaphore_signal(barrier, inc=1, device_id=peer, device_id_type=MESH)

    pl.semaphore_wait(barrier, count)
    rows_met = 0
    for dz, db in ways[:2]:
        rows_met = rows_met + there(dz, db).astype(jnp.int32)

        @pl.when(there(dz, db))
        def _():
            pl.semaphore_signal(row_sem, inc=1, device_id=(z + dz, b + db), device_id_type=MESH)

    goal = [goal_ref[0, 0, j] for j in range(slots)]
    base = b * slots

    def flag(t):
        return t.astype(jnp.int32)

    def nth(hits, n):
        before, found = jnp.int32(0), jnp.int32(0)
        for j in range(slots):
            found = found + jnp.where(hits[j] & (before == n), j, 0)
            before = before + flag(hits[j])
        return found

    to_right = [g >= base + slots for g in goal]
    to_left = [g < base for g in goal]
    first_pick = (nth(to_right, 0), nth(to_left, 0))
    second_pick = (nth(to_right, 1), nth(to_left, 1))

    at_row = lax.broadcasted_iota(jnp.int32, note_s.shape, 0)
    note = jnp.zeros(note_s.shape, jnp.int32)
    for j in range(slots):
        note = jnp.where(at_row == j, goal[j], note)
    note_s[...] = note

    def note_copy(n):
        db = 1 if n == 0 else -1
        return remote(note_s, note_r.at[n], note_send.at[n], note_recv.at[n], (z, b + db))

    for n, db in ((0, 1), (1, -1)):
        @pl.when(there(0, db))
        def _():
            note_copy(n).start()

    pieces = [(early_s.at[0, s], early_s.at[1, s], early_r.at[0, s], early_r.at[1, s], early_p.at[s], n < 2)
              for n, s in enumerate(EARLY)]
    for s, r, p, first in ((hz_s, hz_r, hz_p, True), (hx_s, hx_r, hx_p, False), (hy_s, hy_r, hy_p, False)):
        pieces.append((s.at[0], s.at[1], r.at[0], r.at[1], p, first))
    pieces += [(late_s.at[0, s], late_s.at[1, s], got.at[0, 1, s], got.at[1, 1, s], late_p.at[s], n % 2 == 1)
               for n, s in enumerate(LATE)]

    def send_near(p):
        to_r, to_l, from_l, from_r, passing, first = pieces[p]

        odd = lax.rem(b, 2) == 1

        @pl.when(goes_left & ~odd)
        def _():
            remote(to_l, from_r, send_sem.at[1, p], recv_sem.at[1, p], (z, b - 1)).start()

        @pl.when(goes_right)
        def _():
            remote(to_r, from_l, send_sem.at[0, p], recv_sem.at[0, p], (z, b + 1)).start()

        @pl.when(goes_left & odd)
        def _():
            remote(to_l, from_r, send_sem.at[1, p], recv_sem.at[1, p], (z, b - 1)).start()

    def send_bent(p):
        to_r, to_l, from_l, from_r, passing, first = pieces[p]
        if bends:
            @pl.when(at_cut)
            def _():
                remote(to_r, passing, send_sem.at[0, p], recv_sem.at[2, p], (z, low if first else high)).start()

            @pl.when(past_cut)
            def _():
                remote(to_l, passing, send_sem.at[1, p], recv_sem.at[2, p], (z, high if first else low)).start()

    def forward(p):
        to_r, to_l, from_l, from_r, passing, first = pieces[p]
        if bends:
            for who, ahead in ((is_low, True), (is_high, False)):
                @pl.when(who)
                def _():
                    remote(to_r, passing, send_sem.at[2, p], recv_sem.at[2, p], (z, cut)).wait_recv()
                    if first == ahead:
                        remote(passing, from_l, send_sem.at[2, p], recv_sem.at[0, p], (z, cut + 1)).start()
                    else:
                        remote(passing, from_r, send_sem.at[2, p], recv_sem.at[1, p], (z, cut)).start()

    def arrived(p):
        to_r, to_l, from_l, from_r, passing, first = pieces[p]

        @pl.when(b > 0)
        def _():
            remote(to_r, from_l, send_sem.at[0, p], recv_sem.at[0, p], (z, b - 1)).wait_recv()

        @pl.when(b < nb - 1)
        def _():
            remote(to_l, from_r, send_sem.at[1, p], recv_sem.at[1, p], (z, b + 1)).wait_recv()

    def sent(p):
        to_r, to_l, from_l, from_r, passing, first = pieces[p]

        @pl.when(b < nb - 1)
        def _():
            remote(to_r, from_l, send_sem.at[0, p], recv_sem.at[0, p], (z, b + 1)).wait_send()

        @pl.when(b > 0)
        def _():
            remote(to_l, from_r, send_sem.at[1, p], recv_sem.at[1, p], (z, b - 1)).wait_send()

        if bends:
            @pl.when(is_low | is_high)
            def _():
                remote(passing, from_l, send_sem.at[2, p], recv_sem.at[0, p], (z, cut)).wait_send()

    for n, s in enumerate(EARLY):
        loads[n].wait()

        def gather(i, carry):
            early_s[0, i], early_s[1, i] = choose(first_pick, [a_ref[i, j] for j in range(slots)])
            return carry

        lax.fori_loop(s.start, min(s.stop, Q), gather, 0)
        if s.stop == Q + 1:
            for load in side_loads:
                load.wait()
            early_s[0, Q], early_s[1, Q] = choose(
                first_pick, [jnp.where(fluid_ref[j] > 0, relax_ref[j], 0.0) for j in range(slots)])
        if n == 0:
            send_near(0)
        if n == 2:
            send_bent(2)

    def rate_of(slot):
        return lambda at: jnp.where(fluid_ref[(slot,) + at] > 0, relax_ref[(slot,) + at], 0.0)

    def first_step(slot, carry):
        def put(i, at, value):
            a_ref[(i, slot) + at] = value

        collide_tiles(rows, width, lambda i, at: a_ref[(i, slot) + at], rate_of(slot), put)
        emit_halo(slot, edge, a_ref, fluid_ref, ys1, xs1)
        return carry

    def routes(step):
        ys, xs, cs, yr, xr, cr = ((ys1, xs1, cs1, yr1, xr1, cr1), (ys2, xs2, cs2, yr2, xr2, cr2))[step]
        ends = [(ys.at[0], yr.at[0]), (ys.at[1], yr.at[1]), (xs.at[0], xr.at[0]), (xs.at[1], xr.at[1])]
        ends += [(cs.at[k], cr.at[k]) for k in range(4)]
        return [(src, dst, dz, db, step * 8 + n) for n, ((src, dst), (dz, db)) in enumerate(zip(ends, ways))]

    def exchange(step):
        for src, dst, dz, db, n in routes(step):
            @pl.when(there(dz, db))
            def _():
                remote(src, dst, halo_send.at[n], halo_recv.at[n], (z + dz, b + db)).start()

    def await_halo(step):
        for src, dst, dz, db, n in routes(step):
            @pl.when(there(-dz, -db))
            def _():
                remote(src, dst, halo_send.at[n], halo_recv.at[n], (z - dz, b - db)).wait_recv()

    ys1[...] = jnp.zeros(ys1.shape, jnp.float32)
    ys2[...] = jnp.zeros(ys2.shape, jnp.float32)
    lax.fori_loop(0, slots, first_step, 0)
    emit_corners(rows, ys1, cs1)
    pl.semaphore_wait(row_sem, rows_met)
    exchange(0)
    send_near(1)
    send_near(2)
    send_bent(3)
    send_bent(0)
    await_halo(0)
    forward(2)

    def middle_step(slot, carry):
        halo = (yr1, xr1, cr1)
        make_mask(slot, edge, slots, fluid_ref, halo, mask_ref)

        values = {}

        def write(i, value):
            next_ref[i] = values[i] = value
            pack_shell(0, i, edge, values, hz.at[slot], hx.at[slot], hy.at[slot])

        stream_slot(slot, edge, slots, mask_ref, a_ref, halo, write)

        def put(i, at, value):
            b_ref[(i, slot) + at] = value

        collide_tiles(rows, width, lambda i, at: next_ref[(i,) + at], rate_of(slot), put)
        emit_halo(slot, edge, b_ref, fluid_ref, ys2, xs2)
        return carry

    lax.fori_loop(0, slots, middle_step, 0)
    emit_corners(rows, ys2, cs2)
    exchange(1)
    send_near(3)
    send_bent(1)
    forward(3)
    await_halo(1)

    def last_step(slot, carry):
        values = {}

        def write(i, value):
            a_ref[i, slot] = values[i] = value
            pack_shell(1, i, edge, values, hz.at[slot], hx.at[slot], hy.at[slot])

        stream_slot(slot, edge, slots, mask_ref, b_ref, (yr2, xr2, cr2), write)
        return carry

    lax.fori_loop(0, slots, last_step, 0)
    kept, y_lanes = hx_s.shape[1], hy.shape[2]
    for side, (x_part, y_part) in enumerate(zip(choose(first_pick, [hx[j] for j in range(slots)]),
                                                choose(first_pick, [hy[j] for j in range(slots)]))):
        hx_s[side] = x_part[:kept]
        hy_s[side, :, :y_lanes] = y_part
        for n, t in spare:
            hy_s[side, pl.ds(n * (width // 128) + t, 1), y_lanes:] = x_part[kept + n:kept + n + 1, t * 128:(t + 1) * 128]
    for side, whole in enumerate(choose(first_pick, [hz[j] for j in range(slots)])):
        hz_s[side] = fold(edge, whole)
    for p in (5, 6, 4):
        send_near(p)
        send_bent(p)
    for n, s in enumerate(LATE):
        def gather(i, carry):
            late_s[0, i], late_s[1, i] = choose(second_pick, [a_ref[i, j] for j in range(slots)])
            return carry

        lax.fori_loop(s.start, s.stop, gather, 0)
        send_near(7 + n)
        send_bent(7 + n)

    for p in (0, 5, 6, 1, 4, 7, 9):
        forward(p)
    for p in range(7):
        arrived(p)

    def redo(side, carry):
        hz[0] = unfold(edge, hz_r[side], width)
        hx[0, :kept] = hx_r[side]
        for n, t in spare:
            hx[0, kept + n:kept + n + 1, t * 128:(t + 1) * 128] = hy_r[side, pl.ds(n * (width // 128) + t, 1), y_lanes:]
        redo_block(edge, early_r.at[side], hz.at[0], hx.at[0], hy_r.at[side], redo_mask, got.at[side, 0])
        return carry

    lax.fori_loop(jnp.where(b > 0, 0, 1), jnp.where(b < nb - 1, 2, 1), redo, 0)
    for p in (8, 10):
        forward(p)

    for n, db in ((0, 1), (1, -1)):
        @pl.when(there(0, -db))
        def _():
            remote(note_s, note_r.at[n], note_send.at[n], note_recv.at[n], (z, b - db)).wait_recv()

        @pl.when(there(0, db))
        def _():
            note_copy(n).wait_send()

    fetch = pltpu.make_async_copy(note_r, note_m, note_sem.at[0])
    fetch.start()
    fetch.wait()
    kind = [jnp.int32(0)] * slots
    index = [jnp.int32(k) for k in range(slots)]
    for k in range(slots):
        for j in range(slots):
            index[k] = jnp.where(goal[j] == base + k, j, index[k])
    for source, valid in ((1, b > 0), (2, b < nb - 1)):
        rank = jnp.int32(0)
        for j in range(slots):
            value = note_m[source - 1, j, 0]
            for k in range(slots):
                hit = valid & (value == base + k)
                kind[k] = jnp.where(hit, source, kind[k])
                index[k] = jnp.where(hit, rank, index[k])
            rank = rank + flag(valid & (value >= base) & (value < base + slots))
    line = lax.broadcasted_iota(jnp.int32, table_ref.shape, 0)
    entry = lax.broadcasted_iota(jnp.int32, table_ref.shape, 1)
    table = jnp.zeros(table_ref.shape, jnp.int32)
    for k in range(slots):
        table = jnp.where(entry == k, jnp.where(line == 0, kind[k], index[k]), table)
    table_ref[...] = table

    for step in range(2):
        for src, dst, dz, db, n in routes(step):
            @pl.when(there(dz, db))
            def _():
                remote(src, dst, halo_send.at[n], halo_recv.at[n], (z + dz, b + db)).wait_send()

    for p in range(7):
        sent(p)
    for p in range(7, PIECES):
        sent(p)
        arrived(p)


def solve(pdfs, relax, fluid, targets):
    q, slots, rows, width = pdfs.shape
    edge = rows
    f32, i32 = jnp.float32, jnp.int32
    hbm = pl.BlockSpec(memory_space=pl.ANY)
    vmem = pl.BlockSpec(memory_space=pltpu.VMEM)
    smem = pl.BlockSpec(memory_space=pltpu.SMEM)
    per = 128 // edge
    turns = 2 * len(TURNS[0])
    x_rows = -(-turns // 8) * 8
    y_lanes = -(-turns // per) * 128
    ys, xs, cs = (2, 6, rows, 128), (2, -(-6 * slots // 8) * 8, width), (4, 8, 128)

    z_lanes = 2 * len(TURNS[2]) * (width // edge)

    kept = turns // 8 * 8
    assert (turns - kept) * width <= rows * 128

    def shells(lead, whole=False):
        kinds = ((rows, width), (x_rows, width), (rows, y_lanes))
        if not whole:
            kinds = ((rows, z_lanes), (kept, width), (rows, y_lanes + 128))
        return [pltpu.VMEM(lead + s, f32) for s in kinds]

    halo = [pltpu.VMEM(s, f32) for s in (ys, xs, cs)]
    dma = pltpu.SemaphoreType.DMA
    scratch = [pltpu.VMEM(relax.shape, f32), pltpu.VMEM(fluid.shape, i32), pltpu.VMEM(pdfs.shape, f32), pltpu.VMEM((q, rows, width), f32),
               pltpu.VMEM(fluid.shape, i32)] + halo * 4
    scratch += shells((slots,), True)
    scratch += [pltpu.VMEM((2, q + 1, rows, width), f32)] + shells((2,)) + [pltpu.VMEM((2, q, rows, width), f32)]
    scratch += [pltpu.VMEM((2, q + 1, rows, width), f32)] + shells((2,))
    scratch += [pltpu.VMEM((q + 1, rows, width), f32)] + shells(()) + [pltpu.VMEM((q, rows, width), f32)]
    scratch += [pltpu.VMEM((rows, width), i32)]
    scratch += [pltpu.VMEM((8, 128), i32), pltpu.VMEM((2, 8, 128), i32), pltpu.SMEM((2, 8, 128), i32)]
    scratch += [dma((6,)), pltpu.SemaphoreType.REGULAR, dma((16,)), dma((16,)), dma((2,)), dma((2,)), dma((1,)),
                dma((3, PIECES)), dma((3, PIECES))]
    return pl.pallas_call(
        functools.partial(solve_kernel, edge),
        out_shape=[pltpu.VMEM(pdfs.shape, f32), pltpu.VMEM((2, 2, q, rows, width), f32),
                   pltpu.VMEM((8, 128), i32)],
        in_specs=[hbm, hbm, hbm, smem], out_specs=[vmem, vmem, vmem], scratch_shapes=scratch,
        compiler_params=pltpu.CompilerParams(collective_id=0, has_side_effects=True, vmem_limit_bytes=40 * 1024 * 1024),
        name="solve",
    )(pdfs, relax, fluid, targets)


def place_kernel(table_ref, own, got, out, sem):
    slots = out.shape[1]
    for k in range(slots):
        for kind in range(3):
            @pl.when(table_ref[0, k] == kind)
            def _():
                at = table_ref[1, k]
                for n, s in enumerate(LATE):
                    src = own.at[s, at] if kind == 0 else got.at[kind - 1, at, s]
                    pltpu.make_async_copy(src, out.at[s, k], sem.at[k, n]).start()

    for k in range(slots):
        for n, s in enumerate(LATE):
            pltpu.make_async_copy(own.at[s, k], out.at[s, k], sem.at[k, n]).wait()


def place(own, got, table):
    hbm = pl.BlockSpec(memory_space=pl.ANY)
    smem = pl.BlockSpec(memory_space=pltpu.SMEM)
    return pl.pallas_call(
        place_kernel, out_shape=jax.ShapeDtypeStruct(own.shape, own.dtype),
        in_specs=[smem, hbm, hbm], out_specs=hbm, scratch_shapes=[pltpu.SemaphoreType.DMA((own.shape[1], len(LATE)))],
        compiler_params=pltpu.CompilerParams(vmem_limit_bytes=1024 * 1024), name="place",
    )(table, own, got)


def on_device(pdfs, relax, fluid, targets):
    own, got, table = solve(pdfs, relax, fluid, targets)
    return place(own, got, table)


def solution(mesh):
    placed = (
        P(None, None, "bxy", "bz"),
        P(None, "bxy", "bz"),
        P(None, "bxy", "bz"),
        P("bz", "bxy", None),
    )
    return jax.shard_map(
        on_device, mesh=mesh, in_specs=placed, out_specs=P(None, None, "bxy", "bz"), check_vma=False
    )
```

```python
import functools
import math

import jax
import jax.numpy as jnp
from jax import lax
from jax.experimental import pallas as pl
from jax.experimental.pallas import tpu as pltpu
from jax.sharding import PartitionSpec as P

MESH = pl.DeviceIdType.MESH
VELOCITIES = (
    (0, 0, 0), (1, 0, 0), (-1, 0, 0), (0, 1, 0), (0, -1, 0), (0, 0, 1), (0, 0, -1),
    (1, 1, 0), (-1, -1, 0), (1, -1, 0), (-1, 1, 0), (1, 0, 1), (-1, 0, -1),
    (1, 0, -1), (-1, 0, 1), (0, 1, 1), (0, -1, -1), (0, 1, -1), (0, -1, 1),
)
OPPOSITE = (0, 2, 1, 4, 3, 6, 5, 8, 7, 10, 9, 12, 11, 14, 13, 16, 15, 18, 17)
Q = 19
TURNS = tuple(tuple(i for i in range(Q) if VELOCITIES[i][axis]) for axis in range(3))
Y_SENT = tuple(tuple(i for i in range(Q) if VELOCITIES[i][1] == c) for c in (1, -1))
X_SENT = tuple(tuple(i for i in range(Q) if VELOCITIES[i][0] == c) for c in (1, -1))
CORNERS = (7, 8, 9, 10)
SIDE = {1: 0, -1: 1}
VMEM_LIMIT = 60 * 1024 * 1024


def collide(f, rate):
    pair = {i: (f[i] + f[i + 1], f[i] - f[i + 1]) for i in range(1, Q, 2)}
    density = f[0]
    for i in range(1, Q, 2):
        density = density + pair[i][0]
    scale = 3.0 / density
    flow = []
    for axis in range(3):
        total = None
        for i in range(1, Q, 2):
            c = VELOCITIES[i][axis]
            if c:
                d = pair[i][1]
                total = d if total is None else (total + d if c == 1 else total - d)
        flow.append(total * scale)
    base = 1.0 - (flow[0] * flow[0] + flow[1] * flow[1] + flow[2] * flow[2]) * (1.0 / 6.0)
    keep = 1.0 - rate
    drive = rate * density
    post = [None] * Q
    post[0] = keep * f[0] + (drive * (1.0 / 3.0)) * base
    near, far = drive * (1.0 / 18.0), drive * (1.0 / 36.0)
    for i in range(1, Q, 2):
        along = None
        for axis in range(3):
            c = VELOCITIES[i][axis]
            if c:
                along = flow[axis] if along is None else (along + flow[axis] if c == 1 else along - flow[axis])
        even = base + 0.5 * (along * along)
        weight = near if i < 7 else far
        post[i] = keep * f[i] + weight * (even + along)
        post[i + 1] = keep * f[i + 1] + weight * (even - along)
    return post


def remote(src, dst, send_sem, recv_sem, device):
    return pltpu.make_async_remote_copy(
        src_ref=src, dst_ref=dst, send_sem=send_sem, recv_sem=recv_sem, device_id=device, device_id_type=MESH)


def lane_shift(velocity, slot, edge, here, below, above, beside):
    _cx, cy, cz = velocity
    width = here.shape[1]
    step = cy * edge + cz
    moved = here if step == 0 else pltpu.roll(here, step % width, 1)
    if cz:
        depth = lax.broadcasted_iota(jnp.int32, here.shape, 1) % edge
        other, face = (below, 0) if cz == 1 else (above, edge - 1)
        carry = step - cz * edge
        wrapped = other if carry == 0 else pltpu.roll(other, carry % width, 1)
        moved = jnp.where(depth == face, wrapped, moved)
    if cy:
        lane = lax.broadcasted_iota(jnp.int32, (here.shape[0], 128), 1)
        offset = 128 if cy == 1 else 256 - edge
        outside = pltpu.roll(beside, lax.rem(offset + cz + 128 - slot * edge, 128), 1)
        if cy == 1:
            moved = jnp.concatenate([jnp.where(lane < edge, outside, moved[:, :128]), moved[:, 128:]], axis=1)
        else:
            moved = jnp.concatenate(
                [moved[:, :-128], jnp.where(lane >= 128 - edge, outside, moved[:, -128:])], axis=1)
    return moved


def arrive(i, slot, edge, slots, here, below, above, yr_ref, xr_ref, cr_ref, fluid):
    velocity = cx, cy, cz = VELOCITIES[i]
    beside = None
    if cy:
        side = SIDE[cy]
        beside = yr_ref[side, 5 if fluid else Y_SENT[side].index(i)]
    moved = lane_shift(velocity, slot, edge, here, below, above, beside)
    if cx:
        side = SIDE[cx]
        row = 5 if fluid else X_SENT[side].index(i)
        rows = moved.shape[0]

        def plane(s):
            return jnp.broadcast_to(xr_ref[side, pl.ds(row * slots + s, 1), :], (8, moved.shape[1]))

        corner = None
        if cy:
            k = CORNERS.index(i)
            n = 1 if fluid else 0
            corner = jnp.broadcast_to(cr_ref[k, n:n + 1, :], (8, 128))
        entering = lane_shift(
            velocity, slot, edge, plane(slot), plane(jnp.maximum(slot - 1, 0)) if cz == 1 else None,
            plane(jnp.minimum(slot + 1, slots - 1)) if cz == -1 else None, corner)
        index = lax.broadcasted_iota(jnp.int32, (8, moved.shape[1]), 0)
        moved = pltpu.roll(moved, cx % rows, 0)
        if cx == 1:
            moved = jnp.concatenate([jnp.where(index == 0, entering, moved[:8]), moved[8:]], axis=0)
        else:
            moved = jnp.concatenate([moved[:-8], jnp.where(index == 7, entering, moved[-8:])], axis=0)
    return moved


def collide_tiles(rows, width, read, rate, write):
    tiles = width // 128

    def body(step, carry):
        r = pl.multiple_of((step // tiles) * 8, 8)
        c = pl.multiple_of((step % tiles) * 128, 128)
        at = (pl.ds(r, 8), pl.ds(c, 128))
        post = collide([read(i, at) for i in range(Q)], rate(at))
        for i in range(Q):
            write(i, at, post[i])
        return carry

    lax.fori_loop(0, (rows // 8) * tiles, body, 0, unroll=4)


def emit_halo(slot, edge, post_ref, fluid_ref, ys_ref, xs_ref):
    slots, rows, width = fluid_ref.shape
    lane = lax.broadcasted_iota(jnp.int32, (rows, 128), 1)
    mine = lane // edge == slot
    for side, first in ((0, width - 128), (1, 0)):
        turn = lax.rem(slot * edge + (edge if side == 0 else 0), 128)
        for n in range(6):
            if n < 5:
                tile = post_ref[Y_SENT[side][n], slot, :, first:first + 128]
            else:
                tile = fluid_ref[slot, :, first:first + 128].astype(jnp.float32)
            ys_ref[side, n] = jnp.where(mine, pltpu.roll(tile, turn, 1), ys_ref[side, n])
    for side, row in ((0, rows - 1), (1, 0)):
        for n in range(5):
            xs_ref[side, pl.ds(n * slots + slot, 1), :] = post_ref[X_SENT[side][n], slot, row:row + 1, :]
        xs_ref[side, pl.ds(5 * slots + slot, 1), :] = fluid_ref[slot, row:row + 1, :].astype(jnp.float32)


def emit_corners(rows, ys_ref, cs_ref):
    for k, i in enumerate(CORNERS):
        cx, cy, _z = VELOCITIES[i]
        row = rows - 1 if cx == 1 else 0
        ys = SIDE[cy]
        cs_ref[k, 0:1, :] = ys_ref[ys, Y_SENT[ys].index(i), row:row + 1, :]
        cs_ref[k, 1:2, :] = ys_ref[ys, 5, row:row + 1, :]
        cs_ref[k, 2:8, :] = jnp.zeros((6, 128), jnp.float32)


def stream_slot(slot, edge, slots, mask_ref, post_ref, halo, write):
    below, above = jnp.maximum(slot - 1, 0), jnp.minimum(slot + 1, slots - 1)
    write(0, post_ref[0, slot])
    for i in range(1, Q):
        cz = VELOCITIES[i][2]
        own = post_ref[i, slot]
        value = arrive(
            i, slot, edge, slots, own, post_ref[i, below] if cz == 1 else None,
            post_ref[i, above] if cz == -1 else None, *halo, False)
        mask = mask_ref[slot]
        stay = jnp.where(mask > 0, post_ref[OPPOSITE[i], slot], own)
        write(i, jnp.where((mask & (1 << i)) != 0, value, stay))


def make_mask(slot, edge, slots, fluid_ref, halo, mask_ref):
    rows, width = fluid_ref.shape[1:]
    row = lax.broadcasted_iota(jnp.int32, (rows, width), 0)
    lane = lax.broadcasted_iota(jnp.int32, (rows, width), 1)
    depth = lane % edge
    z, b = lax.axis_index("bz"), lax.axis_index("bxy")
    at_end = (b == 0, b == lax.axis_size("bxy") - 1, z == 0, z == lax.axis_size("bz") - 1)
    fluid = fluid_ref[slot].astype(jnp.float32)
    below = fluid_ref[jnp.maximum(slot - 1, 0)].astype(jnp.float32)
    above = fluid_ref[jnp.minimum(slot + 1, slots - 1)].astype(jnp.float32)
    bits = jnp.ones((rows, width), jnp.int32)
    for i in range(1, Q):
        cx, cy, cz = VELOCITIES[i]
        source = arrive(i, slot, edge, slots, fluid, below if cz == 1 else None,
                        above if cz == -1 else None, *halo, True)
        bit = jnp.where(source > 0.5, 1 << i, 0)
        if cx:
            edge_row = 0 if cx == 1 else rows - 1
            bit = jnp.where((row == edge_row) & at_end[0 if cx == 1 else 1], 0, bit)
        if cy:
            outer = lane < edge if cy == 1 else lane >= width - edge
            bit = jnp.where(outer & at_end[2 if cy == 1 else 3], 0, bit)
        if cz:
            final = 0 if cz == 1 else slots - 1
            face = 0 if cz == 1 else edge - 1
            bit = jnp.where((depth == face) & (slot == final), 0, bit)
        bits = bits | bit
    mask_ref[slot] = jnp.where(fluid_ref[slot] > 0, bits, 0)


def pack_shell(step, i, edge, values, hz, hx, hy):
    value = values[i]
    rows, width = value.shape
    for axis, c in enumerate(VELOCITIES[i]):
        if not c:
            continue
        n = TURNS[axis].index(i) + step * len(TURNS[axis])
        if axis == 0:
            row = 0 if c == 1 else rows - 1
            hx[n:n + 1, :] = value[row:row + 1, :]
        elif axis == 1:
            per = 128 // edge
            t, g = n // per, n % per
            tile = value[:, :128] if c == 1 else value[:, width - 128:]
            shift = (g * edge - (0 if c == 1 else 128 - edge)) % 128
            tile = pltpu.roll(tile, shift, 1) if shift else tile
            if g:
                lane = lax.broadcasted_iota(jnp.int32, tile.shape, 1)
                tile = jnp.where(lane >= g * edge, tile, hy[:, t * 128:(t + 1) * 128])
            hy[:, t * 128:(t + 1) * 128] = tile
        elif n % 2:
            depth = lax.broadcasted_iota(jnp.int32, value.shape, 1) % edge
            pair = (values[i - 1], value) if c == -1 else (value, values[i - 1])
            both = jnp.where(depth == 0, pair[0], pair[1])
            both = pltpu.roll(both, n, 1)
            hz[...] = jnp.where(depth // 2 == n // 2, both, hz[...]) if n > 1 else both


def fold(edge, whole):
    used = 2 * len(TURNS[2])
    free, left = edge - used, 2 * used - edge
    half = whole.shape[1] // 2
    depth = lax.broadcasted_iota(jnp.int32, whole.shape, 1)[:, :half] % edge
    far = whole[:, half:]
    near = jnp.where(depth < used, whole[:, :half], pltpu.roll(far, used, 1))
    far = pltpu.roll(far, half - free, 1)
    while left < edge:
        half = far.shape[1] // 2
        far = jnp.where(depth[:, :half] < left, far[:, :half], pltpu.roll(far[:, half:], left, 1))
        left *= 2
    return jnp.concatenate([near, far], axis=1)


def unfold(edge, folded, width):
    used = 2 * len(TURNS[2])
    free, left = edge - used, 2 * used - edge
    half = width // 2
    depth = lax.broadcasted_iota(jnp.int32, (folded.shape[0], half), 1) % edge
    near, far = folded[:, :half], folded[:, half:]
    size = edge
    while size > left:
        size //= 2
        far = jnp.concatenate([far, pltpu.roll(far, far.shape[1] - size, 1)], axis=1)
    far = pltpu.roll(far, free, 1)
    return jnp.concatenate([near, jnp.where(depth < free, pltpu.roll(near, half - used, 1), far)], axis=1)


def patch_shell(step, i, edge, value, hz, hx, hy):
    rows, width = value.shape
    for axis, c in enumerate(VELOCITIES[i]):
        if not c:
            continue
        n = TURNS[axis].index(i) + step * len(TURNS[axis])
        if axis == 0:
            row = 0 if c == 1 else rows - 1
            index = lax.broadcasted_iota(jnp.int32, value.shape, 0)
            value = jnp.where(index == row, jnp.broadcast_to(hx[n:n + 1, :], value.shape), value)
        elif axis == 1:
            per = 128 // edge
            t, g = n // per, n % per
            shift = ((0 if c == 1 else 128 - edge) - g * edge) % 128
            tile = hy[:, t * 128:(t + 1) * 128]
            tile = pltpu.roll(tile, shift, 1) if shift else tile
            lane = lax.broadcasted_iota(jnp.int32, tile.shape, 1)
            if c == 1:
                value = jnp.concatenate([jnp.where(lane < edge, tile, value[:, :128]), value[:, 128:]], axis=1)
            else:
                value = jnp.concatenate(
                    [value[:, :-128], jnp.where(lane >= 128 - edge, tile, value[:, -128:])], axis=1)
        else:
            depth = lax.broadcasted_iota(jnp.int32, value.shape, 1) % edge
            face = 0 if c == 1 else edge - 1
            turned = pltpu.roll(hz[...], width - (n | 1), 1)
            value = jnp.where(depth == face, turned, value)
    return value


def pulled(i, edge, here):
    cx, cy, cz = VELOCITIES[i]
    lanes = (cy * edge + cz) % here.shape[1]
    here = pltpu.roll(here, lanes, 1) if lanes else here
    return pltpu.roll(here, cx % here.shape[0], 0) if cx else here


def redo_block(edge, f, hz, hx, hy, mask_ref, next_ref):
    rows, width = f.shape[1:]
    fluid = jnp.where(f[Q] > 0.0, 1.0, 0.0)
    bits = jnp.ones((rows, width), jnp.int32)
    for i in range(1, Q):
        bits = bits | jnp.where(pulled(i, edge, fluid) > 0.5, 1 << i, 0)
    mask_ref[...] = jnp.where(f[Q] > 0.0, bits, 0)

    def put(i, at, value):
        f[(i,) + at] = value

    def stream(step):
        next_ref[0] = f[0]
        for i in range(1, Q):
            own = f[i]
            mask = mask_ref[...]
            stay = jnp.where(mask > 0, f[OPPOSITE[i]], own)
            value = jnp.where((mask & (1 << i)) != 0, pulled(i, edge, own), stay)
            next_ref[i] = patch_shell(step, i, edge, value, hz, hx, hy)

    def rate(at):
        return f[(Q,) + at]

    collide_tiles(rows, width, lambda i, at: f[(i,) + at], rate, put)
    stream(0)
    collide_tiles(rows, width, lambda i, at: next_ref[(i,) + at], rate, put)
    stream(1)


def choose(picks, values):
    taken = []
    for pick in picks:
        out = values[0]
        for j in range(1, len(values)):
            out = jnp.where(pick == j, values[j], out)
        taken.append(out)
    return taken


def cuts_of(n):
    half = (n + 1) // 2
    cuts = (0, half // 2, half, half + (n - half + 1) // 2, n)
    return [slice(cuts[k], cuts[k + 1]) for k in range(4)]


EARLY = cuts_of(Q + 1)
LATE = cuts_of(Q)
PIECES = 11
WHOLE = [slice(0, Q)]


def solve_kernel(edge, pdfs, relax, fluid, goal_ref, a_ref, got, table_ref,
                 relax_ref, fluid_ref, b_ref, next_ref, mask_ref, ys1, xs1, cs1, yr1, xr1, cr1, ys2, xs2, cs2, yr2, xr2, cr2,
                 hz, hx, hy, early_s, hz_s, hx_s, hy_s, late_s, early_r, hz_r, hx_r, hy_r,
                 early_p, hz_p, hx_p, hy_p, late_p, redo_mask, note_s, note_r, note_m,
                 load_sem, row_sem, halo_send, halo_recv, note_send, note_recv, note_sem, send_sem, recv_sem):
    slots, rows, width = fluid_ref.shape
    nz, nb = lax.axis_size("bz"), lax.axis_size("bxy")
    z, b = lax.axis_index("bz"), lax.axis_index("bxy")

    loads = [pltpu.make_async_copy(pdfs.at[slice(s.start, min(s.stop, Q))], a_ref.at[slice(s.start, min(s.stop, Q))],
                                   load_sem.at[n]) for n, s in enumerate(EARLY)]
    side_loads = [pltpu.make_async_copy(relax, relax_ref, load_sem.at[4]),
                  pltpu.make_async_copy(fluid, fluid_ref, load_sem.at[5])]
    for load in loads + side_loads:
        load.start()

    spare = [(n, t) for n in range(2 * len(TURNS[0]) - hx_s.shape[1]) for t in range(width // 128)]
    across = math.isqrt(nb // 2)
    row = 2 * across
    bends = across == 2 and nb == 2 * row
    cut = row - 1 if bends else nb
    low, high = cut + 1 - row, cut + row
    no = b < 0
    goes_right, goes_left = (b < nb - 1) & (b != cut), (b > 0) & (b != cut + 1)
    at_cut, past_cut, is_low, is_high = (
        (b == cut, b == cut + 1, b == low, b == high) if bends else (no, no, no, no))

    def there(dz, db):
        exists = None
        for at, step, count in ((z, dz, nz), (b, db, nb)):
            if step:
                inside = at < count - 1 if step == 1 else at > 0
                exists = inside if exists is None else exists & inside
        return exists

    ways = [(1, 0), (-1, 0), (0, 1), (0, -1)] + [(VELOCITIES[i][1], VELOCITIES[i][0]) for i in CORNERS]
    meets = [(there(dz, db), (z + dz, b + db)) for dz, db in ways[:4]]
    if bends:
        for who in (at_cut, past_cut):
            meets += [(who, (z, low)), (who, (z, high))]
        for who in (is_low, is_high):
            meets += [(who, (z, cut)), (who, (z, cut + 1))]
    barrier = pltpu.get_barrier_semaphore()
    count = 0
    for who, peer in meets:
        count = count + who.astype(jnp.int32)

        @pl.when(who)
        def _():
            pl.semaphore_signal(barrier, inc=1, device_id=peer, device_id_type=MESH)

    pl.semaphore_wait(barrier, count)
    rows_met = 0
    for dz, db in ways[:2]:
        rows_met = rows_met + there(dz, db).astype(jnp.int32)

        @pl.when(there(dz, db))
        def _():
            pl.semaphore_signal(row_sem, inc=1, device_id=(z + dz, b + db), device_id_type=MESH)

    goal = [goal_ref[0, 0, j] for j in range(slots)]
    base = b * slots

    def flag(t):
        return t.astype(jnp.int32)

    def nth(hits, n):
        before, found = jnp.int32(0), jnp.int32(0)
        for j in range(slots):
            found = found + jnp.where(hits[j] & (before == n), j, 0)
            before = before + flag(hits[j])
        return found

    to_right = [g >= base + slots for g in goal]
    to_left = [g < base for g in goal]
    first_pick = (nth(to_right, 0), nth(to_left, 0))
    second_pick = (nth(to_right, 1), nth(to_left, 1))

    at_row = lax.broadcasted_iota(jnp.int32, note_s.shape, 0)
    note = jnp.zeros(note_s.shape, jnp.int32)
    for j in range(slots):
        note = jnp.where(at_row == j, goal[j], note)
    note_s[...] = note

    def note_copy(n):
        db = 1 if n == 0 else -1
        return remote(note_s, note_r.at[n], note_send.at[n], note_recv.at[n], (z, b + db))

    for n, db in ((0, 1), (1, -1)):
        @pl.when(there(0, db))
        def _():
            note_copy(n).start()

    pieces = [(early_s.at[0, s], early_s.at[1, s], early_r.at[0, s], early_r.at[1, s], early_p.at[s], n < 2)
              for n, s in enumerate(EARLY)]
    for s, r, p, first in ((hz_s, hz_r, hz_p, True), (hx_s, hx_r, hx_p, False), (hy_s, hy_r, hy_p, False)):
        pieces.append((s.at[0], s.at[1], r.at[0], r.at[1], p, first))
    pieces += [(late_s.at[0, s], late_s.at[1, s], got.at[0, 1, s], got.at[1, 1, s], late_p.at[s], n % 2 == 1)
               for n, s in enumerate(LATE)]

    def send_near(p):
        to_r, to_l, from_l, from_r, passing, first = pieces[p]

        odd = lax.rem(b, 2) == 1

        @pl.when(goes_left & ~odd)
        def _():
            remote(to_l, from_r, send_sem.at[1, p], recv_sem.at[1, p], (z, b - 1)).start()

        @pl.when(goes_right)
        def _():
            remote(to_r, from_l, send_sem.at[0, p], recv_sem.at[0, p], (z, b + 1)).start()

        @pl.when(goes_left & odd)
        def _():
            remote(to_l, from_r, send_sem.at[1, p], recv_sem.at[1, p], (z, b - 1)).start()

    def send_bent(p):
        to_r, to_l, from_l, from_r, passing, first = pieces[p]
        if bends:
            @pl.when(at_cut)
            def _():
                remote(to_r, passing, send_sem.at[0, p], recv_sem.at[2, p], (z, low if first else high)).start()

            @pl.when(past_cut)
            def _():
                remote(to_l, passing, send_sem.at[1, p], recv_sem.at[2, p], (z, high if first else low)).start()

    def forward(p):
        to_r, to_l, from_l, from_r, passing, first = pieces[p]
        if bends:
            for who, ahead in ((is_low, True), (is_high, False)):
                @pl.when(who)
                def _():
                    remote(to_r, passing, send_sem.at[2, p], recv_sem.at[2, p], (z, cut)).wait_recv()
                    if first == ahead:
                        remote(passing, from_l, send_sem.at[2, p], recv_sem.at[0, p], (z, cut + 1)).start()
                    else:
                        remote(passing, from_r, send_sem.at[2, p], recv_sem.at[1, p], (z, cut)).start()

    def arrived(p):
        to_r, to_l, from_l, from_r, passing, first = pieces[p]

        @pl.when(b > 0)
        def _():
            remote(to_r, from_l, send_sem.at[0, p], recv_sem.at[0, p], (z, b - 1)).wait_recv()

        @pl.when(b < nb - 1)
        def _():
            remote(to_l, from_r, send_sem.at[1, p], recv_sem.at[1, p], (z, b + 1)).wait_recv()

    def sent(p):
        to_r, to_l, from_l, from_r, passing, first = pieces[p]

        @pl.when(b < nb - 1)
        def _():
            remote(to_r, from_l, send_sem.at[0, p], recv_sem.at[0, p], (z, b + 1)).wait_send()

        @pl.when(b > 0)
        def _():
            remote(to_l, from_r, send_sem.at[1, p], recv_sem.at[1, p], (z, b - 1)).wait_send()

        if bends:
            @pl.when(is_low | is_high)
            def _():
                remote(passing, from_l, send_sem.at[2, p], recv_sem.at[0, p], (z, cut)).wait_send()

    for n, s in enumerate(EARLY):
        loads[n].wait()

        def gather(i, carry):
            early_s[0, i], early_s[1, i] = choose(first_pick, [a_ref[i, j] for j in range(slots)])
            return carry

        lax.fori_loop(s.start, min(s.stop, Q), gather, 0)
        if s.stop == Q + 1:
            for load in side_loads:
                load.wait()
            early_s[0, Q], early_s[1, Q] = choose(
                first_pick, [jnp.where(fluid_ref[j] > 0, relax_ref[j], 0.0) for j in range(slots)])
        if n == 0:
            send_near(0)
        if n == 2:
            send_bent(2)

    def rate_of(slot):
        return lambda at: jnp.where(fluid_ref[(slot,) + at] > 0, relax_ref[(slot,) + at], 0.0)

    def first_step(slot, carry):
        def put(i, at, value):
            a_ref[(i, slot) + at] = value

        collide_tiles(rows, width, lambda i, at: a_ref[(i, slot) + at], rate_of(slot), put)
        emit_halo(slot, edge, a_ref, fluid_ref, ys1, xs1)
        return carry

    def routes(step):
        ys, xs, cs, yr, xr, cr = ((ys1, xs1, cs1, yr1, xr1, cr1), (ys2, xs2, cs2, yr2, xr2, cr2))[step]
        ends = [(ys.at[0], yr.at[0]), (ys.at[1], yr.at[1]), (xs.at[0], xr.at[0]), (xs.at[1], xr.at[1])]
        ends += [(cs.at[k], cr.at[k]) for k in range(4)]
        return [(src, dst, dz, db, step * 8 + n) for n, ((src, dst), (dz, db)) in enumerate(zip(ends, ways))]

    def exchange(step):
        for src, dst, dz, db, n in routes(step):
            @pl.when(there(dz, db))
            def _():
                remote(src, dst, halo_send.at[n], halo_recv.at[n], (z + dz, b + db)).start()

    def await_halo(step):
        for src, dst, dz, db, n in routes(step):
            @pl.when(there(-dz, -db))
            def _():
                remote(src, dst, halo_send.at[n], halo_recv.at[n], (z - dz, b - db)).wait_recv()

    ys1[...] = jnp.zeros(ys1.shape, jnp.float32)
    ys2[...] = jnp.zeros(ys2.shape, jnp.float32)
    lax.fori_loop(0, slots, first_step, 0)
    emit_corners(rows, ys1, cs1)
    pl.semaphore_wait(row_sem, rows_met)
    exchange(0)
    send_near(1)
    send_near(2)
    send_bent(3)
    send_bent(0)
    await_halo(0)
    forward(2)

    def middle_step(slot, carry):
        halo = (yr1, xr1, cr1)
        make_mask(slot, edge, slots, fluid_ref, halo, mask_ref)

        values = {}

        def write(i, value):
            next_ref[i] = values[i] = value
            pack_shell(0, i, edge, values, hz.at[slot], hx.at[slot], hy.at[slot])

        stream_slot(slot, edge, slots, mask_ref, a_ref, halo, write)

        def put(i, at, value):
            b_ref[(i, slot) + at] = value

        collide_tiles(rows, width, lambda i, at: next_ref[(i,) + at], rate_of(slot), put)
        emit_halo(slot, edge, b_ref, fluid_ref, ys2, xs2)
        return carry

    lax.fori_loop(0, slots, middle_step, 0)
    emit_corners(rows, ys2, cs2)
    exchange(1)
    send_near(3)
    send_bent(1)
    forward(3)
    await_halo(1)

    def last_step(slot, carry):
        values = {}

        def write(i, value):
            a_ref[i, slot] = values[i] = value
            pack_shell(1, i, edge, values, hz.at[slot], hx.at[slot], hy.at[slot])

        stream_slot(slot, edge, slots, mask_ref, b_ref, (yr2, xr2, cr2), write)
        return carry

    lax.fori_loop(0, slots, last_step, 0)
    kept, y_lanes = hx_s.shape[1], hy.shape[2]
    for side, (x_part, y_part) in enumerate(zip(choose(first_pick, [hx[j] for j in range(slots)]),
                                                choose(first_pick, [hy[j] for j in range(slots)]))):
        hx_s[side] = x_part[:kept]
        hy_s[side, :, :y_lanes] = y_part
        for n, t in spare:
            hy_s[side, pl.ds(n * (width // 128) + t, 1), y_lanes:] = x_part[kept + n:kept + n + 1, t * 128:(t + 1) * 128]
    for side, whole in enumerate(choose(first_pick, [hz[j] for j in range(slots)])):
        hz_s[side] = fold(edge, whole)
    for p in (5, 6, 4):
        send_near(p)
        send_bent(p)
    for n, s in enumerate(LATE):
        def gather(i, carry):
            late_s[0, i], late_s[1, i] = choose(second_pick, [a_ref[i, j] for j in range(slots)])
            return carry

        lax.fori_loop(s.start, s.stop, gather, 0)
        send_near(7 + n)
        send_bent(7 + n)

    for p in (0, 5, 6, 1, 4, 7, 9):
        forward(p)
    for p in range(7):
        arrived(p)

    def redo(side, carry):
        hz[0] = unfold(edge, hz_r[side], width)
        hx[0, :kept] = hx_r[side]
        for n, t in spare:
            hx[0, kept + n:kept + n + 1, t * 128:(t + 1) * 128] = hy_r[side, pl.ds(n * (width // 128) + t, 1), y_lanes:]
        redo_block(edge, early_r.at[side], hz.at[0], hx.at[0], hy_r.at[side], redo_mask, got.at[side, 0])
        return carry

    lax.fori_loop(jnp.where(b > 0, 0, 1), jnp.where(b < nb - 1, 2, 1), redo, 0)
    for p in (8, 10):
        forward(p)

    for n, db in ((0, 1), (1, -1)):
        @pl.when(there(0, -db))
        def _():
            remote(note_s, note_r.at[n], note_send.at[n], note_recv.at[n], (z, b - db)).wait_recv()

        @pl.when(there(0, db))
        def _():
            note_copy(n).wait_send()

    fetch = pltpu.make_async_copy(note_r, note_m, note_sem.at[0])
    fetch.start()
    fetch.wait()
    kind = [jnp.int32(0)] * slots
    index = [jnp.int32(k) for k in range(slots)]
    for k in range(slots):
        for j in range(slots):
            index[k] = jnp.where(goal[j] == base + k, j, index[k])
    for source, valid in ((1, b > 0), (2, b < nb - 1)):
        rank = jnp.int32(0)
        for j in range(slots):
            value = note_m[source - 1, j, 0]
            for k in range(slots):
                hit = valid & (value == base + k)
                kind[k] = jnp.where(hit, source, kind[k])
                index[k] = jnp.where(hit, rank, index[k])
            rank = rank + flag(valid & (value >= base) & (value < base + slots))
    line = lax.broadcasted_iota(jnp.int32, table_ref.shape, 0)
    entry = lax.broadcasted_iota(jnp.int32, table_ref.shape, 1)
    table = jnp.zeros(table_ref.shape, jnp.int32)
    for k in range(slots):
        table = jnp.where(entry == k, jnp.where(line == 0, kind[k], index[k]), table)
    table_ref[...] = table

    for step in range(2):
        for src, dst, dz, db, n in routes(step):
            @pl.when(there(dz, db))
            def _():
                remote(src, dst, halo_send.at[n], halo_recv.at[n], (z + dz, b + db)).wait_send()

    for p in range(7):
        sent(p)
    for p in range(7, PIECES):
        sent(p)
        arrived(p)


def solve(pdfs, relax, fluid, targets):
    q, slots, rows, width = pdfs.shape
    edge = rows
    f32, i32 = jnp.float32, jnp.int32
    hbm = pl.BlockSpec(memory_space=pl.ANY)
    vmem = pl.BlockSpec(memory_space=pltpu.VMEM)
    smem = pl.BlockSpec(memory_space=pltpu.SMEM)
    per = 128 // edge
    turns = 2 * len(TURNS[0])
    x_rows = -(-turns // 8) * 8
    y_lanes = -(-turns // per) * 128
    ys, xs, cs = (2, 6, rows, 128), (2, -(-6 * slots // 8) * 8, width), (4, 8, 128)

    z_lanes = 2 * len(TURNS[2]) * (width // edge)

    kept = turns // 8 * 8
    assert (turns - kept) * width <= rows * 128

    def shells(lead, whole=False):
        kinds = ((rows, width), (x_rows, width), (rows, y_lanes))
        if not whole:
            kinds = ((rows, z_lanes), (kept, width), (rows, y_lanes + 128))
        return [pltpu.VMEM(lead + s, f32) for s in kinds]

    halo = [pltpu.VMEM(s, f32) for s in (ys, xs, cs)]
    dma = pltpu.SemaphoreType.DMA
    scratch = [pltpu.VMEM(relax.shape, f32), pltpu.VMEM(fluid.shape, i32), pltpu.VMEM(pdfs.shape, f32), pltpu.VMEM((q, rows, width), f32),
               pltpu.VMEM(fluid.shape, i32)] + halo * 4
    scratch += shells((slots,), True)
    scratch += [pltpu.VMEM((2, q + 1, rows, width), f32)] + shells((2,)) + [pltpu.VMEM((2, q, rows, width), f32)]
    scratch += [pltpu.VMEM((2, q + 1, rows, width), f32)] + shells((2,))
    scratch += [pltpu.VMEM((q + 1, rows, width), f32)] + shells(()) + [pltpu.VMEM((q, rows, width), f32)]
    scratch += [pltpu.VMEM((rows, width), i32)]
    scratch += [pltpu.VMEM((8, 128), i32), pltpu.VMEM((2, 8, 128), i32), pltpu.SMEM((2, 8, 128), i32)]
    scratch += [dma((6,)), pltpu.SemaphoreType.REGULAR, dma((16,)), dma((16,)), dma((2,)), dma((2,)), dma((1,)),
                dma((3, PIECES)), dma((3, PIECES))]
    return pl.pallas_call(
        functools.partial(solve_kernel, edge),
        out_shape=[pltpu.VMEM(pdfs.shape, f32), pltpu.VMEM((2, 2, q, rows, width), f32),
                   pltpu.VMEM((8, 128), i32)],
        in_specs=[hbm, hbm, hbm, smem], out_specs=[vmem, vmem, vmem], scratch_shapes=scratch,
        compiler_params=pltpu.CompilerParams(collective_id=0, has_side_effects=True, vmem_limit_bytes=40 * 1024 * 1024),
        name="solve",
    )(pdfs, relax, fluid, targets)


def place_kernel(table_ref, own, got, out, sem):
    slots = out.shape[1]
    for k in range(slots):
        for kind in range(3):
            @pl.when(table_ref[0, k] == kind)
            def _():
                at = table_ref[1, k]
                for n, s in enumerate(WHOLE):
                    src = own.at[s, at] if kind == 0 else got.at[kind - 1, at, s]
                    pltpu.make_async_copy(src, out.at[s, k], sem.at[k, n]).start()

    for k in range(slots):
        for n, s in enumerate(WHOLE):
            pltpu.make_async_copy(own.at[s, k], out.at[s, k], sem.at[k, n]).wait()


def place(own, got, table):
    hbm = pl.BlockSpec(memory_space=pl.ANY)
    smem = pl.BlockSpec(memory_space=pltpu.SMEM)
    return pl.pallas_call(
        place_kernel, out_shape=jax.ShapeDtypeStruct(own.shape, own.dtype),
        in_specs=[smem, hbm, hbm], out_specs=hbm, scratch_shapes=[pltpu.SemaphoreType.DMA((own.shape[1], len(WHOLE)))],
        compiler_params=pltpu.CompilerParams(vmem_limit_bytes=1024 * 1024), name="place",
    )(table, own, got)


def on_device(pdfs, relax, fluid, targets):
    own, got, table = solve(pdfs, relax, fluid, targets)
    return place(own, got, table)


def solution(mesh):
    placed = (
        P(None, None, "bxy", "bz"),
        P(None, "bxy", "bz"),
        P(None, "bxy", "bz"),
        P("bz", "bxy", None),
    )
    return jax.shard_map(
        on_device, mesh=mesh, in_specs=placed, out_specs=P(None, None, "bxy", "bz"), check_vma=False
    )
```
